32 devices in a mesh: cent: 8 (over z, x), spot: 4 (over y, core).
Axes of the slice: x: 2, y: 2, z: 4, core: 2. Of those that a mesh axis runs over, the one named last changes fastest.
Arguments:
- logits: float32 [20480, 6144], P('cent', 'spot'), may hold values from -6 to 6
- centroid_expr: bfloat16 [20480, 2048], P('cent'), may hold values from -5.1 to 5.1
- target: bfloat16 [2048, 6144], P(None, 'spot'), may hold values from -400 to 400
- sizes: int32 [20480], P('cent'), may hold values from 1 to 22
- counts: int32 [6144], P('spot'), may hold values from 1 to 16
Outputs:
- losses: float32 [4], replicated
- pred_expr: float32 [2048, 6144], P('cent', 'spot')
- logit_grad: float32 [20480, 6144], P('cent', 'spot')
- centroid_grad: float32 [20480, 2048], P('cent', 'spot')
The draws below stay inside these ranges and needn't reach their ends.
All inputs are finite; a program needn't handle non-finite values.
Results may differ from the reference program's by a relative error of at most 0.0029.
Values may be sent and summed in bfloat16 or wider, within the bound.
No kernel may reach another device: no remote copies, remote signals or barrier semaphores. Data moves between devices by JAX's collectives and lax.ppermute only.
A program may use at most 192 MiB of HBM per device.

```python
import jax
import jax.numpy as jnp
from jax import lax

GENES = 2048
CENTROIDS = 20480
SPOTS = 6144


def gene_levels(base_key):
    level_key = jax.random.fold_in(base_key, 11)
    levels = jnp.clip(jax.random.normal(level_key, (GENES,), jnp.float32), -3.0, 3.0)
    return levels


def axis_scales(scale_key, length, spread):
    position = jnp.arange(length, dtype=jnp.float32) / length
    roughness = jax.random.uniform(scale_key, (length,), jnp.float32, 0.0, 1.0)
    return jnp.exp(jnp.log(3.0) * (position - 0.5) + jnp.log(spread) * roughness)


def draw_centroid_expr(key, part):
    levels = gene_levels(key)
    noise_key = jax.random.fold_in(key, 23)
    fluctuation = jnp.clip(jax.random.normal(noise_key, (CENTROIDS, GENES), jnp.float32), -5.0, 5.0)
    offset = 0.03
    return (offset * levels[None, :] + fluctuation).astype(jnp.bfloat16)


def draw_target(key, part):
    levels = gene_levels(key)
    noise_key = jax.random.fold_in(key, 43)
    spread = 3.0
    fluctuation = jnp.clip(jax.random.normal(noise_key, (GENES, SPOTS), jnp.float32), -4.0, 4.0)
    gene_scale = axis_scales(jax.random.fold_in(key, 37), GENES, spread)
    spot_scale = axis_scales(jax.random.fold_in(key, 41), SPOTS, spread)
    return (gene_scale[:, None] * spot_scale[None, :] * (levels[:, None] + fluctuation)).astype(jnp.bfloat16)


def place_ends(values, own_key, least, top_value):
    shape = values.shape
    index_at = [jax.random.randint(jax.random.fold_in(own_key, axis), (), 0, shape[axis]) for axis in range(len(shape))]
    values = values.at[tuple(index_at)].set(least)
    longest = shape.index(max(shape))
    index_at[longest] = (index_at[longest] + 1) % shape[longest]
    return values.at[tuple(index_at)].set(top_value)


def steps_of(rng, extent, cuts, smallest, top_value):
    loudness = 1.0
    for axis_at, shards_of in cuts:
        draws = jax.random.uniform(jax.random.fold_in(jax.random.fold_in(rng, 6), axis_at), (shards_of,), jnp.float32, smallest / len(cuts), top_value / len(cuts))
        loudness = loudness * jnp.repeat(jnp.exp(draws), extent[axis_at] // shards_of).reshape((-1,) + (1,) * (len(extent) - 1 - axis_at))
    return loudness


def normal_values(rng, dims, scale, reach, shards=(), held_as=jnp.bfloat16):
    array = jax.random.normal(rng, dims, jnp.float32) * scale
    if len(shards) > 0:
        array = steps_of(rng, dims, shards, -0.22, 0.18) * array
    return jnp.clip(array, min=-reach, max=reach).astype(held_as)


def setup_inputs(seed: int = 0) -> dict:
    key_of = jax.random.split(jax.random.key(seed), 6)
    return {
        "logits": normal_values(key_of[0], (CENTROIDS, SPOTS), 1.5, 6.0, ((0, 8), (1, 4)), jnp.float32),
        "centroid_expr": draw_centroid_expr(jax.random.fold_in(key_of[5], 71), 0),
        "target": draw_target(jax.random.fold_in(key_of[5], 71), 0),
        "sizes": place_ends(jax.random.randint(key_of[3], (CENTROIDS,), 1, 23), jax.random.fold_in(key_of[3], 1), 1, 22).astype(jnp.int32),
        "counts": place_ends(jax.random.randint(key_of[4], (SPOTS,), 1, 17), jax.random.fold_in(key_of[4], 1), 1, 16).astype(jnp.int32),
    }


@jax.custom_vjp
def low(v):
    return lax.optimization_barrier(v.astype(jnp.bfloat16)).astype(jnp.float32)

@jax.custom_vjp
def low_back(v):
    return v

def low_keep(v):
    return (low(v), None)

def low_pass(kept, grad):
    return (grad,)

def back_keep(v):
    return (v, None)

def back_low(kept, grad):
    return (low(grad),)
low.defvjp(low_keep, low_pass)
low_back.defvjp(back_keep, back_low)
EPS = 1e-06

def reference(logits, centroid_expr, target, sizes, counts):
    expr_f = centroid_expr.astype(jnp.float32)
    target_f = target.astype(jnp.float32)
    sizes_f = sizes.astype(jnp.float32)
    counts_f = counts.astype(jnp.float32)

    def forward(logit_in, expr_in):
        top = lax.optimization_barrier(jnp.max(logit_in, axis=0, keepdims=True))
        expo = jnp.exp(logit_in - top)
        probs = expo / lax.optimization_barrier(jnp.sum(expo, axis=0, keepdims=True))
        weighted = probs * sizes_f[:, None]
        mass = lax.optimization_barrier(jnp.sum(weighted, axis=0))
        pred = jnp.dot(expr_in.T, low(weighted), precision=lax.Precision.HIGHEST)
        pred = low_back(pred)
        gene_dot = lax.optimization_barrier(jnp.sum(pred * target_f, axis=1))
        gene_pp = lax.optimization_barrier(jnp.sum(pred * pred, axis=1))
        gene_tt = lax.optimization_barrier(jnp.sum(target_f * target_f, axis=1))
        cos_gene = gene_dot * lax.rsqrt(gene_pp + EPS) * lax.rsqrt(gene_tt + EPS)
        spot_dot = lax.optimization_barrier(jnp.sum(pred * target_f, axis=0))
        spot_pp = lax.optimization_barrier(jnp.sum(pred * pred, axis=0))
        spot_tt = lax.optimization_barrier(jnp.sum(target_f * target_f, axis=0))
        cos_spot = spot_dot * lax.rsqrt(spot_pp + EPS) * lax.rsqrt(spot_tt + EPS)
        mass_total = jnp.sum(mass)
        count_total = jnp.sum(counts_f)
        kl = jnp.sum(counts_f * (jnp.log(counts_f) - jnp.log(mass))) / count_total + jnp.log(mass_total) - jnp.log(count_total)
        gene_mean = jnp.mean(cos_gene)
        spot_mean = jnp.mean(cos_spot)
        total = kl - gene_mean - spot_mean
        return (total, (pred, gene_mean, spot_mean, kl))
    total, pullback, extras = jax.vjp(forward, logits, expr_f, has_aux=True)
    logit_grad, centroid_grad = pullback(jnp.ones_like(total))
    pred, gene_mean, spot_mean, kl = extras
    losses = jnp.stack([total, gene_mean, spot_mean, kl])
    return (losses, pred, logit_grad, centroid_grad)
```

```python
import functools

import jax
import jax.numpy as jnp
from jax import lax
from jax.experimental import pallas as pl
from jax.experimental.pallas import tpu as pltpu
from jax.sharding import PartitionSpec as P

EPS = 1e-06
F32 = jnp.float32
BF16 = jnp.bfloat16
LANES = 128
CHUNKS = 4
VMEM = 58 << 20


def params(limit=VMEM):
    return pltpu.CompilerParams(vmem_limit_bytes=limit)


def shape(dims, dtype):
    return jax.ShapeDtypeStruct(dims, dtype)


def bits_of(count):
    return count.bit_length() - 1


def reversed_bits(value, bits):
    return sum(((value >> b) & 1) << (bits - 1 - b) for b in range(bits))


def swap(value, axis, bit):
    count = lax.axis_size(axis)
    return lax.ppermute(value, axis, [(i, i ^ (1 << bit)) for i in range(count)])


def sum_over(value, axis):
    for bit in range(bits_of(lax.axis_size(axis))):
        value = value + swap(value, axis, bit)
    return value


def tile_lanes(column, width):
    return jnp.concatenate([column] * (width // LANES), axis=1)


def column_of(row, length):
    return jnp.transpose(jnp.broadcast_to(row, (LANES, length)))


class Order:
    def __init__(self):
        self.last = None

    def run(self, step, *operands):
        if self.last is not None:
            out = lax.optimization_barrier((self.last,) + operands)
            operands = out[1:]
        results = step(*operands)
        self.last = results[-1]
        return results


def column_stats(logits, sizes, tile):
    rows, spots = logits.shape

    def kernel(logit_ref, size_ref, sums_ref, column_ref, acc):
        step = pl.program_id(0)
        expo = jnp.exp(logit_ref[...])
        column = column_of(size_ref[...].astype(F32).reshape(1, tile), tile)
        column_ref[...] = column
        mass = expo * tile_lanes(column, spots)
        total = expo.reshape(tile // 8, 8, spots).sum(0)
        mass = mass.reshape(tile // 8, 8, spots).sum(0)

        @pl.when(step == 0)
        def _():
            acc[0] = total
            acc[1] = mass

        @pl.when(step > 0)
        def _():
            acc[0] += total
            acc[1] += mass

        @pl.when(step == pl.num_programs(0) - 1)
        def _():
            sums_ref[0:1, :] = acc[0].sum(0, keepdims=True)
            sums_ref[1:2, :] = acc[1].sum(0, keepdims=True)

    return pl.pallas_call(
        kernel,
        grid=(rows // tile,),
        in_specs=[
            pl.BlockSpec((tile, spots), lambda i: (i, 0)),
            pl.BlockSpec((1, 1, tile), lambda i: (i, 0, 0)),
        ],
        out_specs=[
            pl.BlockSpec((2, spots), lambda i: (0, 0)),
            pl.BlockSpec((tile, LANES), lambda i: (i, 0)),
        ],
        out_shape=[shape((2, spots), F32), shape((rows, LANES), F32)],
        scratch_shapes=[pltpu.VMEM((2, 8, spots), F32)],
        compiler_params=params(),
        name="column_stats",
    )(logits, sizes.reshape(rows // tile, 1, tile))


def predict(chunk, parts, low_bit, expr, weights, first=None):
    rows, genes = expr.shape
    per_device = genes // parts
    size = per_device // CHUNKS
    starts = [d * per_device + chunk * size for d in range(parts)]
    blocks = sorted({s // LANES for s in starts})
    spots = (weights if first is None else first[0]).shape[1]
    tile = 512

    def kernel(bit_ref, *refs):
        expr_refs = refs[: len(blocks)]
        rest = refs[len(blocks) :]
        if first is None:
            weight_ref, keep_ref, send_ref, turned = rest
        else:
            logit_ref, total_ref, column_ref, keep_ref, send_ref, weight_ref, turned = rest

        @pl.when(pl.program_id(0) == 0)
        def _():
            for at, block in enumerate(blocks):
                block_t = jnp.transpose(expr_refs[at][...])
                for d, start in enumerate(starts):
                    if start // LANES == block:
                        turned[d * size : (d + 1) * size, :] = block_t[start % LANES : start % LANES + size]

        if first is not None:
            scale = 1.0 / total_ref[...]
            weight = jnp.exp(logit_ref[...]) * scale * tile_lanes(column_ref[...], tile)
            weight_ref[...] = weight.astype(BF16)
        out = jnp.dot(turned[...], weight_ref[...], preferred_element_type=F32)
        even = bit_ref[0] == 0
        for j in range(parts // 2):
            a = out[2 * j * size : (2 * j + 1) * size]
            b = out[(2 * j + 1) * size : (2 * j + 2) * size]
            keep_ref[j] = jnp.where(even, a, b)
            send_ref[j] = jnp.where(even, b, a).astype(BF16)

    in_specs = [pl.BlockSpec((rows, LANES), lambda i, s, b=b: (0, b)) for b in blocks]
    operands = [expr] * len(blocks)
    half = pl.BlockSpec((parts // 2, size, tile), lambda i, s: (0, 0, i))
    columns = pl.BlockSpec((rows, tile), lambda i, s: (0, i))
    out_specs = [half, half]
    out_shapes = [shape((parts // 2, size, spots), F32), shape((parts // 2, size, spots), BF16)]
    if first is None:
        in_specs.append(columns)
        operands.append(weights)
    else:
        in_specs += [columns, pl.BlockSpec((1, tile), lambda i, s: (0, i)), pl.BlockSpec((rows, LANES), lambda i, s: (0, 0))]
        operands += list(first)
        out_specs.append(columns)
        out_shapes.append(shape((rows, spots), BF16))
    return pl.pallas_call(
        kernel,
        grid_spec=pltpu.PrefetchScalarGridSpec(
            num_scalar_prefetch=1,
            grid=(spots // tile,),
            in_specs=in_specs,
            out_specs=out_specs,
            scratch_shapes=[pltpu.VMEM((parts * size, rows), BF16)],
        ),
        out_shape=out_shapes,
        compiler_params=params(),
        name="predict",
    )(low_bit, *operands)


def add_and_halve(bit, keep, received):
    count, size, spots = keep.shape

    def kernel(bit_ref, keep_ref, received_ref, keep_out, send_out):
        a = keep_ref[0] + received_ref[0].astype(F32)
        b = keep_ref[1] + received_ref[1].astype(F32)
        even = bit_ref[0] == 0
        keep_out[0] = jnp.where(even, a, b)
        send_out[0] = jnp.where(even, b, a).astype(BF16)

    pair = pl.BlockSpec((2, size, spots), lambda i, s: (i, 0, 0))
    one = pl.BlockSpec((1, size, spots), lambda i, s: (i, 0, 0))
    return pl.pallas_call(
        kernel,
        grid_spec=pltpu.PrefetchScalarGridSpec(
            num_scalar_prefetch=1, grid=(count // 2,), in_specs=[pair, pair], out_specs=[one, one]
        ),
        out_shape=[shape((count // 2, size, spots), F32), shape((count // 2, size, spots), BF16)],
        compiler_params=params(),
        name="add_and_halve",
    )(bit, keep, received)


def finish_rows(row, keep, received, target_rows):
    _, size, spots = keep.shape

    def kernel(row_ref, keep_ref, received_ref, target_ref, pred_ref, gene_ref, spot_ref, low_ref):
        pred = keep_ref[0] + received_ref[0].astype(F32)
        target = target_ref[0].astype(F32)
        pred_ref[...] = pred
        low_ref[0] = pred.astype(BF16)
        for at, product in enumerate((pred * target, pred * pred, target * target)):
            by_gene = jnp.sum(product, axis=1, keepdims=True)
            by_gene = jnp.transpose(jnp.broadcast_to(by_gene, (size, LANES)))
            gene_ref[at : at + 1, :] = by_gene[0:1, :]
            spot_ref[at : at + 1, :] = jnp.sum(product, axis=0, keepdims=True)

    one = pl.BlockSpec((1, size, spots), lambda i, s: (0, 0, 0))
    return pl.pallas_call(
        kernel,
        grid_spec=pltpu.PrefetchScalarGridSpec(
            num_scalar_prefetch=1,
            grid=(1,),
            in_specs=[one, one, pl.BlockSpec((1, size, spots), lambda i, s: (s[0], 0, 0))],
            out_specs=[
                pl.BlockSpec((size, spots), lambda i, s: (0, 0)),
                pl.BlockSpec((3, size), lambda i, s: (0, 0)),
                pl.BlockSpec((3, spots), lambda i, s: (0, 0)),
                one,
            ],
        ),
        out_shape=[
            shape((size, spots), F32),
            shape((3, size), F32),
            shape((3, spots), F32),
            shape((1, size, spots), BF16),
        ],
        compiler_params=params(),
        name="finish_rows",
    )(row, keep, received, target_rows)


def gradients(chunk, places, pred_near, pred_far, target, gene_rows, spot_rows, weights, grads):
    parts, chunks, size, spots = target.shape
    rows = weights.shape[0]
    tile = 512
    width = parts * size

    def kernel(places_ref, near_ref, far_ref, target_ref, gene_ref, spot_ref, weight_ref, *refs):
        grad_ref, back_ref, keep_ref, send_ref, turned, columns = refs[-6:]

        @pl.when(pl.program_id(0) == 0)
        def _():
            columns[0] = column_of(gene_ref[0:1, :], width)
            columns[1] = column_of(gene_ref[1:2, :], width)
            back = jnp.zeros((1, spots), F32)
            for j in range(parts):
                d = places_ref[0, j]
                at = pl.multiple_of(d * size, size)
                pred = (near_ref[j] if j < parts // 2 else far_ref[j - parts // 2]).astype(F32)
                by_target = tile_lanes(columns[0, pl.ds(at, size), :], spots) + spot_ref[0:1, :]
                by_pred = tile_lanes(columns[1, pl.ds(at, size), :], spots) + spot_ref[1:2, :]
                grad = (target_ref[d, 0].astype(F32) * by_target + pred * by_pred).astype(BF16)
                grad_ref[d, 0] = grad
                turned[pl.ds(pl.multiple_of(places_ref[1, d] * size, size), size), :] = grad
                back = back + jnp.sum(grad.astype(F32) * pred, axis=0, keepdims=True)
            back_ref[...] = back

        out = lax.dot_general(weight_ref[...], turned[...], (((1,), (1,)), ((), ())), preferred_element_type=F32)
        keep_ref[...] = out[:, : width // 2]
        send_ref[...] = out[:, width // 2 :]

    half = pl.BlockSpec((parts // 2, size, spots), lambda i, s: (0, 0, 0))
    of_chunk = pl.BlockSpec((parts, 1, size, spots), lambda i, s: (0, chunk, 0, 0))
    piece = pl.BlockSpec((tile, width // 2), lambda i, s: (i, 0))
    in_specs = [
        half,
        half,
        of_chunk,
        pl.BlockSpec((2, width), lambda i, s: (0, 0)),
        pl.BlockSpec((2, spots), lambda i, s: (0, 0)),
        pl.BlockSpec((tile, spots), lambda i, s: (i, 0)),
    ]
    operands = [pred_near, pred_far, target, gene_rows, spot_rows, weights]
    aliases = {}
    if grads is not None:
        in_specs.append(pl.BlockSpec(memory_space=pl.ANY))
        operands.append(grads)
        aliases = {len(operands): 0}
    return pl.pallas_call(
        kernel,
        grid_spec=pltpu.PrefetchScalarGridSpec(
            num_scalar_prefetch=1,
            grid=(rows // tile,),
            in_specs=in_specs,
            out_specs=[of_chunk, pl.BlockSpec((1, spots), lambda i, s: (0, 0)), piece, piece],
            scratch_shapes=[pltpu.VMEM((width, spots), BF16), pltpu.VMEM((2, width, LANES), F32)],
        ),
        out_shape=[
            shape((parts, chunks, size, spots), BF16),
            shape((1, spots), F32),
            shape((rows, width // 2), F32),
            shape((rows, width // 2), F32),
        ],
        input_output_aliases=aliases,
        compiler_params=params(),
        name="gradients",
    )(places, *operands)


def add_columns(keep, received):
    rows, width = keep.shape
    tile = rows // 2

    def kernel(keep_ref, received_ref, keep_out, send_out):
        total = keep_ref[...] + received_ref[...].astype(F32)
        keep_out[...] = total[:, : width // 2]
        send_out[...] = total[:, width // 2 :].astype(BF16)

    whole = pl.BlockSpec((tile, width), lambda i: (i, 0))
    half = pl.BlockSpec((tile, width // 2), lambda i: (i, 0))
    return pl.pallas_call(
        kernel,
        grid=(rows // tile,),
        in_specs=[whole, whole],
        out_specs=[half, half],
        out_shape=[shape((rows, width // 2), F32), shape((rows, width // 2), BF16)],
        compiler_params=params(),
        name="add_columns",
    )(keep, received)


def assemble(kept, received, size):
    rows, width = kept[0].shape
    chunks = len(kept)
    tile = 512

    def kernel(*refs):
        out_ref = refs[-1]
        sums = [refs[k][...] + refs[chunks + k][...].astype(F32) for k in range(chunks)]
        pieces = [sums[k][:, d * size : (d + 1) * size] for d in range(width // size) for k in range(chunks)]
        out_ref[...] = jnp.concatenate(pieces, axis=1)

    spec = pl.BlockSpec((tile, width), lambda i: (i, 0))
    return pl.pallas_call(
        kernel,
        grid=(rows // tile,),
        in_specs=[spec] * (2 * chunks),
        out_specs=pl.BlockSpec((tile, width * chunks), lambda i: (i, 0)),
        out_shape=shape((rows, width * chunks), F32),
        compiler_params=params(),
        name="assemble",
    )(*kept, *received)


def logit_gradient(expr, grads, logits, size_column, spot_rows):
    rows, genes = expr.shape
    spots = logits.shape[1]
    tile = 512

    def kernel(expr_ref, grad_ref, logit_ref, column_ref, spot_ref, out_ref):
        acc = jnp.dot(expr_ref[...], grad_ref[...], preferred_element_type=F32)
        probs = jnp.exp(logit_ref[...]) * (1.0 / spot_ref[0:1, :])
        grad = (acc + spot_ref[1:2, :]) * tile_lanes(column_ref[...], spots)
        out_ref[...] = probs * (grad - spot_ref[2:3, :])

    across = pl.BlockSpec((tile, spots), lambda i: (i, 0))
    return pl.pallas_call(
        kernel,
        grid=(rows // tile,),
        in_specs=[
            pl.BlockSpec((tile, genes), lambda i: (i, 0)),
            pl.BlockSpec((genes, spots), lambda i: (0, 0), pipeline_mode=pl.Buffered(1)),
            across,
            pl.BlockSpec((tile, LANES), lambda i: (i, 0)),
            pl.BlockSpec((3, spots), lambda i: (0, 0)),
        ],
        out_specs=across,
        out_shape=shape((rows, spots), F32),
        compiler_params=params(),
        name="logit_gradient",
    )(expr, grads, logits, size_column, spot_rows)


def on_device(logits, centroid_expr, target, sizes, counts):
    parts = lax.axis_size("cent")
    halves = bits_of(parts)
    n_spot = lax.axis_size("spot")
    spot_bits = bits_of(n_spot)
    me = lax.axis_index("cent")
    my_spot = lax.axis_index("spot")
    rows, genes = centroid_expr.shape
    spots = logits.shape[1]
    spots_all = spots * n_spot
    per_device = genes // parts
    size = per_device // CHUNKS
    counts_f = counts.astype(F32)
    order = Order()

    def bit(b):
        return ((me >> b) & 1).reshape(1)

    sums, size_column = order.run(lambda l, s: column_stats(l, s, rows // 4), logits, sizes)
    sums = sum_over(sums, "cent")
    total, mass = sums[0:1], sums[1] / sums[0]

    keeps, sends = [], []
    weights = None
    target_rows = target.reshape(parts * CHUNKS, size, spots)
    for k in range(CHUNKS):
        if k == 0:
            keep, send, weights = order.run(
                lambda l, t, c, e: predict(0, parts, bit(0), e, None, (l, t, c)), logits, total, size_column, centroid_expr
            )
        else:
            keep, send = order.run(lambda w, e, k=k: predict(k, parts, bit(0), e, w), weights, centroid_expr)
        keeps.append(keep)
        sends.append(send)
    kl_local = jnp.sum(counts_f * (jnp.log(counts_f) - jnp.log(mass)))
    kl_sum, mass_total, count_total = sum_over(jnp.stack([kl_local, jnp.sum(mass), jnp.sum(counts_f)]), "spot")

    preds, gene_parts, spot_parts, nears, fars = [], [], [], [], []
    for k in range(CHUNKS):
        keep, received = keeps[k], swap(sends[k], "cent", 0)
        for b in range(1, halves):
            keep, send = order.run(functools.partial(add_and_halve, bit(b)), keep, received)
            received = swap(send, "cent", b)
        pred, by_gene, by_spot, low = order.run(
            functools.partial(finish_rows, (me * CHUNKS + k).reshape(1)), keep, received, target_rows
        )
        preds.append(pred)
        gene_parts.append(by_gene)
        spot_parts.append(by_spot)
        for b in range(halves - 1, 0, -1):
            low = jnp.concatenate([low, swap(low, "cent", b)], axis=0)
        nears.append(low)
        fars.append(swap(low, "cent", 0))
    pred_rows = jnp.concatenate(preds, axis=0)

    gene_dot, gene_pp, gene_tt = sum_over(jnp.concatenate(gene_parts, axis=1), "spot")
    gene_rp, gene_rt = lax.rsqrt(gene_pp + EPS), lax.rsqrt(gene_tt + EPS)
    cos_gene = gene_dot * gene_rp * gene_rt
    mine = jnp.stack([(-1.0 / genes) * gene_rp * gene_rt, (1.0 / genes) * cos_gene / (gene_pp + EPS), cos_gene])
    slots = jnp.where(jnp.arange(parts)[:, None, None] == me, mine[None], 0.0)
    both = jnp.concatenate([slots.reshape(-1), sum(spot_parts).reshape(-1)])
    both = sum_over(both, "cent")
    gene_terms = both[: 3 * genes].reshape(parts, 3, CHUNKS, size).transpose(1, 2, 0, 3).reshape(3, CHUNKS, parts * size)
    spot_dot, spot_pp, spot_tt = both[3 * genes :].reshape(3, spots)
    spot_rp, spot_rt = lax.rsqrt(spot_pp + EPS), lax.rsqrt(spot_tt + EPS)
    cos_spot = spot_dot * spot_rp * spot_rt
    spot_terms = jnp.stack([(-1.0 / spots_all) * spot_rp * spot_rt, (1.0 / spots_all) * cos_spot / (spot_pp + EPS)])
    gene_mean = jnp.sum(gene_terms[2]) / genes
    spot_mean = sum_over(jnp.sum(cos_spot), "spot") / spots_all
    kl = kl_sum / count_total + jnp.log(mass_total) - jnp.log(count_total)
    losses = jnp.stack([kl - gene_mean - spot_mean, gene_mean, spot_mean, kl])

    per_spot = parts // n_spot
    device_at = [me ^ reversed_bits(j, halves) for j in range(parts)]
    place_of = []
    for d in range(parts):
        apart = (d // per_spot) ^ my_spot
        place_of.append(reversed_bits(apart, spot_bits) * per_spot + d % per_spot)
    places = jnp.stack([jnp.stack(device_at), jnp.stack(place_of)]).astype(jnp.int32)
    target_chunks = target.reshape(parts, CHUNKS, size, spots)
    grads, backs, kept, arrived = None, [], [], []
    for k in range(CHUNKS):
        operands = (nears[k], fars[k], target_chunks, gene_terms[:2, k], spot_terms, weights)
        step = functools.partial(gradients, k, places)
        if grads is None:
            grads, back, keep, send = order.run(lambda *a: step(*a, None), *operands)
        else:
            grads, back, keep, send = order.run(step, *operands, grads)
        backs.append(back)
        received = swap(send, "spot", 0)
        for b in range(1, spot_bits):
            keep, send = order.run(add_columns, keep, received)
            received = swap(send, "spot", b)
        kept.append(keep)
        arrived.append(received)
    mass_grad = 1.0 / mass_total - counts_f / (count_total * mass)
    back_total = sum(backs)[0] + mass * mass_grad
    spot_rows = jnp.stack([total[0], mass_grad, back_total])
    (logit_grad,) = order.run(
        lambda *a: (logit_gradient(*a),), centroid_expr, grads.reshape(genes, spots), logits, size_column, spot_rows
    )
    (centroid_grad,) = order.run(lambda *a: (assemble(a[:CHUNKS], a[CHUNKS:], size),), *kept, *arrived)
    return losses, pred_rows, logit_grad, centroid_grad


def solution(mesh):
    in_specs = (P("cent", "spot"), P("cent", None), P(None, "spot"), P("cent"), P("spot"))
    out_specs = (P(), P("cent", "spot"), P("cent", "spot"), P("cent", "spot"))
    return jax.shard_map(
        on_device, mesh=mesh, in_specs=in_specs, out_specs=out_specs, check_vma=False
    )
```

```python
import functools

import jax
import jax.numpy as jnp
from jax import lax
from jax.experimental import pallas as pl
from jax.experimental.pallas import tpu as pltpu
from jax.sharding import PartitionSpec as P

EPS = 1e-06
F32 = jnp.float32
BF16 = jnp.bfloat16
LANES = 128
CHUNKS = 4
COST = pl.CostEstimate(flops=1, transcendentals=0, bytes_accessed=1)


def params(mebibytes):
    return pltpu.CompilerParams(vmem_limit_bytes=mebibytes << 20)


def shape(dims, dtype):
    return jax.ShapeDtypeStruct(dims, dtype)


def in_hbm(value):
    return pltpu.with_memory_space_constraint(value, pltpu.HBM)


def bits_of(count):
    return count.bit_length() - 1


def reversed_bits(value, bits):
    return sum(((value >> b) & 1) << (bits - 1 - b) for b in range(bits))


def swap(value, axis, bit):
    count = lax.axis_size(axis)
    return lax.ppermute(value, axis, [(i, i ^ (1 << bit)) for i in range(count)])


def sum_over(value, axis):
    for bit in range(bits_of(lax.axis_size(axis))):
        value = value + swap(value, axis, bit)
    return value


def tile_lanes(column, width):
    return jnp.concatenate([column] * (width // LANES), axis=1)


def column_of(row, length):
    return jnp.transpose(jnp.broadcast_to(row, (LANES, length)))


class Order:
    def __init__(self):
        self.last = None

    def run(self, step, first, *others):
        if self.last is not None:
            first = lax.optimization_barrier((first, self.last))[0]
        results = step(first, *others)
        self.last = results[-1]
        return results


def column_stats(logits, sizes, tile):
    rows, spots = logits.shape

    def kernel(logit_ref, size_ref, sums_ref, column_ref, acc):
        step = pl.program_id(0)
        expo = jnp.exp(logit_ref[...])
        column = column_of(size_ref[...].astype(F32).reshape(1, tile), tile)
        column_ref[...] = column
        mass = expo * tile_lanes(column, spots)
        total = expo.reshape(tile // 8, 8, spots).sum(0)
        mass = mass.reshape(tile // 8, 8, spots).sum(0)

        @pl.when(step == 0)
        def _():
            acc[0] = total
            acc[1] = mass

        @pl.when(step > 0)
        def _():
            acc[0] += total
            acc[1] += mass

        @pl.when(step == pl.num_programs(0) - 1)
        def _():
            sums_ref[0:1, :] = acc[0].sum(0, keepdims=True)
            sums_ref[1:2, :] = acc[1].sum(0, keepdims=True)

    return pl.pallas_call(
        kernel,
        grid=(rows // tile,),
        in_specs=[
            pl.BlockSpec((tile, spots), lambda i: (i, 0)),
            pl.BlockSpec((1, 1, tile), lambda i: (i, 0, 0)),
        ],
        out_specs=[
            pl.BlockSpec((2, spots), lambda i: (0, 0)),
            pl.BlockSpec((tile, LANES), lambda i: (i, 0)),
        ],
        out_shape=[shape((2, spots), F32), shape((rows, LANES), F32)],
        scratch_shapes=[pltpu.VMEM((2, 8, spots), F32)],
        cost_estimate=COST,
        compiler_params=params(20),
        name="column_stats",
    )(in_hbm(logits), sizes.reshape(rows // tile, 1, tile))


def predict(chunk, parts, low_bit, expr, weights, first=None):
    rows, genes = expr.shape
    per_device = genes // parts
    size = per_device // CHUNKS
    starts = [d * per_device + chunk * size for d in range(parts)]
    blocks = sorted({s // LANES for s in starts})
    spots = (weights if first is None else first[0]).shape[1]
    tile = 512

    def kernel(bit_ref, *refs):
        expr_refs = refs[: len(blocks)]
        rest = refs[len(blocks) :]
        if first is None:
            weight_ref, keep_ref, send_ref, turned = rest
        else:
            logit_ref, total_ref, column_ref, keep_ref, send_ref, weight_ref, turned = rest

        @pl.when(pl.program_id(0) == 0)
        def _():
            for at, block in enumerate(blocks):
                block_t = jnp.transpose(expr_refs[at][...])
                for d, start in enumerate(starts):
                    if start // LANES == block:
                        turned[d * size : (d + 1) * size, :] = block_t[start % LANES : start % LANES + size]

        if first is not None:
            scale = 1.0 / total_ref[...]
            weight = jnp.exp(logit_ref[...]) * scale * tile_lanes(column_ref[...], tile)
            weight_ref[...] = weight.astype(BF16)
        out = jnp.dot(turned[...], weight_ref[...], preferred_element_type=F32)
        even = bit_ref[0] == 0
        for j in range(parts // 2):
            a = out[2 * j * size : (2 * j + 1) * size]
            b = out[(2 * j + 1) * size : (2 * j + 2) * size]
            keep_ref[j] = jnp.where(even, a, b)
            send_ref[j] = jnp.where(even, b, a).astype(BF16)

    in_specs = [pl.BlockSpec((rows, LANES), lambda i, s, b=b: (0, b), pipeline_mode=pl.Buffered(1)) for b in blocks]
    operands = [in_hbm(expr)] * len(blocks)
    half = pl.BlockSpec((parts // 2, size, tile), lambda i, s: (0, 0, i))
    columns = pl.BlockSpec((rows, tile), lambda i, s: (0, i))
    out_specs = [half, half]
    out_shapes = [pltpu.HBM((parts // 2, size, spots), F32), shape((parts // 2, size, spots), BF16)]
    if first is None:
        in_specs.append(columns)
        operands.append(in_hbm(weights))
    else:
        in_specs += [columns, pl.BlockSpec((1, tile), lambda i, s: (0, i)), pl.BlockSpec((rows, LANES), lambda i, s: (0, 0))]
        operands += [in_hbm(first[0]), *first[1:]]
        out_specs.append(columns)
        out_shapes.append(pltpu.HBM((rows, spots), BF16))
    return pl.pallas_call(
        kernel,
        grid_spec=pltpu.PrefetchScalarGridSpec(
            num_scalar_prefetch=1,
            grid=(spots // tile,),
            in_specs=in_specs,
            out_specs=out_specs,
            scratch_shapes=[pltpu.VMEM((parts * size, rows), BF16)],
        ),
        out_shape=out_shapes,
        cost_estimate=COST,
        compiler_params=params(20 if first is None else 36),
        name="predict",
    )(low_bit, *operands)


def add_and_halve(bit, keep, received):
    count, size, spots = keep.shape

    def kernel(bit_ref, keep_ref, received_ref, keep_out, send_out):
        a = keep_ref[0] + received_ref[0].astype(F32)
        b = keep_ref[1] + received_ref[1].astype(F32)
        even = bit_ref[0] == 0
        keep_out[0] = jnp.where(even, a, b)
        send_out[0] = jnp.where(even, b, a).astype(BF16)

    pair = pl.BlockSpec((2, size, spots), lambda i, s: (i, 0, 0))
    one = pl.BlockSpec((1, size, spots), lambda i, s: (i, 0, 0))
    return pl.pallas_call(
        kernel,
        grid_spec=pltpu.PrefetchScalarGridSpec(
            num_scalar_prefetch=1, grid=(count // 2,), in_specs=[pair, pair], out_specs=[one, one]
        ),
        out_shape=[pltpu.HBM((count // 2, size, spots), F32), shape((count // 2, size, spots), BF16)],
        cost_estimate=COST,
        compiler_params=params(10),
        name="add_and_halve",
    )(bit, in_hbm(keep), received)


def finish_rows(row, keep, received, target_rows, running):
    _, size, spots = keep.shape

    def kernel(row_ref, keep_ref, received_ref, target_ref, *refs):
        pred_ref, gene_ref, spot_ref, low_ref = refs[-4:]
        pred = keep_ref[0] + received_ref[0].astype(F32)
        target = target_ref[0].astype(F32)
        pred_ref[...] = pred
        low_ref[0] = pred.astype(BF16)
        for at, product in enumerate((pred * target, pred * pred, target * target)):
            by_gene = jnp.sum(product, axis=1, keepdims=True)
            by_gene = jnp.transpose(jnp.broadcast_to(by_gene, (size, LANES)))
            gene_ref[0, at : at + 1, :] = by_gene[0:1, :]
            by_spot = jnp.sum(product, axis=0, keepdims=True)
            if running is not None:
                by_spot = by_spot + refs[0][at : at + 1, :]
            spot_ref[at : at + 1, :] = by_spot

    one = pl.BlockSpec((1, size, spots), lambda i, s: (0, 0, 0))
    by_spot = pl.BlockSpec((3, spots), lambda i, s: (0, 0))
    return pl.pallas_call(
        kernel,
        grid_spec=pltpu.PrefetchScalarGridSpec(
            num_scalar_prefetch=1,
            grid=(1,),
            in_specs=[one, one, pl.BlockSpec((1, size, spots), lambda i, s: (s[0], 0, 0))]
            + [by_spot] * (running is not None),
            out_specs=[
                pl.BlockSpec((size, spots), lambda i, s: (0, 0)),
                pl.BlockSpec((1, 3, size), lambda i, s: (0, 0, 0)),
                by_spot,
                one,
            ],
        ),
        out_shape=[
            pltpu.HBM((size, spots), F32),
            shape((1, 3, size), F32),
            shape((3, spots), F32),
            shape((1, size, spots), BF16),
        ],
        cost_estimate=COST,
        compiler_params=params(10),
        name="finish_rows",
    )(row, in_hbm(keep), received, in_hbm(target_rows), *([] if running is None else [running]))


def row_of(*values):
    lane = lax.broadcasted_iota(jnp.int32, (1, LANES), 1)
    return sum(jnp.where(lane == at, value, 0.0) for at, value in enumerate(values))


def spot_totals(sums, counts):
    def kernel(sums_ref, counts_ref, out_ref):
        mass = sums_ref[1:2, :] / sums_ref[0:1, :]
        count = counts_ref[...]
        diverged = count * (jnp.log(count) - jnp.log(mass))
        out_ref[...] = row_of(jnp.sum(diverged), jnp.sum(mass), jnp.sum(count))

    return pl.pallas_call(
        kernel, out_shape=shape((1, LANES), F32), cost_estimate=COST, compiler_params=params(4), name="spot_totals"
    )(sums, counts)


def gene_slots(me, gene_sums, spot_sums, parts):
    chunks, _, size = gene_sums.shape
    spots = spot_sums.shape[1]
    genes = parts * chunks * size
    width = max(genes, spots)

    def kernel(me_ref, gene_ref, spot_ref, out_ref):
        out_ref[...] = jnp.zeros((8, width), F32)
        out_ref[3:6, 0:spots] = spot_ref[...]
        lane = lax.broadcasted_iota(jnp.int32, (1, parts * size), 1)
        mine = (lane >= me_ref[0] * size) & (lane < (me_ref[0] + 1) * size)
        for k in range(chunks):
            dot, pp, tt = (gene_ref[k, at : at + 1, :] for at in range(3))
            scale = lax.rsqrt(pp + EPS) * lax.rsqrt(tt + EPS)
            cosine = dot * scale
            for at, value in enumerate(((-1.0 / genes) * scale, (1.0 / genes) * cosine / (pp + EPS), cosine)):
                spread = jnp.concatenate([value] * parts, axis=1)
                out_ref[at : at + 1, k * parts * size : (k + 1) * parts * size] = jnp.where(mine, spread, 0.0)

    smem = pl.BlockSpec(memory_space=pltpu.SMEM)
    vmem = pl.BlockSpec(memory_space=pltpu.VMEM)
    return pl.pallas_call(
        kernel,
        in_specs=[smem, vmem, vmem],
        out_shape=shape((8, width), F32),
        cost_estimate=COST,
        compiler_params=params(4),
        name="gene_slots",
    )(me, gene_sums, spot_sums)


def gradient_terms(slots, genes, spots, chunks, spots_all):
    def kernel(slots_ref, gene_ref, spot_ref, sums_ref):
        for k in range(chunks):
            gene_ref[k] = slots_ref[0:2, k * (genes // chunks) : (k + 1) * (genes // chunks)]
        dot, pp, tt = (slots_ref[3 + at : 4 + at, 0:spots] for at in range(3))
        scale = lax.rsqrt(pp + EPS) * lax.rsqrt(tt + EPS)
        cosine = dot * scale
        spot_ref[0:1, :] = (-1.0 / spots_all) * scale
        spot_ref[1:2, :] = (1.0 / spots_all) * cosine / (pp + EPS)
        sums_ref[...] = row_of(jnp.sum(slots_ref[2:3, 0:genes]), jnp.sum(cosine))

    return pl.pallas_call(
        kernel,
        out_shape=[shape((chunks, 2, genes // chunks), F32), shape((2, spots), F32), shape((1, LANES), F32)],
        cost_estimate=COST,
        compiler_params=params(4),
        name="gradient_terms",
    )(slots)


def loss_row(cosines, summed, totals, genes, spots_all):
    def kernel(cosines_ref, summed_ref, totals_ref, out_ref):
        gene_mean = cosines_ref[0:1, 0:1] / genes
        spot_mean = summed_ref[0:1, 1:2] / spots_all
        kl_sum, mass_total, count_total = (totals_ref[0:1, at : at + 1] for at in range(3))
        kl = kl_sum / count_total + jnp.log(mass_total) - jnp.log(count_total)
        out_ref[...] = row_of(kl - gene_mean - spot_mean, gene_mean, spot_mean, kl)

    return pl.pallas_call(
        kernel, out_shape=shape((1, LANES), F32), cost_estimate=COST, compiler_params=params(4), name="loss_row"
    )(cosines, summed, totals)


def gradients(chunk, places, pred_near, pred_far, target, gene_rows, spot_rows, weights, grads):
    parts, chunks, size, spots = target.shape
    rows = weights.shape[0]
    tile = 512
    width = parts * size

    def kernel(places_ref, near_ref, far_ref, target_ref, gene_ref, spot_ref, weight_ref, *refs):
        grad_ref, back_ref, keep_ref, send_ref, turned, columns = refs[-6:]

        @pl.when(pl.program_id(0) == 0)
        def _():
            columns[0] = column_of(gene_ref[0, 0:1, :], width)
            columns[1] = column_of(gene_ref[0, 1:2, :], width)
            back = jnp.zeros((1, spots), F32)
            for j in range(parts):
                d = places_ref[0, j]
                at = pl.multiple_of(d * size, size)
                pred = (near_ref[j] if j < parts // 2 else far_ref[j - parts // 2]).astype(F32)
                by_target = tile_lanes(columns[0, pl.ds(at, size), :], spots) + spot_ref[0:1, :]
                by_pred = tile_lanes(columns[1, pl.ds(at, size), :], spots) + spot_ref[1:2, :]
                grad = (target_ref[d, 0].astype(F32) * by_target + pred * by_pred).astype(BF16)
                grad_ref[d, 0] = grad
                turned[pl.ds(pl.multiple_of(places_ref[1, d] * size, size), size), :] = grad
                back = back + jnp.sum(grad.astype(F32) * pred, axis=0, keepdims=True)
            back_ref[...] = back

        out = lax.dot_general(weight_ref[...], turned[...], (((1,), (1,)), ((), ())), preferred_element_type=F32)
        keep_ref[...] = out[:, : width // 2]
        send_ref[...] = out[:, width // 2 :]

    half = pl.BlockSpec((parts // 2, size, spots), lambda i, s: (0, 0, 0))
    of_chunk = pl.BlockSpec((parts, 1, size, spots), lambda i, s: (0, chunk, 0, 0))
    piece = pl.BlockSpec((tile, width // 2), lambda i, s: (i, 0))
    in_specs = [
        half,
        half,
        of_chunk,
        pl.BlockSpec((1, 2, width), lambda i, s: (chunk, 0, 0)),
        pl.BlockSpec((2, spots), lambda i, s: (0, 0)),
        pl.BlockSpec((tile, spots), lambda i, s: (i, 0)),
    ]
    operands = [pred_near, pred_far, in_hbm(target), gene_rows, spot_rows, in_hbm(weights)]
    aliases = {}
    if grads is not None:
        in_specs.append(pl.BlockSpec(memory_space=pl.ANY))
        operands.append(in_hbm(grads))
        aliases = {len(operands): 0}
    return pl.pallas_call(
        kernel,
        grid_spec=pltpu.PrefetchScalarGridSpec(
            num_scalar_prefetch=1,
            grid=(rows // tile,),
            in_specs=in_specs,
            out_specs=[of_chunk, pl.BlockSpec((1, spots), lambda i, s: (0, 0)), piece, piece],
            scratch_shapes=[pltpu.VMEM((width, spots), BF16), pltpu.VMEM((2, width, LANES), F32)],
        ),
        out_shape=[
            pltpu.HBM((parts, chunks, size, spots), BF16),
            shape((1, spots), F32),
            shape((rows, width // 2), F32),
            shape((rows, width // 2), F32),
        ],
        input_output_aliases=aliases,
        cost_estimate=COST,
        compiler_params=params(26),
        name="gradients",
    )(places, *operands)


def add_columns(keep, received):
    rows, width = keep.shape
    tile = rows // 2

    def kernel(keep_ref, received_ref, keep_out, send_out):
        total = keep_ref[...] + received_ref[...].astype(F32)
        keep_out[...] = total[:, : width // 2]
        send_out[...] = total[:, width // 2 :].astype(BF16)

    whole = pl.BlockSpec((tile, width), lambda i: (i, 0))
    half = pl.BlockSpec((tile, width // 2), lambda i: (i, 0))
    return pl.pallas_call(
        kernel,
        grid=(rows // tile,),
        in_specs=[whole, whole],
        out_specs=[half, half],
        out_shape=[shape((rows, width // 2), F32), shape((rows, width // 2), BF16)],
        cost_estimate=COST,
        compiler_params=params(20),
        name="add_columns",
    )(keep, received)


def assemble(kept, received, size):
    rows, width = kept[0].shape
    chunks = len(kept)
    tile = 512

    def kernel(*refs):
        out_ref = refs[-1]
        sums = [refs[k][...] + refs[chunks + k][...].astype(F32) for k in range(chunks)]
        pieces = [sums[k][:, d * size : (d + 1) * size] for d in range(width // size) for k in range(chunks)]
        out_ref[...] = jnp.concatenate(pieces, axis=1)

    spec = pl.BlockSpec((tile, width), lambda i: (i, 0))
    return pl.pallas_call(
        kernel,
        grid=(rows // tile,),
        in_specs=[spec] * (2 * chunks),
        out_specs=pl.BlockSpec((tile, width * chunks), lambda i: (i, 0)),
        out_shape=shape((rows, width * chunks), F32),
        cost_estimate=COST,
        compiler_params=params(24),
        name="assemble",
    )(*kept, *received)


def logit_gradient(sums, expr, grads, logits, size_column, counts, totals, backs):
    rows, genes = expr.shape
    spots = logits.shape[1]
    tile = 512

    def kernel(sums_ref, expr_ref, grad_ref, logit_ref, column_ref, counts_ref, totals_ref, *refs):
        back_refs, out_ref = refs[:-1], refs[-1]
        inverse = 1.0 / sums_ref[0:1, :]
        mass = sums_ref[1:2, :] / sums_ref[0:1, :]
        mass_grad = 1.0 / totals_ref[0:1, 1:2] - counts_ref[...] / (totals_ref[0:1, 2:3] * mass)
        back = sum(ref[...] for ref in back_refs) + mass * mass_grad
        acc = jnp.dot(expr_ref[...], grad_ref[...], preferred_element_type=F32)
        probs = jnp.exp(logit_ref[...]) * inverse
        grad = (acc + mass_grad) * tile_lanes(column_ref[...], spots)
        out_ref[...] = probs * (grad - back)

    across = pl.BlockSpec((tile, spots), lambda i: (i, 0))
    row = pl.BlockSpec((1, spots), lambda i: (0, 0))
    return pl.pallas_call(
        kernel,
        grid=(rows // tile,),
        in_specs=[
            pl.BlockSpec((2, spots), lambda i: (0, 0)),
            pl.BlockSpec((tile, genes), lambda i: (i, 0)),
            pl.BlockSpec((genes, spots), lambda i: (0, 0), pipeline_mode=pl.Buffered(1)),
            across,
            pl.BlockSpec((tile, LANES), lambda i: (i, 0)),
            row,
            pl.BlockSpec((1, LANES), lambda i: (0, 0)),
        ]
        + [row] * len(backs),
        out_specs=across,
        out_shape=pltpu.HBM((rows, spots), F32),
        cost_estimate=COST,
        compiler_params=params(34),
        name="logit_gradient",
    )(sums, in_hbm(expr), in_hbm(grads), in_hbm(logits), size_column, counts, totals, *backs)


def on_device(logits, centroid_expr, target, sizes, counts):
    parts = lax.axis_size("cent")
    halves = bits_of(parts)
    n_spot = lax.axis_size("spot")
    spot_bits = bits_of(n_spot)
    me = lax.axis_index("cent")
    my_spot = lax.axis_index("spot")
    rows, genes = centroid_expr.shape
    spots = logits.shape[1]
    spots_all = spots * n_spot
    per_device = genes // parts
    size = per_device // CHUNKS
    counts_f = counts.astype(F32).reshape(1, spots)
    order = Order()

    def bit(b):
        return ((me >> b) & 1).reshape(1)

    sums, size_column = order.run(lambda l, s: column_stats(l, s, rows // 4), logits, sizes)
    sums = sum_over(sums, "cent")

    target_rows = target.reshape(parts * CHUNKS, size, spots)
    target_chunks = target.reshape(parts, CHUNKS, size, spots)
    per_spot = parts // n_spot
    device_at = [me ^ reversed_bits(j, halves) for j in range(parts)]
    place_of = []
    for d in range(parts):
        apart = (d // per_spot) ^ my_spot
        place_of.append(reversed_bits(apart, spot_bits) * per_spot + d % per_spot)
    places = jnp.stack([jnp.stack(device_at), jnp.stack(place_of)]).astype(jnp.int32)

    made = {}
    keeps, arrived, preds, gene_sums, nears, fars, backs, kept, landed = ([None] * CHUNKS for _ in range(9))

    def predict_step(k):
        if k == 0:
            keeps[k], send, made["weights"] = order.run(
                lambda t, l, c, e: predict(0, parts, bit(0), e, None, (l, t, c)), sums[0:1], logits, size_column, centroid_expr
            )
        else:
            keeps[k], send = order.run(lambda b, w, e: predict(k, parts, b, e, w), bit(0), made["weights"], centroid_expr)
        arrived[k] = swap(send, "cent", 0)

    def halve_step(b):
        def step(k):
            keeps[k], send = order.run(add_and_halve, bit(b), keeps[k], arrived[k])
            arrived[k] = swap(send, "cent", b)

        return step

    def finish_step(k):
        preds[k], gene_sums[k], made["spots"], nears[k] = order.run(
            finish_rows, (me * CHUNKS + k).reshape(1), keeps[k], arrived[k], target_rows, made.get("spots")
        )
        fars[k] = swap(nears[k], "cent", halves - 1)

    def double_step(b):
        def step(k):
            (nears[k],) = order.run(lambda *a: (jnp.concatenate(a, axis=0),), nears[k], fars[k])
            fars[k] = swap(nears[k], "cent", b)

        return step

    def totals_step():
        (totals,) = order.run(lambda *a: (spot_totals(*a),), sums, counts_f)
        made["totals"] = sum_over(totals, "spot")

    def slots_step():
        by_gene = sum_over(jnp.concatenate(gene_sums, axis=0), "spot")
        (slots,) = order.run(lambda *a: (gene_slots(*a, parts),), me.reshape(1), by_gene, made["spots"])
        made["slots"] = sum_over(slots, "cent")

    def terms_step():
        made["genes"], made["terms"], made["cosines"] = order.run(
            lambda a: gradient_terms(a, genes, spots, CHUNKS, spots_all), made["slots"]
        )
        made["summed"] = sum_over(made["cosines"], "spot")

    def losses_step():
        (made["losses"],) = order.run(
            lambda *a: (loss_row(*a, genes, spots_all),), made["cosines"], made["summed"], made["totals"]
        )

    def gradients_step(k):
        operands = (nears[k], fars[k], target_chunks, made["genes"], made["terms"], made["weights"], made.get("grads"))
        made["grads"], backs[k], kept[k], send = order.run(functools.partial(gradients, k), places, *operands)
        landed[k] = swap(send, "spot", 0)

    def columns_step(b):
        def step(k):
            kept[k], send = order.run(add_columns, kept[k], landed[k])
            landed[k] = swap(send, "spot", b)

        return step

    def logits_step():
        (made["logit_grad"],) = order.run(
            lambda *a: (logit_gradient(*a[:7], a[7:]),),
            sums, centroid_expr, made["grads"].reshape(genes, spots), logits, size_column, counts_f, made["totals"], *backs
        )

    def centroids_step():
        (made["centroid_grad"],) = order.run(lambda *a: (assemble(a[:CHUNKS], a[CHUNKS:], size),), *kept, *landed)

    steps = {"P": predict_step, "F": finish_step, "G": gradients_step, "T": totals_step, "S": slots_step}
    steps |= {"R": terms_step, "L": losses_step, "X": logits_step, "Y": centroids_step}
    steps |= {f"a{b}": halve_step(b) for b in range(1, halves)}
    steps |= {f"c{b}": double_step(b) for b in range(halves - 1)}
    steps |= {f"e{b}": columns_step(b) for b in range(1, spot_bits)}
    for name in schedule(halves, spot_bits).split():
        step, _, k = name.partition(".")
        steps[step](*([int(k)] if k else []))
    pred_rows = jnp.concatenate(preds, axis=0)
    return made["losses"][0, :4], pred_rows, made["logit_grad"], made["centroid_grad"]


def schedule(halves, spot_bits):
    if (halves, spot_bits) == (3, 2):
        return (
            "P.0 P.1 P.2 a1.0 P.3 a2.0 a1.1 F.0 a2.1 c1.0 a1.2 F.1 c0.0 a2.2 c1.1 a1.3 F.2 c0.1 a2.3 c1.2 F.3 c0.2 "
            "T S c1.3 c0.3 R G.0 G.1 e1.0 L G.2 e1.1 G.3 e1.2 e1.3 X Y"
        )
    forward = ["P", *(f"a{b}" for b in range(1, halves)), "F", *(f"c{b}" for b in range(halves - 2, -1, -1))]
    backward = ["G", *(f"e{b}" for b in range(1, spot_bits))]
    waves = [
        [f"{chain[wave - k]}.{k}" for wave in range(len(chain) + CHUNKS) for k in range(CHUNKS) if 0 <= wave - k < len(chain)]
        for chain in (forward, backward)
    ]
    return " ".join(waves[0] + ["T", "S", "R", "L"] + waves[1] + ["X", "Y"])


def solution(mesh):
    in_specs = (P("cent", "spot"), P("cent", None), P(None, "spot"), P("cent"), P("spot"))
    out_specs = (P(), P("cent", "spot"), P("cent", "spot"), P("cent", "spot"))
    return jax.shard_map(
        on_device, mesh=mesh, in_specs=in_specs, out_specs=out_specs, check_vma=False
    )
```

```python
import functools

import jax
import jax.numpy as jnp
from jax import lax
from jax.experimental import pallas as pl
from jax.experimental.pallas import tpu as pltpu
from jax.sharding import PartitionSpec as P

EPS = 1e-06
F32 = jnp.float32
BF16 = jnp.bfloat16
LANES = 128
CHUNKS = 4
TILE_P = 512
TILE_G = 1280
TILE_X = 512
TILE_Y = 512
COST = pl.CostEstimate(flops=1, transcendentals=0, bytes_accessed=1)


def params(mebibytes):
    return pltpu.CompilerParams(vmem_limit_bytes=mebibytes << 20)


def shape(dims, dtype):
    return jax.ShapeDtypeStruct(dims, dtype)


def in_hbm(value):
    return pltpu.with_memory_space_constraint(value, pltpu.HBM)


def bits_of(count):
    return count.bit_length() - 1


def reversed_bits(value, bits):
    return sum(((value >> b) & 1) << (bits - 1 - b) for b in range(bits))


def bit_order(chunk, bits):
    return (1, 0, *range(2, bits)) if chunk == 1 and bits > 2 else tuple(range(bits))


def place_among(device, order):
    return sum(((device >> bit) & 1) << at for at, bit in enumerate(order))


def exchange(value, axis, bits):
    return lax.ppermute(value, axis, [(i, i ^ bits) for i in range(lax.axis_size(axis))])


def swap(value, axis, bit):
    return exchange(value, axis, 1 << bit)


def sum_over(value, axis):
    for bit in range(bits_of(lax.axis_size(axis))):
        value = value + swap(value, axis, bit)
    return value


def tile_lanes(column, width):
    return jnp.concatenate([column] * (width // LANES), axis=1)


def column_of(row, length):
    return jnp.transpose(jnp.broadcast_to(row, (LANES, length)))


class Order:
    def __init__(self):
        self.last = ()

    def wait(self, value):
        self.last += (value,)

    def run(self, step, first, *others):
        if self.last:
            first = lax.optimization_barrier((first, *self.last))[0]
        results = step(first, *others)
        self.last = (results[-1],)
        return results


def column_stats(index, logits, sizes, tile):
    rows, spots = logits.shape

    def kernel(index_ref, logit_ref, size_ref, sums_ref, column_ref, acc):
        step = pl.program_id(0)
        expo = jnp.exp(logit_ref[...])
        column = column_of(size_ref[...].astype(F32).reshape(1, tile), tile)
        column_ref[...] = column
        mass = expo * tile_lanes(column, spots)
        total = expo.reshape(tile // 8, 8, spots).sum(0)
        mass = mass.reshape(tile // 8, 8, spots).sum(0)

        @pl.when(step == 0)
        def _():
            acc[0] = total
            acc[1] = mass

        @pl.when(step > 0)
        def _():
            acc[0] += total
            acc[1] += mass

        @pl.when(step == pl.num_programs(0) - 1)
        def _():
            sums_ref[0:1, :] = acc[0].sum(0, keepdims=True)
            sums_ref[1:2, :] = acc[1].sum(0, keepdims=True)

    return pl.pallas_call(
        kernel,
        grid_spec=pltpu.PrefetchScalarGridSpec(
            num_scalar_prefetch=1,
            grid=(rows // tile,),
            in_specs=[
                pl.BlockSpec((tile, spots), lambda i, s: (i, 0)),
                pl.BlockSpec((1, 1, tile), lambda i, s: (i, 0, 0)),
            ],
            out_specs=[
                pl.BlockSpec((2, spots), lambda i, s: (0, 0)),
                pl.BlockSpec((tile, LANES), lambda i, s: (i, 0)),
            ],
            scratch_shapes=[pltpu.VMEM((2, 8, spots), F32)],
        ),
        out_shape=[shape((2, spots), F32), shape((rows, LANES), F32)],
        cost_estimate=COST,
        compiler_params=params(20),
        name="column_stats",
    )(index, in_hbm(logits), sizes.reshape(rows // tile, 1, tile))


def predict(index, chunk, parts, expr, weights, first=None, turned_before=None):
    rows = first[0].shape[0] if first is not None else weights.shape[0]
    spots = (weights if first is None else first[0]).shape[1]
    genes = expr.shape[1]
    per_device = genes // parts
    size = per_device // CHUNKS
    width = parts * size
    starts = [d * per_device + chunk * size for d in range(parts)]
    blocks = sorted({s // LANES for s in starts})
    shares = chunk + 1 < CHUNKS and sorted({(s + size) // LANES for s in starts}) == blocks
    shares = shares and turned_before is None
    tile = TILE_P
    order = bit_order(chunk, bits_of(parts))
    order_next = bit_order(chunk + 1, bits_of(parts))
    n_in = (1 if turned_before is not None else len(blocks)) + (1 if first is None else 3)

    def kernel(index_ref, *refs):
        inputs, rest = refs[:n_in], refs[n_in:]
        keep_ref, send_ref = rest[:2]
        turned = inputs[0] if turned_before is not None else rest[-1]
        turned_next = rest[2] if shares else None
        if first is None:
            weight_ref = inputs[-1]
        else:
            logit_ref, sums_ref, column_ref = inputs[-3:]
            weight_ref = rest[3 if shares else 2]

        if turned_before is None:

            @pl.when(pl.program_id(0) == 0)
            def _():
                for number, block in enumerate(blocks):
                    block_t = jnp.transpose(inputs[number][...])
                    for d, start in enumerate(starts):
                        if start // LANES == block:
                            at_row = start % LANES
                            at = place_among(d, order) * size
                            turned[at : at + size, :] = block_t[at_row : at_row + size]
                            if shares:
                                at = place_among(d, order_next) * size
                                turned_next[at : at + size, :] = block_t[at_row + size : at_row + 2 * size]

        if first is not None:
            scale = 1.0 / sums_ref[0:1, :]
            weight = jnp.exp(logit_ref[...]) * scale * tile_lanes(column_ref[...], tile)
            weight_ref[...] = weight.astype(BF16)
        out = jnp.dot(turned[...], weight_ref[...], preferred_element_type=F32)
        even = ((index_ref[0] >> order[0]) & 1) == 0
        for j in range(parts // 2):
            a = out[2 * j * size : (2 * j + 1) * size]
            b = out[(2 * j + 1) * size : (2 * j + 2) * size]
            keep_ref[j] = jnp.where(even, a, b)
            send_ref[j] = jnp.where(even, b, a).astype(BF16)

    half = pl.BlockSpec((parts // 2, size, tile), lambda i, s: (0, 0, i))
    columns = pl.BlockSpec((rows, tile), lambda i, s: (0, i))
    whole = pl.BlockSpec((width, rows), lambda i, s: (0, 0))
    if turned_before is None:
        in_specs = [
            pl.BlockSpec((rows, LANES), lambda i, s, b=b: (0, b), pipeline_mode=pl.Buffered(1)) for b in blocks
        ]
        operands = [in_hbm(expr)] * len(blocks)
    else:
        in_specs, operands = [whole], [turned_before]
    out_specs = [half, half]
    out_shapes = [shape((parts // 2, size, spots), F32), shape((parts // 2, size, spots), BF16)]
    if shares:
        out_specs.append(whole)
        out_shapes.append(shape((width, rows), BF16))
    if first is None:
        in_specs.append(columns)
        operands.append(weights)
    else:
        in_specs += [columns, pl.BlockSpec((2, tile), lambda i, s: (0, i)), pl.BlockSpec((rows, LANES), lambda i, s: (0, 0))]
        operands += [in_hbm(first[0]), *first[1:]]
        out_specs.append(columns)
        out_shapes.append(shape((rows, spots), BF16))
    return pl.pallas_call(
        kernel,
        grid_spec=pltpu.PrefetchScalarGridSpec(
            num_scalar_prefetch=1,
            grid=(spots // tile,),
            in_specs=in_specs,
            out_specs=out_specs,
            scratch_shapes=[pltpu.VMEM((width, rows), BF16)] if turned_before is None else [],
        ),
        out_shape=out_shapes,
        cost_estimate=COST,
        compiler_params=params(20 if first is None else 36),
        name="predict",
    )(index, *operands)


def add_and_halve(index, bit, keep, received):
    count, size, spots = keep.shape

    def kernel(index_ref, keep_ref, received_ref, keep_out, send_out):
        a = keep_ref[0] + received_ref[0].astype(F32)
        b = keep_ref[1] + received_ref[1].astype(F32)
        even = ((index_ref[0] >> bit) & 1) == 0
        keep_out[0] = jnp.where(even, a, b)
        send_out[0] = jnp.where(even, b, a).astype(BF16)

    pair = pl.BlockSpec((2, size, spots), lambda i, s: (i, 0, 0))
    one = pl.BlockSpec((1, size, spots), lambda i, s: (i, 0, 0))
    return pl.pallas_call(
        kernel,
        grid_spec=pltpu.PrefetchScalarGridSpec(
            num_scalar_prefetch=1, grid=(count // 2,), in_specs=[pair, pair], out_specs=[one, one]
        ),
        out_shape=[shape((count // 2, size, spots), F32), shape((count // 2, size, spots), BF16)],
        cost_estimate=COST,
        compiler_params=params(10),
        name="add_and_halve",
    )(index, keep, received)


def finish_rows(index, chunk, keep, received, target_rows, running):
    _, size, spots = keep.shape

    def kernel(index_ref, keep_ref, received_ref, target_ref, *refs):
        pred_ref, gene_ref, spot_ref, low_ref = refs[-4:]
        pred = keep_ref[0] + received_ref[0].astype(F32)
        target = target_ref[0].astype(F32)
        pred_ref[...] = pred
        low_ref[0] = pred.astype(BF16)
        for at, product in enumerate((pred * target, pred * pred, target * target)):
            by_gene = jnp.sum(product, axis=1, keepdims=True)
            by_gene = jnp.transpose(jnp.broadcast_to(by_gene, (size, LANES)))
            gene_ref[0, at : at + 1, :] = by_gene[0:1, :]
            by_spot = jnp.sum(product, axis=0, keepdims=True)
            if running is not None:
                by_spot = by_spot + refs[0][at : at + 1, :]
            spot_ref[at : at + 1, :] = by_spot

    one = pl.BlockSpec((1, size, spots), lambda i, s: (0, 0, 0))
    by_spot = pl.BlockSpec((3, spots), lambda i, s: (0, 0))
    return pl.pallas_call(
        kernel,
        grid_spec=pltpu.PrefetchScalarGridSpec(
            num_scalar_prefetch=1,
            grid=(1,),
            in_specs=[one, one, pl.BlockSpec((1, size, spots), lambda i, s: (s[0] * CHUNKS + chunk, 0, 0))]
            + [by_spot] * (running is not None),
            out_specs=[
                pl.BlockSpec((size, spots), lambda i, s: (0, 0)),
                pl.BlockSpec((1, 3, size), lambda i, s: (0, 0, 0)),
                by_spot,
                one,
            ],
        ),
        out_shape=[
            pltpu.HBM((size, spots), F32),
            shape((1, 3, size), F32),
            shape((3, spots), F32),
            shape((1, size, spots), BF16),
        ],
        cost_estimate=COST,
        compiler_params=params(10),
        name="finish_rows",
    )(index, keep, received, in_hbm(target_rows), *([] if running is None else [running]))


def row_of(*values):
    lane = lax.broadcasted_iota(jnp.int32, (1, LANES), 1)
    return sum(jnp.where(lane == at, value, 0.0) for at, value in enumerate(values))


def spot_totals(sums, counts):
    def kernel(sums_ref, counts_ref, out_ref):
        mass = sums_ref[1:2, :] / sums_ref[0:1, :]
        count = counts_ref[...]
        diverged = count * (jnp.log(count) - jnp.log(mass))
        out_ref[...] = row_of(jnp.sum(diverged), jnp.sum(mass), jnp.sum(count))

    return pl.pallas_call(
        kernel, out_shape=shape((1, LANES), F32), cost_estimate=COST, compiler_params=params(4), name="spot_totals"
    )(sums, counts)


def gene_slots(index, gene_sums, spot_sums, parts):
    chunks, _, size = gene_sums.shape
    spots = spot_sums.shape[1]
    genes = parts * chunks * size
    width = max(genes, spots)

    def kernel(index_ref, gene_ref, spot_ref, out_ref):
        out_ref[...] = jnp.zeros((8, width), F32)
        out_ref[3:6, 0:spots] = spot_ref[...]
        lane = lax.broadcasted_iota(jnp.int32, (1, parts * size), 1)
        mine = (lane >= index_ref[0] * size) & (lane < (index_ref[0] + 1) * size)
        for k in range(chunks):
            dot, pp, tt = (gene_ref[k, at : at + 1, :] for at in range(3))
            scale = lax.rsqrt(pp + EPS) * lax.rsqrt(tt + EPS)
            cosine = dot * scale
            for at, value in enumerate(((-1.0 / genes) * scale, (1.0 / genes) * cosine / (pp + EPS), cosine)):
                spread = jnp.concatenate([value] * parts, axis=1)
                out_ref[at : at + 1, k * parts * size : (k + 1) * parts * size] = jnp.where(mine, spread, 0.0)

    smem = pl.BlockSpec(memory_space=pltpu.SMEM)
    vmem = pl.BlockSpec(memory_space=pltpu.VMEM)
    return pl.pallas_call(
        kernel,
        in_specs=[smem, vmem, vmem],
        out_shape=shape((8, width), F32),
        cost_estimate=COST,
        compiler_params=params(4),
        name="gene_slots",
    )(index, gene_sums, spot_sums)


def gradient_terms(slots, totals, genes, spots, chunks, spots_all):
    def kernel(slots_ref, totals_ref, gene_ref, spot_ref, row_ref):
        for k in range(chunks):
            gene_ref[k] = slots_ref[0:2, k * (genes // chunks) : (k + 1) * (genes // chunks)]
        dot, pp, tt = (slots_ref[3 + at : 4 + at, 0:spots] for at in range(3))
        scale = lax.rsqrt(pp + EPS) * lax.rsqrt(tt + EPS)
        cosine = dot * scale
        spot_ref[0:1, :] = (-1.0 / spots_all) * scale
        spot_ref[1:2, :] = (1.0 / spots_all) * cosine / (pp + EPS)
        row_ref[...] = totals_ref[...] + row_of(0.0, 0.0, 0.0, jnp.sum(slots_ref[2:3, 0:genes]), jnp.sum(cosine))

    return pl.pallas_call(
        kernel,
        out_shape=[shape((chunks, 2, genes // chunks), F32), shape((2, spots), F32), shape((1, LANES), F32)],
        cost_estimate=COST,
        compiler_params=params(4),
        name="gradient_terms",
    )(slots, totals)


def loss_row(row, genes, spots_all, n_spot):
    def kernel(row_ref, out_ref):
        kl_sum, mass_total, count_total, gene_sum, spot_sum = (row_ref[0:1, at : at + 1] for at in range(5))
        gene_mean = gene_sum / (genes * n_spot)
        spot_mean = spot_sum / spots_all
        kl = kl_sum / count_total + jnp.log(mass_total) - jnp.log(count_total)
        out_ref[...] = row_of(kl - gene_mean - spot_mean, gene_mean, spot_mean, kl)

    return pl.pallas_call(
        kernel, out_shape=shape((1, LANES), F32), cost_estimate=COST, compiler_params=params(4), name="loss_row"
    )(row)


def join(*pieces):
    count, size, spots = pieces[0].shape

    def kernel(*refs):
        for at, ref in enumerate(refs[:-1]):
            refs[-1][at * count : (at + 1) * count] = ref[...]

    vmem = pl.BlockSpec(memory_space=pltpu.VMEM)
    return pl.pallas_call(
        kernel,
        in_specs=[vmem] * len(pieces),
        out_specs=vmem,
        out_shape=shape((len(pieces) * count, size, spots), BF16),
        cost_estimate=COST,
        compiler_params=params(4),
        name="join",
    )(*pieces)


def gradients(index, chunk, n_spot, pred_near, pred_far, target, gene_rows, spot_rows, weights):
    parts, chunks, size, spots = target.shape
    rows = weights.shape[0]
    tile = TILE_G
    width = parts * size
    per_spot = parts // n_spot
    spot_bits = bits_of(n_spot)
    order = bit_order(chunk, bits_of(parts))

    def kernel(index_ref, near_ref, far_ref, target_ref, gene_ref, spot_ref, weight_ref, *refs):
        grad_ref, back_ref, keep_ref, send_ref, turned, columns = refs

        @pl.when(pl.program_id(0) == 0)
        def _():
            columns[0] = column_of(gene_ref[0, 0:1, :], width)
            columns[1] = column_of(gene_ref[0, 1:2, :], width)
            back = jnp.zeros((1, spots), F32)
            for j in range(parts):
                d = index_ref[0] ^ j
                apart = reversed_bits((d // per_spot) ^ index_ref[1], spot_bits)
                place = apart * per_spot + d % per_spot
                at = pl.multiple_of(d * size, size)
                among = place_among(j, order[:0:-1])
                pred = (far_ref if (j >> order[0]) & 1 else near_ref)[among].astype(F32)
                by_target = tile_lanes(columns[0, pl.ds(at, size), :], spots) + spot_ref[0:1, :]
                by_pred = tile_lanes(columns[1, pl.ds(at, size), :], spots) + spot_ref[1:2, :]
                grad = (target_ref[d, 0].astype(F32) * by_target + pred * by_pred).astype(BF16)
                grad_ref[d] = grad
                turned[pl.ds(pl.multiple_of(place * size, size), size), :] = grad
                back = back + jnp.sum(grad.astype(F32) * pred, axis=0, keepdims=True)
            back_ref[...] = back

        out = lax.dot_general(weight_ref[...], turned[...], (((1,), (1,)), ((), ())), preferred_element_type=F32)
        keep_ref[...] = out[:, : width // 2]
        send_ref[...] = out[:, width // 2 :].astype(BF16)

    half = pl.BlockSpec((parts // 2, size, spots), lambda i, s: (0, 0, 0))
    piece = pl.BlockSpec((tile, width // 2), lambda i, s: (i, 0))
    return pl.pallas_call(
        kernel,
        grid_spec=pltpu.PrefetchScalarGridSpec(
            num_scalar_prefetch=1,
            grid=(rows // tile,),
            in_specs=[
                half,
                half,
                pl.BlockSpec((parts, 1, size, spots), lambda i, s: (0, chunk, 0, 0)),
                pl.BlockSpec((1, 2, width), lambda i, s: (chunk, 0, 0)),
                pl.BlockSpec((2, spots), lambda i, s: (0, 0)),
                pl.BlockSpec((tile, spots), lambda i, s: (i, 0)),
            ],
            out_specs=[
                pl.BlockSpec((parts, size, spots), lambda i, s: (0, 0, 0)),
                pl.BlockSpec((1, spots), lambda i, s: (0, 0)),
                piece,
                piece,
            ],
            scratch_shapes=[pltpu.VMEM((width, spots), BF16), pltpu.VMEM((2, width, LANES), F32)],
        ),
        out_shape=[
            shape((parts, size, spots), BF16),
            shape((1, spots), F32),
            shape((rows, width // 2), F32),
            shape((rows, width // 2), BF16),
        ],
        cost_estimate=COST,
        compiler_params=params(30),
        name="gradients",
    )(index, pred_near, pred_far, in_hbm(target), gene_rows, spot_rows, weights)


def add_columns(keep, received):
    rows, width = keep.shape
    tile = rows // 2

    def kernel(keep_ref, received_ref, keep_out, send_out):
        total = keep_ref[...] + received_ref[...].astype(F32)
        keep_out[...] = total[:, : width // 2]
        send_out[...] = total[:, width // 2 :].astype(BF16)

    whole = pl.BlockSpec((tile, width), lambda i: (i, 0))
    half = pl.BlockSpec((tile, width // 2), lambda i: (i, 0))
    return pl.pallas_call(
        kernel,
        grid=(rows // tile,),
        in_specs=[whole, whole],
        out_specs=[half, half],
        out_shape=[shape((rows, width // 2), F32), shape((rows, width // 2), BF16)],
        cost_estimate=COST,
        compiler_params=params(20),
        name="add_columns",
    )(keep, received)


def assemble(kept, received, size):
    rows, width = kept[0].shape
    chunks = len(kept)
    tile = TILE_Y

    def kernel(*refs):
        out_ref = refs[-1]
        sums = [refs[k][...] + refs[chunks + k][...].astype(F32) for k in range(chunks)]
        pieces = [sums[k][:, d * size : (d + 1) * size] for d in range(width // size) for k in range(chunks)]
        out_ref[...] = jnp.concatenate(pieces, axis=1)

    spec = pl.BlockSpec((tile, width), lambda i: (i, 0))
    return pl.pallas_call(
        kernel,
        grid=(rows // tile,),
        in_specs=[spec] * (2 * chunks),
        out_specs=pl.BlockSpec((tile, width * chunks), lambda i: (i, 0)),
        out_shape=shape((rows, width * chunks), F32),
        cost_estimate=COST,
        compiler_params=params(24),
        name="assemble",
    )(*kept, *received)


def logit_gradient(sums, expr, grads, logits, size_column, counts, totals, backs):
    rows, genes = expr.shape
    parts, size, spots = grads[0].shape
    chunks = len(grads)
    tile = TILE_X

    def kernel(sums_ref, expr_ref, logit_ref, column_ref, counts_ref, totals_ref, *refs):
        grad_refs, back_refs, (out_ref, grad) = refs[:chunks], refs[chunks : 2 * chunks], refs[2 * chunks :]

        @pl.when(pl.program_id(0) == 0)
        def _():
            for k, ref in enumerate(grad_refs):
                for d in range(parts):
                    at = (d * chunks + k) * size
                    grad[at : at + size, :] = ref[d]

        inverse = 1.0 / sums_ref[0:1, :]
        mass = sums_ref[1:2, :] / sums_ref[0:1, :]
        mass_grad = 1.0 / totals_ref[0:1, 1:2] - counts_ref[...] / (totals_ref[0:1, 2:3] * mass)
        back = sum(ref[...] for ref in back_refs) + mass * mass_grad
        acc = jnp.dot(expr_ref[...], grad[...], preferred_element_type=F32)
        probs = jnp.exp(logit_ref[...]) * inverse
        out_ref[...] = probs * ((acc + mass_grad) * tile_lanes(column_ref[...], spots) - back)

    across = pl.BlockSpec((tile, spots), lambda i: (i, 0))
    row = pl.BlockSpec((1, spots), lambda i: (0, 0))
    vmem = pl.BlockSpec(memory_space=pltpu.VMEM)
    return pl.pallas_call(
        kernel,
        grid=(rows // tile,),
        in_specs=[
            pl.BlockSpec((2, spots), lambda i: (0, 0)),
            pl.BlockSpec((tile, genes), lambda i: (i, 0)),
            across,
            pl.BlockSpec((tile, LANES), lambda i: (i, 0)),
            row,
            pl.BlockSpec((1, LANES), lambda i: (0, 0)),
        ]
        + [vmem] * chunks
        + [row] * chunks,
        out_specs=across,
        out_shape=pltpu.HBM((rows, spots), F32),
        scratch_shapes=[pltpu.VMEM((genes, spots), BF16)],
        cost_estimate=COST,
        compiler_params=params(34),
        name="logit_gradient",
    )(sums, in_hbm(expr), in_hbm(logits), size_column, counts, totals, *grads, *backs)


def on_device(logits, centroid_expr, target, sizes, counts):
    parts = lax.axis_size("cent")
    halves = bits_of(parts)
    n_spot = lax.axis_size("spot")
    spot_bits = bits_of(n_spot)
    rows, genes = centroid_expr.shape
    spots = logits.shape[1]
    spots_all = spots * n_spot
    per_device = genes // parts
    size = per_device // CHUNKS
    counts_f = counts.astype(F32).reshape(1, spots)
    target_rows = target.reshape(parts * CHUNKS, size, spots)
    target_chunks = target.reshape(parts, CHUNKS, size, spots)
    order = Order()
    index = jnp.stack([lax.axis_index("cent"), lax.axis_index("spot")])

    made = {}
    names = ("keeps", "arrived", "preds", "gene_sums", "nears", "fars", "grads", "backs", "kept", "landed")
    keeps, arrived, preds, gene_sums, nears, fars, grads, backs, kept, landed = ([None] * CHUNKS for _ in names)

    def stats_step():
        sums, made["column"] = order.run(lambda i, *a: column_stats(i, *a, rows // 4), index, logits, sizes)
        made["total"] = sum_over(sums, "cent")

    def predict_step(k):
        if k == 0:
            out = order.run(
                lambda i, e, *a: predict(i, 0, parts, e, None, a), index, centroid_expr, logits, made["total"], made["column"]
            )
            made["weights"] = out[-1]
        else:
            before = made.pop("turned", None)
            out = order.run(lambda i, e, w: predict(i, k, parts, e, w, None, before), index, centroid_expr, made["weights"])
        if len(out) > (3 if k == 0 else 2):
            made["turned"] = out[2]
        keeps[k] = out[0]
        arrived[k] = swap(out[1], "cent", bit_order(k, halves)[0])

    def halve_step(at):
        def step(k):
            b = bit_order(k, halves)[at]
            keeps[k], send = order.run(lambda i, *a: add_and_halve(i, b, *a), index, keeps[k], arrived[k])
            arrived[k] = swap(send, "cent", b)

        return step

    def finish_step(k):
        preds[k], gene_sums[k], made["spots"], low = order.run(
            lambda i, *a: finish_rows(i, k, *a), index, keeps[k], arrived[k], target_rows, made.get("spots")
        )
        nears[k], fars[k] = low, swap(low, "cent", bit_order(k, halves)[-1])

    def join_step(at):
        def step(k):
            (nears[k],) = order.run(lambda *a: (join(*a),), nears[k], fars[k])
            fars[k] = swap(nears[k], "cent", bit_order(k, halves)[at])

        return step

    def totals_step():
        (made["totals"],) = order.run(lambda *a: (spot_totals(*a),), made["total"], counts_f)

    def genes_step():
        made["sums"] = jnp.concatenate(gene_sums, axis=0)
        made["hop"] = swap(made["sums"], "spot", 0)

    def genes_hop(b):
        def step():
            (made["sums"],) = order.run(lambda *a: (a[0] + a[1],), made["sums"], made["hop"])
            if b + 1 < spot_bits:
                made["hop"] = swap(made["sums"], "spot", b + 1)

        return step

    def slots_step():
        (made["slots"],) = order.run(lambda *a: (gene_slots(*a, parts),), index, made["sums"], made["spots"])
        made["hop"] = [swap(made["slots"], "cent", 0)]

    def slots_hop(last):
        def step():
            (made["slots"],) = order.run(lambda *a: (sum(a),), made["slots"], *made["hop"])
            if not last:
                made["hop"] = [exchange(made["slots"], "cent", 2 * j) for j in range(1, parts // 2)]

        return step

    def terms_step():
        made["genes"], made["terms"], made["row"] = order.run(
            lambda *a: gradient_terms(*a, genes, spots, CHUNKS, spots_all), made["slots"], made["totals"]
        )
        made["row_hop"] = swap(made["row"], "spot", 0)

    def row_hop(b):
        def step():
            (made["row"],) = order.run(lambda *a: (a[0] + a[1],), made["row"], made["row_hop"])
            if b + 1 < spot_bits:
                made["row_hop"] = swap(made["row"], "spot", b + 1)

        return step

    def losses_step():
        (made["losses"],) = order.run(lambda *a: (loss_row(*a, genes, spots_all, n_spot),), made["row"])

    def gradients_step(k):
        operands = (nears[k], fars[k], target_chunks, made["genes"], made["terms"], made["weights"])
        grads[k], backs[k], kept[k], send = order.run(lambda i, *a: gradients(i, k, n_spot, *a), index, *operands)
        landed[k] = swap(send, "spot", 0)

    def columns_step(b):
        def step(k):
            kept[k], send = order.run(add_columns, kept[k], landed[k])
            landed[k] = swap(send, "spot", b)

        return step

    def logits_step():
        (made["logit_grad"],) = order.run(
            lambda t, e, *a: (logit_gradient(t, e, grads, *a, backs),),
            *(made["total"], centroid_expr, logits, made["column"], counts_f, made["row"])
        )

    def centroids_step():
        (made["centroid_grad"],) = order.run(lambda *a: (assemble(a[:CHUNKS], a[CHUNKS:], size),), *kept, *landed)

    def wait_for(values):
        return lambda k: order.wait(values[k])

    steps = {"C": stats_step, "P": predict_step, "F": finish_step, "T": totals_step, "g": genes_step}
    steps |= {"S": slots_step, "s0": slots_hop(False), "s1": slots_hop(True), "R": terms_step, "L": losses_step}
    steps |= {"G": gradients_step, "X": logits_step, "Y": centroids_step}
    steps |= {"wa": wait_for(arrived), "wf": wait_for(fars), "wl": wait_for(landed)}
    steps |= {f"a{b}": halve_step(b) for b in range(1, halves)}
    steps |= {f"j{b}": join_step(b) for b in range(halves - 1)}
    steps |= {f"e{b}": columns_step(b) for b in range(1, spot_bits)}
    steps |= {f"g{b}": genes_hop(b) for b in range(spot_bits)}
    steps |= {f"r{b}": row_hop(b) for b in range(spot_bits)}
    for name in schedule(halves, spot_bits).split():
        step, _, k = name.partition(".")
        steps[step](*([int(k)] if k else []))
    pred_rows = jnp.concatenate(preds, axis=0)
    return made["losses"][0, :4], pred_rows, made["logit_grad"], made["centroid_grad"]


def schedule(halves, spot_bits):
    if (halves, spot_bits) == (3, 2):
        steps = (
            "C P.0 P.1 P.2", "a1.0 P.3 a2.0 a1.1", "a1.2 wa.0 F.0 a1.3", "a2.1 a2.2 j1.0 F.2",
            "wa.1 wa.0 a2.3 F.1", "wf.0 j0.0 wf.2 j1.2", "F.3 wa.0 wa.2 g", "g0 wa.3 g1 S",
            "wf.1 j1.1 s0 j0.2", "j1.3 s1 T R", "r0 wa.0 G.0 wa.0", "j0.3 j0.1 G.2 G.1",
            "r1 G.3 wa.1 e1.0", "e1.3 wa.1 wa.1 X", "e1.2 wf.3 wf.2 wa.2", "L wl.1 e1.1 Y",
        )
        return " ".join(steps)
    forward = ["P", *(f"a{b}" for b in range(1, halves)), "F"]
    forward += [f"j{b}" for b in range(halves - 2, -1, -1)]
    backward = ["G", *(f"e{b}" for b in range(1, spot_bits))]
    waves = [
        [f"{chain[wave - k]}.{k}" for wave in range(len(chain) + CHUNKS) for k in range(CHUNKS) if 0 <= wave - k < len(chain)]
        for chain in (forward, backward)
    ]
    middle = ["T", "g", *(f"g{b}" for b in range(spot_bits)), "S", "s0", "s1", "R"]
    middle += [*(f"r{b}" for b in range(spot_bits)), "L"]
    return " ".join(["C"] + waves[0] + middle + waves[1] + ["X", "Y"])


def solution(mesh):
    in_specs = (P("cent", "spot"), P("cent", None), P(None, "spot"), P("cent"), P("spot"))
    out_specs = (P(), P("cent", "spot"), P("cent", "spot"), P("cent", "spot"))
    return jax.shard_map(
        on_device, mesh=mesh, in_specs=in_specs, out_specs=out_specs, check_vma=False
    )
```

```python
import functools

import jax
import jax.numpy as jnp
from jax import lax
from jax.experimental import pallas as pl
from jax.experimental.pallas import tpu as pltpu
from jax.sharding import PartitionSpec as P

EPS = 1e-06
F32 = jnp.float32
BF16 = jnp.bfloat16
LANES = 128
CHUNKS = 4
TILE_P = 512
TILE_G = 1280
TILE_X = 512
TILE_Y = 512
COST = pl.CostEstimate(flops=1, transcendentals=0, bytes_accessed=1)


def params(mebibytes):
    return pltpu.CompilerParams(vmem_limit_bytes=mebibytes << 20)


def shape(dims, dtype):
    return jax.ShapeDtypeStruct(dims, dtype)


def in_hbm(value):
    return pltpu.with_memory_space_constraint(value, pltpu.HBM)


def bits_of(count):
    return count.bit_length() - 1


def reversed_bits(value, bits):
    return sum(((value >> b) & 1) << (bits - 1 - b) for b in range(bits))


def bit_order(chunk, bits):
    return (1, 0, *range(2, bits)) if chunk == 1 and bits > 2 else tuple(range(bits))


def gathered_with(chunk):
    last = [CHUNKS - 2, CHUNKS - 1]
    return last if chunk in last else [chunk]


def place_among(device, order):
    return sum(((device >> bit) & 1) << at for at, bit in enumerate(order))


def exchange(value, axis, bits):
    return lax.ppermute(value, axis, [(i, i ^ bits) for i in range(lax.axis_size(axis))])


def swap(value, axis, bit):
    return exchange(value, axis, 1 << bit)


def sum_over(value, axis):
    for bit in range(bits_of(lax.axis_size(axis))):
        value = value + swap(value, axis, bit)
    return value


def tile_lanes(column, width):
    return jnp.concatenate([column] * (width // LANES), axis=1)


def column_of(row, length):
    return jnp.transpose(jnp.broadcast_to(row, (LANES, length)))


class Order:
    def __init__(self):
        self.last = ()

    def wait(self, value):
        self.last += tuple(value) if isinstance(value, list) else (value,)

    def run(self, step, first, *others):
        if self.last:
            first = lax.optimization_barrier((first, *self.last))[0]
        results = step(first, *others)
        self.last = (results[-1],)
        return results


def column_stats(index, logits, sizes, tile):
    rows, spots = logits.shape

    def kernel(index_ref, logit_ref, size_ref, sums_ref, column_ref, acc):
        step = pl.program_id(0)
        expo = jnp.exp(logit_ref[...])
        column = column_of(size_ref[...].astype(F32).reshape(1, tile), tile)
        column_ref[...] = column
        mass = expo * tile_lanes(column, spots)
        total = expo.reshape(tile // 8, 8, spots).sum(0)
        mass = mass.reshape(tile // 8, 8, spots).sum(0)

        @pl.when(step == 0)
        def _():
            acc[0] = total
            acc[1] = mass

        @pl.when(step > 0)
        def _():
            acc[0] += total
            acc[1] += mass

        @pl.when(step == pl.num_programs(0) - 1)
        def _():
            sums_ref[0:1, :] = acc[0].sum(0, keepdims=True)
            sums_ref[1:2, :] = acc[1].sum(0, keepdims=True)

    return pl.pallas_call(
        kernel,
        grid_spec=pltpu.PrefetchScalarGridSpec(
            num_scalar_prefetch=1,
            grid=(rows // tile,),
            in_specs=[
                pl.BlockSpec((tile, spots), lambda i, s: (i, 0)),
                pl.BlockSpec((1, 1, tile), lambda i, s: (i, 0, 0)),
            ],
            out_specs=[
                pl.BlockSpec((2, spots), lambda i, s: (0, 0)),
                pl.BlockSpec((tile, LANES), lambda i, s: (i, 0)),
            ],
            scratch_shapes=[pltpu.VMEM((2, 8, spots), F32)],
        ),
        out_shape=[shape((2, spots), F32), shape((rows, LANES), F32)],
        cost_estimate=COST,
        compiler_params=params(20),
        name="column_stats",
    )(index, in_hbm(logits), sizes.reshape(rows // tile, 1, tile))


def predict(index, chunk, parts, expr, weights, first=None, turned_before=None):
    rows = first[0].shape[0] if first is not None else weights.shape[0]
    spots = (weights if first is None else first[0]).shape[1]
    genes = expr.shape[1]
    per_device = genes // parts
    size = per_device // CHUNKS
    width = parts * size
    starts = [d * per_device + chunk * size for d in range(parts)]
    blocks = sorted({s // LANES for s in starts})
    shares = chunk + 1 < CHUNKS and sorted({(s + size) // LANES for s in starts}) == blocks
    shares = shares and turned_before is None
    tile = TILE_P
    order = bit_order(chunk, bits_of(parts))
    order_next = bit_order(chunk + 1, bits_of(parts))
    n_in = (1 if turned_before is not None else len(blocks)) + (1 if first is None else 3)

    def kernel(index_ref, *refs):
        inputs, rest = refs[:n_in], refs[n_in:]
        keep_ref, send_ref = rest[:2]
        turned = inputs[0] if turned_before is not None else rest[-1]
        turned_next = rest[2] if shares else None
        if first is None:
            weight_ref = inputs[-1]
        else:
            logit_ref, sums_ref, column_ref = inputs[-3:]
            weight_ref = rest[3 if shares else 2]

        if turned_before is None:

            @pl.when(pl.program_id(0) == 0)
            def _():
                for number, block in enumerate(blocks):
                    block_t = jnp.transpose(inputs[number][...])
                    for d, start in enumerate(starts):
                        if start // LANES == block:
                            at_row = start % LANES
                            at = place_among(d, order) * size
                            turned[at : at + size, :] = block_t[at_row : at_row + size]
                            if shares:
                                at = place_among(d, order_next) * size
                                turned_next[at : at + size, :] = block_t[at_row + size : at_row + 2 * size]

        if first is not None:
            scale = 1.0 / sums_ref[0:1, :]
            weight = jnp.exp(logit_ref[...]) * scale * tile_lanes(column_ref[...], tile)
            weight_ref[...] = weight.astype(BF16)
        out = jnp.dot(turned[...], weight_ref[...], preferred_element_type=F32)
        even = ((index_ref[0] >> order[0]) & 1) == 0
        for j in range(parts // 2):
            a = out[2 * j * size : (2 * j + 1) * size]
            b = out[(2 * j + 1) * size : (2 * j + 2) * size]
            keep_ref[j] = jnp.where(even, a, b)
            send_ref[j] = jnp.where(even, b, a).astype(BF16)

    half = pl.BlockSpec((parts // 2, size, tile), lambda i, s: (0, 0, i))
    columns = pl.BlockSpec((rows, tile), lambda i, s: (0, i))
    whole = pl.BlockSpec((width, rows), lambda i, s: (0, 0))
    if turned_before is None:
        in_specs = [
            pl.BlockSpec((rows, LANES), lambda i, s, b=b: (0, b), pipeline_mode=pl.Buffered(1)) for b in blocks
        ]
        operands = [in_hbm(expr)] * len(blocks)
    else:
        in_specs, operands = [whole], [turned_before]
    out_specs = [half, half]
    out_shapes = [shape((parts // 2, size, spots), F32), shape((parts // 2, size, spots), BF16)]
    if shares:
        out_specs.append(whole)
        out_shapes.append(shape((width, rows), BF16))
    if first is None:
        in_specs.append(columns)
        operands.append(weights)
    else:
        in_specs += [columns, pl.BlockSpec((2, tile), lambda i, s: (0, i)), pl.BlockSpec((rows, LANES), lambda i, s: (0, 0))]
        operands += [in_hbm(first[0]), *first[1:]]
        out_specs.append(columns)
        out_shapes.append(shape((rows, spots), BF16))
    return pl.pallas_call(
        kernel,
        grid_spec=pltpu.PrefetchScalarGridSpec(
            num_scalar_prefetch=1,
            grid=(spots // tile,),
            in_specs=in_specs,
            out_specs=out_specs,
            scratch_shapes=[pltpu.VMEM((width, rows), BF16)] if turned_before is None else [],
        ),
        out_shape=out_shapes,
        cost_estimate=COST,
        compiler_params=params(20 if first is None else 36),
        name="predict",
    )(index, *operands)


def add_and_halve(index, bit, keep, received):
    count, size, spots = keep.shape

    def kernel(index_ref, keep_ref, received_ref, keep_out, send_out):
        a = keep_ref[0] + received_ref[0].astype(F32)
        b = keep_ref[1] + received_ref[1].astype(F32)
        even = ((index_ref[0] >> bit) & 1) == 0
        keep_out[0] = jnp.where(even, a, b)
        send_out[0] = jnp.where(even, b, a).astype(BF16)

    pair = pl.BlockSpec((2, size, spots), lambda i, s: (i, 0, 0))
    one = pl.BlockSpec((1, size, spots), lambda i, s: (i, 0, 0))
    return pl.pallas_call(
        kernel,
        grid_spec=pltpu.PrefetchScalarGridSpec(
            num_scalar_prefetch=1, grid=(count // 2,), in_specs=[pair, pair], out_specs=[one, one]
        ),
        out_shape=[shape((count // 2, size, spots), F32), shape((count // 2, size, spots), BF16)],
        cost_estimate=COST,
        compiler_params=params(10),
        name="add_and_halve",
    )(index, keep, received)


def finish_rows(index, chunk, per_device, keep, received, target_rows, earlier):
    _, size, spots = keep.shape

    def kernel(index_ref, keep_ref, received_ref, target_ref, *refs):
        pred_ref, gene_ref, spot_ref, low_ref = refs[-4:]
        pred = keep_ref[0] + received_ref[0].astype(F32)
        target = target_ref[0].astype(F32)
        pred_ref[...] = pred
        low_ref[0] = pred.astype(BF16)
        for at, product in enumerate((pred * target, pred * pred, target * target)):
            by_gene = jnp.sum(product, axis=1, keepdims=True)
            by_gene = jnp.transpose(jnp.broadcast_to(by_gene, (size, LANES)))
            gene_ref[0, at : at + 1, :] = by_gene[0:1, :]
            by_spot = jnp.sum(product, axis=0, keepdims=True)
            if earlier is not None:
                by_spot = by_spot + refs[0][at : at + 1, :]
            spot_ref[at : at + 1, :] = by_spot

    one = pl.BlockSpec((1, size, spots), lambda i, s: (0, 0, 0))
    by_spot = pl.BlockSpec((3, spots), lambda i, s: (0, 0))
    whole = pl.BlockSpec(memory_space=pl.ANY)
    operands = [] if earlier is None else [earlier[2], in_hbm(earlier[0]), earlier[1]]
    return pl.pallas_call(
        kernel,
        grid_spec=pltpu.PrefetchScalarGridSpec(
            num_scalar_prefetch=1,
            grid=(1,),
            in_specs=[one, one, pl.BlockSpec((1, size, spots), lambda i, s: (s[0] * CHUNKS + chunk, 0, 0))]
            + [by_spot, whole, whole][: len(operands)],
            out_specs=[
                pl.BlockSpec((size, spots), lambda i, s: (chunk, 0)),
                pl.BlockSpec((1, 3, size), lambda i, s: (chunk, 0, 0)),
                by_spot,
                one,
            ],
        ),
        out_shape=[
            pltpu.HBM((per_device, spots), F32),
            shape((CHUNKS, 3, size), F32),
            shape((3, spots), F32),
            shape((1, size, spots), BF16),
        ],
        input_output_aliases={5: 0, 6: 1} if operands else {},
        cost_estimate=COST,
        compiler_params=params(10),
        name="finish_rows",
    )(index, keep, received, in_hbm(target_rows), *operands)


def row_of(*values):
    lane = lax.broadcasted_iota(jnp.int32, (1, LANES), 1)
    return sum(jnp.where(lane == at, value, 0.0) for at, value in enumerate(values))


def spot_totals(sums, counts):
    def kernel(sums_ref, counts_ref, out_ref):
        mass = sums_ref[1:2, :] / sums_ref[0:1, :]
        count = counts_ref[...]
        diverged = count * (jnp.log(count) - jnp.log(mass))
        out_ref[...] = row_of(jnp.sum(diverged), jnp.sum(mass), jnp.sum(count))

    return pl.pallas_call(
        kernel, out_shape=shape((1, LANES), F32), cost_estimate=COST, compiler_params=params(4), name="spot_totals"
    )(sums, counts)


def gene_slots(index, gene_sums, spot_sums, parts):
    chunks, _, size = gene_sums.shape
    spots = spot_sums.shape[1]
    genes = parts * chunks * size
    width = max(genes, spots)

    def kernel(index_ref, gene_ref, spot_ref, out_ref):
        out_ref[...] = jnp.zeros((8, width), F32)
        out_ref[3:6, 0:spots] = spot_ref[...]
        lane = lax.broadcasted_iota(jnp.int32, (1, parts * size), 1)
        mine = (lane >= index_ref[0] * size) & (lane < (index_ref[0] + 1) * size)
        for k in range(chunks):
            dot, pp, tt = (gene_ref[k, at : at + 1, :] for at in range(3))
            scale = lax.rsqrt(pp + EPS) * lax.rsqrt(tt + EPS)
            cosine = dot * scale
            for at, value in enumerate(((-1.0 / genes) * scale, (1.0 / genes) * cosine / (pp + EPS), cosine)):
                spread = jnp.concatenate([value] * parts, axis=1)
                out_ref[at : at + 1, k * parts * size : (k + 1) * parts * size] = jnp.where(mine, spread, 0.0)

    smem = pl.BlockSpec(memory_space=pltpu.SMEM)
    vmem = pl.BlockSpec(memory_space=pltpu.VMEM)
    return pl.pallas_call(
        kernel,
        in_specs=[smem, vmem, vmem],
        out_shape=shape((8, width), F32),
        cost_estimate=COST,
        compiler_params=params(4),
        name="gene_slots",
    )(index, gene_sums, spot_sums)


def gradient_terms(slots, totals, genes, spots, chunks, spots_all):
    def kernel(slots_ref, totals_ref, gene_ref, spot_ref, row_ref):
        for k in range(chunks):
            gene_ref[k] = slots_ref[0:2, k * (genes // chunks) : (k + 1) * (genes // chunks)]
        dot, pp, tt = (slots_ref[3 + at : 4 + at, 0:spots] for at in range(3))
        scale = lax.rsqrt(pp + EPS) * lax.rsqrt(tt + EPS)
        cosine = dot * scale
        spot_ref[0:1, :] = (-1.0 / spots_all) * scale
        spot_ref[1:2, :] = (1.0 / spots_all) * cosine / (pp + EPS)
        row_ref[...] = totals_ref[...] + row_of(0.0, 0.0, 0.0, jnp.sum(slots_ref[2:3, 0:genes]), jnp.sum(cosine))

    return pl.pallas_call(
        kernel,
        out_shape=[shape((chunks, 2, genes // chunks), F32), shape((2, spots), F32), shape((1, LANES), F32)],
        cost_estimate=COST,
        compiler_params=params(4),
        name="gradient_terms",
    )(slots, totals)


def loss_row(row, genes, spots_all, n_spot):
    def kernel(row_ref, out_ref):
        kl_sum, mass_total, count_total, gene_sum, spot_sum = (row_ref[0:1, at : at + 1] for at in range(5))
        gene_mean = gene_sum / (genes * n_spot)
        spot_mean = spot_sum / spots_all
        kl = kl_sum / count_total + jnp.log(mass_total) - jnp.log(count_total)
        out_ref[...] = row_of(kl - gene_mean - spot_mean, gene_mean, spot_mean, kl)

    return pl.pallas_call(
        kernel, out_shape=shape((1, LANES), F32), cost_estimate=COST, compiler_params=params(4), name="loss_row"
    )(row)


def join(*pieces):
    count, size, spots = pieces[0].shape

    def kernel(*refs):
        for at, ref in enumerate(refs[:-1]):
            refs[-1][at * count : (at + 1) * count] = ref[...]

    vmem = pl.BlockSpec(memory_space=pltpu.VMEM)
    return pl.pallas_call(
        kernel,
        in_specs=[vmem] * len(pieces),
        out_specs=vmem,
        out_shape=shape((len(pieces) * count, size, spots), BF16),
        cost_estimate=COST,
        compiler_params=params(4),
        name="join",
    )(*pieces)


def gradients(index, chunk, n_spot, pred_near, pred_far, target, gene_rows, spot_rows, weights):
    parts, chunks, size, spots = target.shape
    rows = weights.shape[0]
    tile = TILE_G
    width = parts * size
    per_spot = parts // n_spot
    spot_bits = bits_of(n_spot)
    order = bit_order(chunk, bits_of(parts))

    def kernel(index_ref, near_ref, far_ref, target_ref, gene_ref, spot_ref, weight_ref, *refs):
        grad_ref, back_ref, keep_ref, *send_refs, turned, columns = refs

        @pl.when(pl.program_id(0) == 0)
        def _():
            columns[0] = column_of(gene_ref[0, 0:1, :], width)
            columns[1] = column_of(gene_ref[0, 1:2, :], width)
            back = jnp.zeros((1, spots), F32)
            for j in range(parts):
                d = index_ref[0] ^ j
                apart = reversed_bits((d // per_spot) ^ index_ref[1], spot_bits)
                place = apart * per_spot + d % per_spot
                at = pl.multiple_of(d * size, size)
                among = place_among(j, order[:0:-1])
                pred = (far_ref if (j >> order[0]) & 1 else near_ref)[0, among].astype(F32)
                by_target = tile_lanes(columns[0, pl.ds(at, size), :], spots) + spot_ref[0:1, :]
                by_pred = tile_lanes(columns[1, pl.ds(at, size), :], spots) + spot_ref[1:2, :]
                grad = (target_ref[d, 0].astype(F32) * by_target + pred * by_pred).astype(BF16)
                grad_ref[d] = grad
                turned[pl.ds(pl.multiple_of(place * size, size), size), :] = grad
                back = back + jnp.sum(grad.astype(F32) * pred, axis=0, keepdims=True)
            back_ref[...] = back

        out = lax.dot_general(weight_ref[...], turned[...], (((1,), (1,)), ((), ())), preferred_element_type=F32)
        keep_ref[...] = out[:, : width // 2]
        for column, send_ref in enumerate(send_refs):
            left = width // 2 + column * (width // 4)
            send_ref[...] = out[:, left : left + width // 4].astype(BF16)

    member = gathered_with(chunk).index(chunk)
    half = pl.BlockSpec((1, parts // 2, size, spots), lambda i, s: (member, 0, 0, 0))
    piece = pl.BlockSpec((tile, width // 2), lambda i, s: (i, 0))
    return pl.pallas_call(
        kernel,
        grid_spec=pltpu.PrefetchScalarGridSpec(
            num_scalar_prefetch=1,
            grid=(rows // tile,),
            in_specs=[
                half,
                half,
                pl.BlockSpec((parts, 1, size, spots), lambda i, s: (0, chunk, 0, 0)),
                pl.BlockSpec((1, 2, width), lambda i, s: (chunk, 0, 0)),
                pl.BlockSpec((2, spots), lambda i, s: (0, 0)),
                pl.BlockSpec((tile, spots), lambda i, s: (i, 0)),
            ],
            out_specs=[
                pl.BlockSpec((parts, size, spots), lambda i, s: (0, 0, 0)),
                pl.BlockSpec((1, spots), lambda i, s: (0, 0)),
                piece,
            ]
            + [pl.BlockSpec((tile, width // 4), lambda i, s: (i, 0))] * 2,
            scratch_shapes=[pltpu.VMEM((width, spots), BF16), pltpu.VMEM((2, width, LANES), F32)],
        ),
        out_shape=[
            shape((parts, size, spots), BF16),
            shape((1, spots), F32),
            shape((rows, width // 2), F32),
        ]
        + [shape((rows, width // 4), BF16)] * 2,
        cost_estimate=COST,
        compiler_params=params(30),
        name="gradients",
    )(index, pred_near, pred_far, in_hbm(target), gene_rows, spot_rows, weights)


def add_columns(keep, *received):
    rows, width = keep.shape
    tile = rows // 2
    half = width // 2

    def kernel(keep_ref, *refs):
        received_refs, (keep_out, send_out) = refs[:-2], refs[-2:]
        if len(received) == 1:
            keep_out[...] = keep_ref[:, :half] + received_refs[0][:, :half].astype(F32)
            send_out[...] = (keep_ref[:, half:] + received_refs[0][:, half:].astype(F32)).astype(BF16)
        else:
            keep_out[...] = keep_ref[:, :half] + received_refs[0][...].astype(F32)
            send_out[...] = (keep_ref[:, half:] + received_refs[1][...].astype(F32)).astype(BF16)

    whole = pl.BlockSpec((tile, width), lambda i: (i, 0))
    out = pl.BlockSpec((tile, half), lambda i: (i, 0))
    return pl.pallas_call(
        kernel,
        grid=(rows // tile,),
        in_specs=[whole] + ([whole] if len(received) == 1 else [out] * 2),
        out_specs=[out, out],
        out_shape=[shape((rows, half), F32), shape((rows, half), BF16)],
        cost_estimate=COST,
        compiler_params=params(20),
        name="add_columns",
    )(keep, *received)


def assemble(kept, received, size):
    rows, width = kept[0].shape
    chunks = len(kept)
    tile = TILE_Y

    def kernel(*refs):
        out_ref = refs[-1]
        sums = [refs[k][...] + refs[chunks + k][...].astype(F32) for k in range(chunks)]
        pieces = [sums[k][:, d * size : (d + 1) * size] for d in range(width // size) for k in range(chunks)]
        out_ref[...] = jnp.concatenate(pieces, axis=1)

    spec = pl.BlockSpec((tile, width), lambda i: (i, 0))
    return pl.pallas_call(
        kernel,
        grid=(rows // tile,),
        in_specs=[spec] * (2 * chunks),
        out_specs=pl.BlockSpec((tile, width * chunks), lambda i: (i, 0)),
        out_shape=shape((rows, width * chunks), F32),
        cost_estimate=COST,
        compiler_params=params(24),
        name="assemble",
    )(*kept, *received)


def assemble_pair(pair, kept, received, size, before):
    rows, width = kept[0].shape
    tile = rows // 2

    def kernel(*refs):
        out_ref = refs[-1]
        sums = [refs[k][...] + refs[2 + k][...].astype(F32) for k in range(2)]
        for d in range(width // size):

            @pl.when(pl.program_id(1) == d)
            def _():
                out_ref[...] = jnp.concatenate([v[:, d * size : (d + 1) * size] for v in sums], axis=1)

    spec = pl.BlockSpec((tile, width), lambda i, d: (i, 0))
    others = [] if before is None else [before]
    return pl.pallas_call(
        kernel,
        grid=(rows // tile, width // size),
        in_specs=[spec] * 4 + [pl.BlockSpec(memory_space=pl.ANY)] * len(others),
        out_specs=pl.BlockSpec((tile, 2 * size), lambda i, d: (i, d * (CHUNKS // 2) + pair)),
        out_shape=pltpu.HBM((rows, width * CHUNKS), F32),
        input_output_aliases={4: 0} if others else {},
        cost_estimate=COST,
        compiler_params=params(24),
        name="assemble_pair",
    )(*kept, *received, *[in_hbm(v) for v in others])


def logit_gradient(sums, expr, grads, logits, size_column, counts, totals, backs):
    rows, genes = expr.shape
    parts, size, spots = grads[0].shape
    chunks = len(grads)
    tile = TILE_X

    def kernel(sums_ref, expr_ref, logit_ref, column_ref, counts_ref, totals_ref, *refs):
        grad_refs, back_refs, (out_ref, grad) = refs[:chunks], refs[chunks : 2 * chunks], refs[2 * chunks :]

        @pl.when(pl.program_id(0) == 0)
        def _():
            for k, ref in enumerate(grad_refs):
                for d in range(parts):
                    at = (d * chunks + k) * size
                    grad[at : at + size, :] = ref[d]

        inverse = 1.0 / sums_ref[0:1, :]
        mass = sums_ref[1:2, :] / sums_ref[0:1, :]
        mass_grad = 1.0 / totals_ref[0:1, 1:2] - counts_ref[...] / (totals_ref[0:1, 2:3] * mass)
        back = sum(ref[...] for ref in back_refs) + mass * mass_grad
        acc = jnp.dot(expr_ref[...], grad[...], preferred_element_type=F32)
        probs = jnp.exp(logit_ref[...]) * inverse
        out_ref[...] = probs * ((acc + mass_grad) * tile_lanes(column_ref[...], spots) - back)

    across = pl.BlockSpec((tile, spots), lambda i: (i, 0))
    row = pl.BlockSpec((1, spots), lambda i: (0, 0))
    vmem = pl.BlockSpec(memory_space=pltpu.VMEM)
    return pl.pallas_call(
        kernel,
        grid=(rows // tile,),
        in_specs=[
            pl.BlockSpec((2, spots), lambda i: (0, 0)),
            pl.BlockSpec((tile, genes), lambda i: (i, 0)),
            across,
            pl.BlockSpec((tile, LANES), lambda i: (i, 0)),
            row,
            pl.BlockSpec((1, LANES), lambda i: (0, 0)),
        ]
        + [vmem] * chunks
        + [row] * chunks,
        out_specs=across,
        out_shape=pltpu.HBM((rows, spots), F32),
        scratch_shapes=[pltpu.VMEM((genes, spots), BF16)],
        cost_estimate=COST,
        compiler_params=params(34),
        name="logit_gradient",
    )(sums, in_hbm(expr), in_hbm(logits), size_column, counts, totals, *grads, *backs)


def on_device(logits, centroid_expr, target, sizes, counts):
    parts = lax.axis_size("cent")
    halves = bits_of(parts)
    n_spot = lax.axis_size("spot")
    spot_bits = bits_of(n_spot)
    rows, genes = centroid_expr.shape
    spots = logits.shape[1]
    spots_all = spots * n_spot
    per_device = genes // parts
    size = per_device // CHUNKS
    counts_f = counts.astype(F32).reshape(1, spots)
    target_rows = target.reshape(parts * CHUNKS, size, spots)
    target_chunks = target.reshape(parts, CHUNKS, size, spots)
    order = Order()
    index = jnp.stack([lax.axis_index("cent"), lax.axis_index("spot")])

    made = {}
    keeps, arrived, nears, fars, grads, backs, kept, landed = ([None] * CHUNKS for _ in range(8))

    def stats_step():
        sums, made["column"] = order.run(lambda i, *a: column_stats(i, *a, rows // 4), index, logits, sizes)
        made["total"] = sum_over(sums, "cent")

    def predict_step(k):
        if k == 0:
            out = order.run(
                lambda i, e, *a: predict(i, 0, parts, e, None, a), index, centroid_expr, logits, made["total"], made["column"]
            )
            made["weights"] = out[-1]
        else:
            before = made.pop("turned", None)
            out = order.run(lambda i, e, w: predict(i, k, parts, e, w, None, before), index, centroid_expr, made["weights"])
        if len(out) > (3 if k == 0 else 2):
            made["turned"] = out[2]
        keeps[k] = out[0]
        arrived[k] = swap(out[1], "cent", bit_order(k, halves)[0])

    def halve_step(at):
        def step(k):
            b = bit_order(k, halves)[at]
            keeps[k], send = order.run(lambda i, *a: add_and_halve(i, b, *a), index, keeps[k], arrived[k])
            arrived[k] = swap(send, "cent", b)

        return step

    def finish_step(k):
        *made["rows"], low = order.run(
            lambda i, *a: finish_rows(i, k, per_device, *a), index, keeps[k], arrived[k], target_rows, made.get("rows")
        )
        nears[k], fars[k] = low, swap(low, "cent", bit_order(k, halves)[-1])

    def pair_up_step(k):
        pieces = [v[c] for c in gathered_with(k) for v in (nears, fars)]
        (nears[k],) = order.run(lambda *a: (join(*a),), *pieces)
        fars[k] = swap(nears[k], "cent", bit_order(k, halves)[0])

    def join_step(at):
        def step(k):
            (nears[k],) = order.run(lambda *a: (join(*a),), nears[k], fars[k])
            fars[k] = swap(nears[k], "cent", bit_order(k, halves)[at])

        return step

    def totals_step():
        (made["totals"],) = order.run(lambda *a: (spot_totals(*a),), made["total"], counts_f)

    def genes_step():
        made["sums"] = made["rows"][1]
        made["hop"] = swap(made["sums"], "spot", 0)

    def genes_hop(b):
        def step():
            (made["sums"],) = order.run(lambda *a: (a[0] + a[1],), made["sums"], made["hop"])
            if b + 1 < spot_bits:
                made["hop"] = swap(made["sums"], "spot", b + 1)

        return step

    def slots_step():
        (made["slots"],) = order.run(lambda *a: (gene_slots(*a, parts),), index, made["sums"], made["rows"][2])
        made["hop"] = [swap(made["slots"], "cent", 0)]

    def slots_hop(last):
        def step():
            (made["slots"],) = order.run(lambda *a: (sum(a),), made["slots"], *made["hop"])
            if not last:
                made["hop"] = [exchange(made["slots"], "cent", 2 * j) for j in range(1, parts // 2)]

        return step

    def terms_step():
        made["genes"], made["terms"], made["row"] = order.run(
            lambda *a: gradient_terms(*a, genes, spots, CHUNKS, spots_all), made["slots"], made["totals"]
        )
        made["row_hop"] = swap(made["row"], "spot", 0)

    def row_hop(b):
        def step():
            (made["row"],) = order.run(lambda *a: (a[0] + a[1],), made["row"], made["row_hop"])
            if b + 1 < spot_bits:
                made["row_hop"] = swap(made["row"], "spot", b + 1)

        return step

    def losses_step():
        (made["losses"],) = order.run(lambda *a: (loss_row(*a, genes, spots_all, n_spot),), made["row"])

    def gradients_step(k):
        first, *_ = group = gathered_with(k)
        near, far = (v[first].reshape(len(group), parts // 2, size, spots) for v in (nears, fars))
        operands = (near, far, target_chunks, made["genes"], made["terms"], made["weights"])
        grads[k], backs[k], kept[k], *sends = order.run(lambda i, *a: gradients(i, k, n_spot, *a), index, *operands)
        landed[k] = [swap(send, "spot", 0) for send in sends]

    def columns_step(b):
        def step(k):
            kept[k], send = order.run(add_columns, kept[k], *landed[k])
            landed[k] = [swap(send, "spot", b)]

        return step

    def logits_step():
        (made["logit_grad"],) = order.run(
            lambda t, e, *a: (logit_gradient(t, e, grads, *a, backs),),
            *(made["total"], centroid_expr, logits, made["column"], counts_f, made["row"])
        )

    def centroids_step():
        (made["centroid_grad"],) = order.run(lambda *a: (assemble(a[:CHUNKS], a[CHUNKS:], size),), *kept, *sum(landed, []))

    def pair_step(pair):
        chunks = slice(2 * pair, 2 * pair + 2)
        before = made.get("centroid_grad")
        (made["centroid_grad"],) = order.run(
            lambda *a: (assemble_pair(pair, a[:2], a[2:], size, before),), *kept[chunks], *sum(landed[chunks], [])
        )

    def wait_for(values):
        return lambda k: order.wait(values[k])

    steps = {"C": stats_step, "P": predict_step, "F": finish_step, "T": totals_step, "g": genes_step}
    steps |= {"S": slots_step, "s0": slots_hop(False), "s1": slots_hop(True), "R": terms_step, "L": losses_step}
    steps |= {"p": pair_up_step, "G": gradients_step, "X": logits_step, "Y": centroids_step, "y": pair_step}
    steps |= {"wa": wait_for(arrived), "wf": wait_for(fars), "wl": wait_for(landed)}
    steps |= {f"a{b}": halve_step(b) for b in range(1, halves)}
    steps |= {f"j{b}": join_step(b) for b in range(halves - 1)}
    steps |= {f"e{b}": columns_step(b) for b in range(1, spot_bits)}
    steps |= {f"g{b}": genes_hop(b) for b in range(spot_bits)}
    steps |= {f"r{b}": row_hop(b) for b in range(spot_bits)}
    for name in schedule(halves, spot_bits).split():
        step, _, k = name.partition(".")
        steps[step](*([int(k)] if k else []))
    return made["losses"][0, :4], made["rows"][0], made["logit_grad"], made["centroid_grad"]


def schedule(halves, spot_bits):
    if (halves, spot_bits) == (3, 2):
        steps = (
            "C P.0 P.1 P.2", "a1.0 P.3 a1.1 a2.0", "a1.2 wa.0 F.0 a1.3", "a2.1 a2.2 j1.0 F.2",
            "a2.3 F.1 wf.0 j0.0", "F.3 j1.2 g g0", "g1 S j1.1 j1.3", "s0 s1 T R",
            "j0.1 p.2 G.0 r0", "G.1 e1.0 e1.1 G.2", "wl.0 r1 G.3 e1.2", "L wl.1 e1.3 y.0",
            "X y.1",
        )
        return " ".join(steps)
    forward = ["P", *(f"a{b}" for b in range(1, halves)), "F"]
    backward = ["G", *(f"e{b}" for b in range(1, spot_bits))]
    waves = [
        [f"{chain[wave - k]}.{k}" for wave in range(len(chain) + CHUNKS) for k in range(CHUNKS) if 0 <= wave - k < len(chain)]
        for chain in (forward, backward)
    ]
    gather = []
    for group in sorted({tuple(gathered_with(k)) for k in range(CHUNKS)}):
        gather += [f"j{b}.{k}" for k in group for b in range(halves - 2, 0, -1)]
        gather.append(f"j0.{group[0]}" if len(group) == 1 else f"p.{group[0]}")
    middle = gather + ["T", "g", *(f"g{b}" for b in range(spot_bits)), "S", "s0", "s1", "R"]
    middle += [*(f"r{b}" for b in range(spot_bits)), "L"]
    return " ".join(["C"] + waves[0] + middle + waves[1] + ["X", "Y"])


def solution(mesh):
    in_specs = (P("cent", "spot"), P("cent", None), P(None, "spot"), P("cent"), P("spot"))
    out_specs = (P(), P("cent", "spot"), P("cent", "spot"), P("cent", "spot"))
    return jax.shard_map(
        on_device, mesh=mesh, in_specs=in_specs, out_specs=out_specs, check_vma=False
    )
```

```python
import functools

import jax
import jax.numpy as jnp
from jax import lax
from jax.experimental import pallas as pl
from jax.experimental.pallas import tpu as pltpu
from jax.sharding import PartitionSpec as P

EPS = 1e-06
F32 = jnp.float32
BF16 = jnp.bfloat16
LANES = 128
CHUNKS = 4
TILE_P = 512
TILE_G = 1280
TILE_X = 512
TILE_Y = 512
COST = pl.CostEstimate(flops=1, transcendentals=0, bytes_accessed=1)


def params(mebibytes):
    return pltpu.CompilerParams(vmem_limit_bytes=mebibytes << 20)


def shape(dims, dtype):
    return jax.ShapeDtypeStruct(dims, dtype)


def in_hbm(value):
    return pltpu.with_memory_space_constraint(value, pltpu.HBM)


def bits_of(count):
    return count.bit_length() - 1


def reversed_bits(value, bits):
    return sum(((value >> b) & 1) << (bits - 1 - b) for b in range(bits))


def bit_order(chunk, bits):
    return (1, 0, *range(2, bits)) if chunk == 1 and bits > 2 else tuple(range(bits))


def gathered_with(chunk):
    last = [CHUNKS - 2, CHUNKS - 1]
    return last if chunk in last else [chunk]


def place_among(device, order):
    return sum(((device >> bit) & 1) << at for at, bit in enumerate(order))


def exchange(value, axis, bits):
    return lax.ppermute(value, axis, [(i, i ^ bits) for i in range(lax.axis_size(axis))])


def swap(value, axis, bit):
    return exchange(value, axis, 1 << bit)


def sum_over(value, axis):
    for bit in range(bits_of(lax.axis_size(axis))):
        value = value + swap(value, axis, bit)
    return value


def tile_lanes(column, width):
    return jnp.concatenate([column] * (width // LANES), axis=1)


def column_of(row, length):
    return jnp.transpose(jnp.broadcast_to(row, (LANES, length)))


class Order:
    def __init__(self):
        self.last = ()

    def wait(self, value):
        self.last += tuple(value) if isinstance(value, list) else (value,)

    def run(self, step, first, *others):
        if self.last:
            first = lax.optimization_barrier((first, *self.last))[0]
        results = step(first, *others)
        self.last = (results[-1],)
        return results


def column_stats(index, logits, sizes, tile):
    rows, spots = logits.shape

    def kernel(index_ref, logit_ref, size_ref, sums_ref, column_ref, acc):
        step = pl.program_id(0)
        expo = jnp.exp(logit_ref[...])
        part = size_ref[pl.ds(pl.multiple_of(step * tile, LANES), tile)]
        column = column_of(part.astype(F32).reshape(1, tile), tile)
        column_ref[...] = column
        mass = expo * tile_lanes(column, spots)
        total = expo.reshape(tile // 8, 8, spots).sum(0)
        mass = mass.reshape(tile // 8, 8, spots).sum(0)

        @pl.when(step == 0)
        def _():
            acc[0] = total
            acc[1] = mass

        @pl.when(step > 0)
        def _():
            acc[0] += total
            acc[1] += mass

        @pl.when(step == pl.num_programs(0) - 1)
        def _():
            sums_ref[0:1, :] = acc[0].sum(0, keepdims=True)
            sums_ref[1:2, :] = acc[1].sum(0, keepdims=True)

    return pl.pallas_call(
        kernel,
        grid_spec=pltpu.PrefetchScalarGridSpec(
            num_scalar_prefetch=1,
            grid=(rows // tile,),
            in_specs=[
                pl.BlockSpec((tile, spots), lambda i, s: (i, 0)),
                pl.BlockSpec((rows,), lambda i, s: (0,)),
            ],
            out_specs=[
                pl.BlockSpec((2, spots), lambda i, s: (0, 0)),
                pl.BlockSpec((tile, LANES), lambda i, s: (i, 0)),
            ],
            scratch_shapes=[pltpu.VMEM((2, 8, spots), F32)],
        ),
        out_shape=[shape((2, spots), F32), shape((rows, LANES), F32)],
        cost_estimate=COST,
        compiler_params=params(20),
        name="column_stats",
    )(index, in_hbm(logits), in_hbm(sizes))


def predict(index, chunk, parts, expr, weights, first=None, turned_before=None):
    rows = first[0].shape[0] if first is not None else weights.shape[0]
    spots = (weights if first is None else first[0]).shape[1]
    genes = expr.shape[1]
    per_device = genes // parts
    size = per_device // CHUNKS
    width = parts * size
    starts = [d * per_device + chunk * size for d in range(parts)]
    blocks = sorted({s // LANES for s in starts})
    shares = chunk + 1 < CHUNKS and sorted({(s + size) // LANES for s in starts}) == blocks
    shares = shares and turned_before is None
    tile = TILE_P
    order = bit_order(chunk, bits_of(parts))
    order_next = bit_order(chunk + 1, bits_of(parts))
    n_in = (1 if turned_before is not None else len(blocks)) + (1 if first is None else 3)

    def kernel(index_ref, *refs):
        inputs, rest = refs[:n_in], refs[n_in:]
        keep_ref, send_ref = rest[:2]
        turned = inputs[0] if turned_before is not None else rest[-1]
        turned_next = rest[2] if shares else None
        if first is None:
            weight_ref = inputs[-1]
        else:
            logit_ref, sums_ref, column_ref = inputs[-3:]
            weight_ref = rest[3 if shares else 2]

        if turned_before is None:

            @pl.when(pl.program_id(0) == 0)
            def _():
                for number, block in enumerate(blocks):
                    block_t = jnp.transpose(inputs[number][...])
                    for d, start in enumerate(starts):
                        if start // LANES == block:
                            at_row = start % LANES
                            at = place_among(d, order) * size
                            turned[at : at + size, :] = block_t[at_row : at_row + size]
                            if shares:
                                at = place_among(d, order_next) * size
                                turned_next[at : at + size, :] = block_t[at_row + size : at_row + 2 * size]

        if first is not None:
            scale = 1.0 / sums_ref[0:1, :]
            weight = jnp.exp(logit_ref[...]) * scale * tile_lanes(column_ref[...], tile)
            weight_ref[...] = weight.astype(BF16)
        out = jnp.dot(turned[...], weight_ref[...], preferred_element_type=F32)
        even = ((index_ref[0] >> order[0]) & 1) == 0
        for j in range(parts // 2):
            a = out[2 * j * size : (2 * j + 1) * size]
            b = out[(2 * j + 1) * size : (2 * j + 2) * size]
            keep_ref[j] = jnp.where(even, a, b)
            send_ref[j] = jnp.where(even, b, a).astype(BF16)

    half = pl.BlockSpec((parts // 2, size, tile), lambda i, s: (0, 0, i))
    columns = pl.BlockSpec((rows, tile), lambda i, s: (0, i))
    whole = pl.BlockSpec((width, rows), lambda i, s: (0, 0))
    if turned_before is None:
        in_specs = [
            pl.BlockSpec((rows, LANES), lambda i, s, b=b: (0, b), pipeline_mode=pl.Buffered(1)) for b in blocks
        ]
        operands = [in_hbm(expr)] * len(blocks)
    else:
        in_specs, operands = [whole], [turned_before]
    out_specs = [half, half]
    out_shapes = [shape((parts // 2, size, spots), F32), shape((parts // 2, size, spots), BF16)]
    if shares:
        out_specs.append(whole)
        out_shapes.append(shape((width, rows), BF16))
    if first is None:
        in_specs.append(columns)
        operands.append(weights)
    else:
        in_specs += [columns, pl.BlockSpec((2, tile), lambda i, s: (0, i)), pl.BlockSpec((rows, LANES), lambda i, s: (0, 0))]
        operands += [in_hbm(first[0]), *first[1:]]
        out_specs.append(columns)
        out_shapes.append(shape((rows, spots), BF16))
    return pl.pallas_call(
        kernel,
        grid_spec=pltpu.PrefetchScalarGridSpec(
            num_scalar_prefetch=1,
            grid=(spots // tile,),
            in_specs=in_specs,
            out_specs=out_specs,
            scratch_shapes=[pltpu.VMEM((width, rows), BF16)] if turned_before is None else [],
        ),
        out_shape=out_shapes,
        cost_estimate=COST,
        compiler_params=params(20 if first is None else 36),
        name="predict",
    )(index, *operands)


def add_and_halve(index, bit, keep, received):
    count, size, spots = keep.shape

    def kernel(index_ref, keep_ref, received_ref, keep_out, send_out):
        a = keep_ref[0] + received_ref[0].astype(F32)
        b = keep_ref[1] + received_ref[1].astype(F32)
        even = ((index_ref[0] >> bit) & 1) == 0
        keep_out[0] = jnp.where(even, a, b)
        send_out[0] = jnp.where(even, b, a).astype(BF16)

    pair = pl.BlockSpec((2, size, spots), lambda i, s: (i, 0, 0))
    one = pl.BlockSpec((1, size, spots), lambda i, s: (i, 0, 0))
    return pl.pallas_call(
        kernel,
        grid_spec=pltpu.PrefetchScalarGridSpec(
            num_scalar_prefetch=1, grid=(count // 2,), in_specs=[pair, pair], out_specs=[one, one]
        ),
        out_shape=[shape((count // 2, size, spots), F32), shape((count // 2, size, spots), BF16)],
        cost_estimate=COST,
        compiler_params=params(10),
        name="add_and_halve",
    )(index, keep, received)


def finish_rows(index, chunk, per_device, keep, received, target_rows, earlier):
    _, size, spots = keep.shape

    def kernel(index_ref, keep_ref, received_ref, target_ref, *refs):
        pred_ref, gene_ref, spot_ref, low_ref = refs[-4:]
        pred = keep_ref[0] + received_ref[0].astype(F32)
        target = target_ref[0].astype(F32)
        pred_ref[...] = pred
        low_ref[0] = pred.astype(BF16)
        for at, product in enumerate((pred * target, pred * pred, target * target)):
            by_gene = jnp.sum(product, axis=1, keepdims=True)
            by_gene = jnp.transpose(jnp.broadcast_to(by_gene, (size, LANES)))
            gene_ref[0, at : at + 1, :] = by_gene[0:1, :]
            by_spot = jnp.sum(product, axis=0, keepdims=True)
            if earlier is not None:
                by_spot = by_spot + refs[0][at : at + 1, :]
            spot_ref[at : at + 1, :] = by_spot

    one = pl.BlockSpec((1, size, spots), lambda i, s: (0, 0, 0))
    by_spot = pl.BlockSpec((3, spots), lambda i, s: (0, 0))
    whole = pl.BlockSpec(memory_space=pl.ANY)
    operands = [] if earlier is None else [earlier[2], in_hbm(earlier[0]), earlier[1]]
    return pl.pallas_call(
        kernel,
        grid_spec=pltpu.PrefetchScalarGridSpec(
            num_scalar_prefetch=1,
            grid=(1,),
            in_specs=[one, one, pl.BlockSpec((1, size, spots), lambda i, s: (s[0] * CHUNKS + chunk, 0, 0))]
            + [by_spot, whole, whole][: len(operands)],
            out_specs=[
                pl.BlockSpec((size, spots), lambda i, s: (chunk, 0)),
                pl.BlockSpec((1, 3, size), lambda i, s: (chunk, 0, 0)),
                by_spot,
                one,
            ],
        ),
        out_shape=[
            pltpu.HBM((per_device, spots), F32),
            shape((CHUNKS, 3, size), F32),
            shape((3, spots), F32),
            shape((1, size, spots), BF16),
        ],
        input_output_aliases={5: 0, 6: 1} if operands else {},
        cost_estimate=COST,
        compiler_params=params(10),
        name="finish_rows",
    )(index, keep, received, in_hbm(target_rows), *operands)


def row_of(*values):
    lane = lax.broadcasted_iota(jnp.int32, (1, LANES), 1)
    return sum(jnp.where(lane == at, value, 0.0) for at, value in enumerate(values))


def spot_totals(sums, counts):
    def kernel(sums_ref, counts_ref, out_ref):
        mass = sums_ref[1:2, :] / sums_ref[0:1, :]
        count = counts_ref[...]
        diverged = count * (jnp.log(count) - jnp.log(mass))
        out_ref[...] = row_of(jnp.sum(diverged), jnp.sum(mass), jnp.sum(count))

    return pl.pallas_call(
        kernel, out_shape=shape((1, LANES), F32), cost_estimate=COST, compiler_params=params(4), name="spot_totals"
    )(sums, counts)


def gene_slots(index, gene_sums, spot_sums, parts):
    chunks, _, size = gene_sums.shape
    spots = spot_sums.shape[1]
    genes = parts * chunks * size
    width = max(genes, spots)

    def kernel(index_ref, gene_ref, spot_ref, out_ref):
        out_ref[...] = jnp.zeros((8, width), F32)
        out_ref[3:6, 0:spots] = spot_ref[...]
        lane = lax.broadcasted_iota(jnp.int32, (1, parts * size), 1)
        mine = (lane >= index_ref[0] * size) & (lane < (index_ref[0] + 1) * size)
        for k in range(chunks):
            dot, pp, tt = (gene_ref[k, at : at + 1, :] for at in range(3))
            scale = lax.rsqrt(pp + EPS) * lax.rsqrt(tt + EPS)
            cosine = dot * scale
            for at, value in enumerate(((-1.0 / genes) * scale, (1.0 / genes) * cosine / (pp + EPS), cosine)):
                spread = jnp.concatenate([value] * parts, axis=1)
                out_ref[at : at + 1, k * parts * size : (k + 1) * parts * size] = jnp.where(mine, spread, 0.0)

    smem = pl.BlockSpec(memory_space=pltpu.SMEM)
    vmem = pl.BlockSpec(memory_space=pltpu.VMEM)
    return pl.pallas_call(
        kernel,
        in_specs=[smem, vmem, vmem],
        out_shape=shape((8, width), F32),
        cost_estimate=COST,
        compiler_params=params(4),
        name="gene_slots",
    )(index, gene_sums, spot_sums)


def gradient_terms(slots, totals, genes, spots, chunks, spots_all):
    def kernel(slots_ref, totals_ref, gene_ref, spot_ref, row_ref):
        for k in range(chunks):
            gene_ref[k] = slots_ref[0:2, k * (genes // chunks) : (k + 1) * (genes // chunks)]
        dot, pp, tt = (slots_ref[3 + at : 4 + at, 0:spots] for at in range(3))
        scale = lax.rsqrt(pp + EPS) * lax.rsqrt(tt + EPS)
        cosine = dot * scale
        spot_ref[0:1, :] = (-1.0 / spots_all) * scale
        spot_ref[1:2, :] = (1.0 / spots_all) * cosine / (pp + EPS)
        row_ref[...] = totals_ref[...] + row_of(0.0, 0.0, 0.0, jnp.sum(slots_ref[2:3, 0:genes]), jnp.sum(cosine))

    return pl.pallas_call(
        kernel,
        out_shape=[shape((chunks, 2, genes // chunks), F32), shape((2, spots), F32), shape((1, LANES), F32)],
        cost_estimate=COST,
        compiler_params=params(4),
        name="gradient_terms",
    )(slots, totals)


def loss_row(row, genes, spots_all, n_spot):
    def kernel(row_ref, out_ref):
        kl_sum, mass_total, count_total, gene_sum, spot_sum = (row_ref[0:1, at : at + 1] for at in range(5))
        gene_mean = gene_sum / (genes * n_spot)
        spot_mean = spot_sum / spots_all
        kl = kl_sum / count_total + jnp.log(mass_total) - jnp.log(count_total)
        out_ref[...] = row_of(kl - gene_mean - spot_mean, gene_mean, spot_mean, kl)

    return pl.pallas_call(
        kernel, out_shape=shape((1, LANES), F32), cost_estimate=COST, compiler_params=params(4), name="loss_row"
    )(row)


def join(*pieces):
    count, size, spots = pieces[0].shape

    def kernel(*refs):
        for at, ref in enumerate(refs[:-1]):
            refs[-1][at * count : (at + 1) * count] = ref[...]

    vmem = pl.BlockSpec(memory_space=pltpu.VMEM)
    return pl.pallas_call(
        kernel,
        in_specs=[vmem] * len(pieces),
        out_specs=vmem,
        out_shape=shape((len(pieces) * count, size, spots), BF16),
        cost_estimate=COST,
        compiler_params=params(4),
        name="join",
    )(*pieces)


def gradients(index, chunk, n_spot, pred_near, pred_far, target, gene_rows, spot_rows, weights):
    parts, chunks, size, spots = target.shape
    rows = weights.shape[0]
    tile = TILE_G
    width = parts * size
    per_spot = parts // n_spot
    spot_bits = bits_of(n_spot)
    order = bit_order(chunk, bits_of(parts))

    def kernel(index_ref, near_ref, far_ref, target_ref, gene_ref, spot_ref, weight_ref, *refs):
        grad_ref, back_ref, keep_ref, *send_refs, turned, columns = refs

        @pl.when(pl.program_id(0) == 0)
        def _():
            columns[0] = column_of(gene_ref[0, 0:1, :], width)
            columns[1] = column_of(gene_ref[0, 1:2, :], width)
            back = jnp.zeros((1, spots), F32)
            for j in range(parts):
                d = index_ref[0] ^ j
                apart = reversed_bits((d // per_spot) ^ index_ref[1], spot_bits)
                place = apart * per_spot + d % per_spot
                at = pl.multiple_of(d * size, size)
                among = place_among(j, order[:0:-1])
                pred = (far_ref if (j >> order[0]) & 1 else near_ref)[0, among].astype(F32)
                by_target = tile_lanes(columns[0, pl.ds(at, size), :], spots) + spot_ref[0:1, :]
                by_pred = tile_lanes(columns[1, pl.ds(at, size), :], spots) + spot_ref[1:2, :]
                grad = (target_ref[d, 0].astype(F32) * by_target + pred * by_pred).astype(BF16)
                grad_ref[d] = grad
                turned[pl.ds(pl.multiple_of(place * size, size), size), :] = grad
                back = back + jnp.sum(grad.astype(F32) * pred, axis=0, keepdims=True)
            back_ref[...] = back

        out = lax.dot_general(weight_ref[...], turned[...], (((1,), (1,)), ((), ())), preferred_element_type=F32)
        keep_ref[...] = out[:, : width // 2]
        for column, send_ref in enumerate(send_refs):
            left = width // 2 + column * (width // 4)
            send_ref[...] = out[:, left : left + width // 4].astype(BF16)

    member = gathered_with(chunk).index(chunk)
    half = pl.BlockSpec((1, parts // 2, size, spots), lambda i, s: (member, 0, 0, 0))
    piece = pl.BlockSpec((tile, width // 2), lambda i, s: (i, 0))
    return pl.pallas_call(
        kernel,
        grid_spec=pltpu.PrefetchScalarGridSpec(
            num_scalar_prefetch=1,
            grid=(rows // tile,),
            in_specs=[
                half,
                half,
                pl.BlockSpec((parts, 1, size, spots), lambda i, s: (0, chunk, 0, 0)),
                pl.BlockSpec((1, 2, width), lambda i, s: (chunk, 0, 0)),
                pl.BlockSpec((2, spots), lambda i, s: (0, 0)),
                pl.BlockSpec((tile, spots), lambda i, s: (i, 0)),
            ],
            out_specs=[
                pl.BlockSpec((parts, size, spots), lambda i, s: (0, 0, 0)),
                pl.BlockSpec((1, spots), lambda i, s: (0, 0)),
                piece,
            ]
            + [pl.BlockSpec((tile, width // 4), lambda i, s: (i, 0))] * 2,
            scratch_shapes=[pltpu.VMEM((width, spots), BF16), pltpu.VMEM((2, width, LANES), F32)],
        ),
        out_shape=[
            shape((parts, size, spots), BF16),
            shape((1, spots), F32),
            shape((rows, width // 2), F32),
        ]
        + [shape((rows, width // 4), BF16)] * 2,
        cost_estimate=COST,
        compiler_params=params(30),
        name="gradients",
    )(index, pred_near, pred_far, in_hbm(target), gene_rows, spot_rows, weights)


def add_columns(keep, *received):
    rows, width = keep.shape
    tile = rows // 2
    half = width // 2

    def kernel(keep_ref, *refs):
        received_refs, (keep_out, send_out) = refs[:-2], refs[-2:]
        if len(received) == 1:
            keep_out[...] = keep_ref[:, :half] + received_refs[0][:, :half].astype(F32)
            send_out[...] = (keep_ref[:, half:] + received_refs[0][:, half:].astype(F32)).astype(BF16)
        else:
            keep_out[...] = keep_ref[:, :half] + received_refs[0][...].astype(F32)
            send_out[...] = (keep_ref[:, half:] + received_refs[1][...].astype(F32)).astype(BF16)

    whole = pl.BlockSpec((tile, width), lambda i: (i, 0))
    out = pl.BlockSpec((tile, half), lambda i: (i, 0))
    return pl.pallas_call(
        kernel,
        grid=(rows // tile,),
        in_specs=[whole] + ([whole] if len(received) == 1 else [out] * 2),
        out_specs=[out, out],
        out_shape=[shape((rows, half), F32), shape((rows, half), BF16)],
        cost_estimate=COST,
        compiler_params=params(20),
        name="add_columns",
    )(keep, *received)


def assemble(kept, received, size):
    rows, width = kept[0].shape
    chunks = len(kept)
    tile = TILE_Y

    def kernel(*refs):
        out_ref = refs[-1]
        sums = [refs[k][...] + refs[chunks + k][...].astype(F32) for k in range(chunks)]
        pieces = [sums[k][:, d * size : (d + 1) * size] for d in range(width // size) for k in range(chunks)]
        out_ref[...] = jnp.concatenate(pieces, axis=1)

    spec = pl.BlockSpec((tile, width), lambda i: (i, 0))
    return pl.pallas_call(
        kernel,
        grid=(rows // tile,),
        in_specs=[spec] * (2 * chunks),
        out_specs=pl.BlockSpec((tile, width * chunks), lambda i: (i, 0)),
        out_shape=shape((rows, width * chunks), F32),
        cost_estimate=COST,
        compiler_params=params(24),
        name="assemble",
    )(*kept, *received)


def assemble_pair(pair, kept, received, size, before):
    rows, width = kept[0].shape
    tile = rows // 2

    def kernel(*refs):
        out_ref = refs[-1]
        sums = [refs[k][...] + refs[2 + k][...].astype(F32) for k in range(2)]
        for d in range(width // size):

            @pl.when(pl.program_id(1) == d)
            def _():
                out_ref[...] = jnp.concatenate([v[:, d * size : (d + 1) * size] for v in sums], axis=1)

    spec = pl.BlockSpec((tile, width), lambda i, d: (i, 0))
    others = [] if before is None else [before]
    return pl.pallas_call(
        kernel,
        grid=(rows // tile, width // size),
        in_specs=[spec] * 4 + [pl.BlockSpec(memory_space=pl.ANY)] * len(others),
        out_specs=pl.BlockSpec((tile, 2 * size), lambda i, d: (i, d * (CHUNKS // 2) + pair)),
        out_shape=pltpu.HBM((rows, width * CHUNKS), F32),
        input_output_aliases={4: 0} if others else {},
        cost_estimate=COST,
        compiler_params=params(24),
        name="assemble_pair",
    )(*kept, *received, *[in_hbm(v) for v in others])


def logit_gradient(sums, expr, grads, logits, size_column, counts, totals, backs):
    rows, genes = expr.shape
    parts, size, spots = grads[0].shape
    chunks = len(grads)
    tile = TILE_X

    def kernel(sums_ref, expr_ref, logit_ref, column_ref, counts_ref, totals_ref, *refs):
        grad_refs, back_refs, (out_ref, grad) = refs[:chunks], refs[chunks : 2 * chunks], refs[2 * chunks :]

        @pl.when(pl.program_id(0) == 0)
        def _():
            for k, ref in enumerate(grad_refs):
                for d in range(parts):
                    at = (d * chunks + k) * size
                    grad[at : at + size, :] = ref[d]

        inverse = 1.0 / sums_ref[0:1, :]
        mass = sums_ref[1:2, :] / sums_ref[0:1, :]
        mass_grad = 1.0 / totals_ref[0:1, 1:2] - counts_ref[...] / (totals_ref[0:1, 2:3] * mass)
        back = sum(ref[...] for ref in back_refs) + mass * mass_grad
        acc = jnp.dot(expr_ref[...], grad[...], preferred_element_type=F32)
        probs = jnp.exp(logit_ref[...]) * inverse
        out_ref[...] = probs * ((acc + mass_grad) * tile_lanes(column_ref[...], spots) - back)

    across = pl.BlockSpec((tile, spots), lambda i: (i, 0))
    row = pl.BlockSpec((1, spots), lambda i: (0, 0))
    vmem = pl.BlockSpec(memory_space=pltpu.VMEM)
    return pl.pallas_call(
        kernel,
        grid=(rows // tile,),
        in_specs=[
            pl.BlockSpec((2, spots), lambda i: (0, 0)),
            pl.BlockSpec((tile, genes), lambda i: (i, 0)),
            across,
            pl.BlockSpec((tile, LANES), lambda i: (i, 0)),
            row,
            pl.BlockSpec((1, LANES), lambda i: (0, 0)),
        ]
        + [vmem] * chunks
        + [row] * chunks,
        out_specs=across,
        out_shape=pltpu.HBM((rows, spots), F32),
        scratch_shapes=[pltpu.VMEM((genes, spots), BF16)],
        cost_estimate=COST,
        compiler_params=params(34),
        name="logit_gradient",
    )(sums, in_hbm(expr), in_hbm(logits), size_column, counts, totals, *grads, *backs)


def on_device(logits, centroid_expr, target, sizes, counts):
    parts = lax.axis_size("cent")
    halves = bits_of(parts)
    n_spot = lax.axis_size("spot")
    spot_bits = bits_of(n_spot)
    rows, genes = centroid_expr.shape
    spots = logits.shape[1]
    spots_all = spots * n_spot
    per_device = genes // parts
    size = per_device // CHUNKS
    counts_f = counts.astype(F32).reshape(1, spots)
    target_rows = target.reshape(parts * CHUNKS, size, spots)
    target_chunks = target.reshape(parts, CHUNKS, size, spots)
    order = Order()
    index = jnp.stack([lax.axis_index("cent"), lax.axis_index("spot")])

    made = {}
    keeps, arrived, nears, fars, grads, backs, kept, landed = ([None] * CHUNKS for _ in range(8))

    def stats_step():
        sums, made["column"] = order.run(lambda i, *a: column_stats(i, *a, rows // 4), index, logits, sizes)
        made["total"] = sum_over(sums, "cent")

    def predict_step(k):
        if k == 0:
            out = order.run(
                lambda i, e, *a: predict(i, 0, parts, e, None, a), index, centroid_expr, logits, made["total"], made["column"]
            )
            made["weights"] = out[-1]
        else:
            before = made.pop("turned", None)
            out = order.run(lambda i, e, w: predict(i, k, parts, e, w, None, before), index, centroid_expr, made["weights"])
        if len(out) > (3 if k == 0 else 2):
            made["turned"] = out[2]
        keeps[k] = out[0]
        arrived[k] = swap(out[1], "cent", bit_order(k, halves)[0])

    def halve_step(at):
        def step(k):
            b = bit_order(k, halves)[at]
            keeps[k], send = order.run(lambda i, *a: add_and_halve(i, b, *a), index, keeps[k], arrived[k])
            arrived[k] = swap(send, "cent", b)

        return step

    def finish_step(k):
        *made["rows"], low = order.run(
            lambda i, *a: finish_rows(i, k, per_device, *a), index, keeps[k], arrived[k], target_rows, made.get("rows")
        )
        nears[k], fars[k] = low, swap(low, "cent", bit_order(k, halves)[-1])

    def pair_up_step(k):
        pieces = [v[c] for c in gathered_with(k) for v in (nears, fars)]
        (nears[k],) = order.run(lambda *a: (join(*a),), *pieces)
        fars[k] = swap(nears[k], "cent", bit_order(k, halves)[0])

    def join_step(at):
        def step(k):
            (nears[k],) = order.run(lambda *a: (join(*a),), nears[k], fars[k])
            fars[k] = swap(nears[k], "cent", bit_order(k, halves)[at])

        return step

    def totals_step():
        (made["totals"],) = order.run(lambda *a: (spot_totals(*a),), made["total"], counts_f)

    def genes_step():
        made["sums"] = made["rows"][1]
        made["hop"] = swap(made["sums"], "spot", 0)

    def genes_hop(b):
        def step():
            (made["sums"],) = order.run(lambda *a: (a[0] + a[1],), made["sums"], made["hop"])
            if b + 1 < spot_bits:
                made["hop"] = swap(made["sums"], "spot", b + 1)

        return step

    def slots_step():
        (made["slots"],) = order.run(lambda *a: (gene_slots(*a, parts),), index, made["sums"], made["rows"][2])
        made["hop"] = [swap(made["slots"], "cent", 0)]

    def slots_hop(last):
        def step():
            (made["slots"],) = order.run(lambda *a: (sum(a),), made["slots"], *made["hop"])
            if not last:
                made["hop"] = [exchange(made["slots"], "cent", 2 * j) for j in range(1, parts // 2)]

        return step

    def terms_step():
        made["genes"], made["terms"], made["row"] = order.run(
            lambda *a: gradient_terms(*a, genes, spots, CHUNKS, spots_all), made["slots"], made["totals"]
        )
        made["row_hop"] = swap(made["row"], "spot", 0)

    def row_hop(b):
        def step():
            (made["row"],) = order.run(lambda *a: (a[0] + a[1],), made["row"], made["row_hop"])
            if b + 1 < spot_bits:
                made["row_hop"] = swap(made["row"], "spot", b + 1)

        return step

    def losses_step():
        (made["losses"],) = order.run(lambda *a: (loss_row(*a, genes, spots_all, n_spot),), made["row"])

    def gradients_step(k):
        first, *_ = group = gathered_with(k)
        near, far = (v[first].reshape(len(group), parts // 2, size, spots) for v in (nears, fars))
        operands = (near, far, target_chunks, made["genes"], made["terms"], made["weights"])
        grads[k], backs[k], kept[k], *sends = order.run(lambda i, *a: gradients(i, k, n_spot, *a), index, *operands)
        landed[k] = [swap(send, "spot", 0) for send in sends]

    def columns_step(b):
        def step(k):
            kept[k], send = order.run(add_columns, kept[k], *landed[k])
            landed[k] = [swap(send, "spot", b)]

        return step

    def logits_step():
        (made["logit_grad"],) = order.run(
            lambda t, e, *a: (logit_gradient(t, e, grads, *a, backs),),
            *(made["total"], centroid_expr, logits, made["column"], counts_f, made["row"])
        )

    def centroids_step():
        (made["centroid_grad"],) = order.run(lambda *a: (assemble(a[:CHUNKS], a[CHUNKS:], size),), *kept, *sum(landed, []))

    def pair_step(pair):
        chunks = slice(2 * pair, 2 * pair + 2)
        before = made.get("centroid_grad")
        (made["centroid_grad"],) = order.run(
            lambda *a: (assemble_pair(pair, a[:2], a[2:], size, before),), *kept[chunks], *sum(landed[chunks], [])
        )

    def wait_for(values):
        return lambda k: order.wait(values[k])

    steps = {"C": stats_step, "P": predict_step, "F": finish_step, "T": totals_step, "g": genes_step}
    steps |= {"S": slots_step, "s0": slots_hop(False), "s1": slots_hop(True), "R": terms_step, "L": losses_step}
    steps |= {"p": pair_up_step, "G": gradients_step, "X": logits_step, "Y": centroids_step, "y": pair_step}
    steps |= {"wa": wait_for(arrived), "wf": wait_for(fars), "wl": wait_for(landed)}
    steps |= {f"a{b}": halve_step(b) for b in range(1, halves)}
    steps |= {f"j{b}": join_step(b) for b in range(halves - 1)}
    steps |= {f"e{b}": columns_step(b) for b in range(1, spot_bits)}
    steps |= {f"g{b}": genes_hop(b) for b in range(spot_bits)}
    steps |= {f"r{b}": row_hop(b) for b in range(spot_bits)}
    for name in schedule(halves, spot_bits).split():
        step, _, k = name.partition(".")
        steps[step](*([int(k)] if k else []))
    return made["losses"][0, :4], made["rows"][0], made["logit_grad"], made["centroid_grad"]


def schedule(halves, spot_bits):
    if (halves, spot_bits) == (3, 2):
        steps = (
            "C P.0 P.1 P.2", "a1.0 P.3 a1.1 a2.0", "a1.2 wa.0 F.0 a1.3", "a2.2 j1.0 a2.1 F.2",
            "a2.3 wf.0 F.1 F.3", "wf.2 g j0.0 g0", "j1.2 g1 T S", "s0 wf.2 j1.1 j1.3",
            "s1 R r0 p.2", "j0.1 G.0 e1.0 G.1", "wl.0 e1.1 G.2 r1", "L G.3 e1.2 y.0",
            "e1.3 X y.1",
        )
        return " ".join(steps)
    forward = ["P", *(f"a{b}" for b in range(1, halves)), "F"]
    backward = ["G", *(f"e{b}" for b in range(1, spot_bits))]
    waves = [
        [f"{chain[wave - k]}.{k}" for wave in range(len(chain) + CHUNKS) for k in range(CHUNKS) if 0 <= wave - k < len(chain)]
        for chain in (forward, backward)
    ]
    gather = []
    for group in sorted({tuple(gathered_with(k)) for k in range(CHUNKS)}):
        gather += [f"j{b}.{k}" for k in group for b in range(halves - 2, 0, -1)]
        gather.append(f"j0.{group[0]}" if len(group) == 1 else f"p.{group[0]}")
    middle = gather + ["T", "g", *(f"g{b}" for b in range(spot_bits)), "S", "s0", "s1", "R"]
    middle += [*(f"r{b}" for b in range(spot_bits)), "L"]
    return " ".join(["C"] + waves[0] + middle + waves[1] + ["X", "Y"])


def solution(mesh):
    in_specs = (P("cent", "spot"), P("cent", None), P(None, "spot"), P("cent"), P("spot"))
    out_specs = (P(), P("cent", "spot"), P("cent", "spot"), P("cent", "spot"))
    return jax.shard_map(
        on_device, mesh=mesh, in_specs=in_specs, out_specs=out_specs, check_vma=False
    )
```

```python
import functools

import jax
import jax.numpy as jnp
from jax import lax
from jax.experimental import pallas as pl
from jax.experimental.pallas import tpu as pltpu
from jax.sharding import PartitionSpec as P

EPS = 1e-06
F32 = jnp.float32
BF16 = jnp.bfloat16
LANES = 128
CHUNKS = 4
TILE_P = 512
TILE_G = 2560
PART_G = 640
TILE_X = 512
TILE_Y = 512
COST = pl.CostEstimate(flops=1, transcendentals=0, bytes_accessed=1)


def params(mebibytes):
    return pltpu.CompilerParams(vmem_limit_bytes=mebibytes << 20)


def shape(dims, dtype):
    return jax.ShapeDtypeStruct(dims, dtype)


def in_hbm(value):
    return pltpu.with_memory_space_constraint(value, pltpu.HBM)


def bits_of(count):
    return count.bit_length() - 1


def reversed_bits(value, bits):
    return sum(((value >> b) & 1) << (bits - 1 - b) for b in range(bits))


def bit_order(chunk, bits):
    return (1, 0, *range(2, bits)) if chunk == 1 and bits > 2 else tuple(range(bits))


def gathered_with(chunk):
    last = [CHUNKS - 2, CHUNKS - 1]
    return last if chunk in last else [chunk]


def place_among(device, order):
    return sum(((device >> bit) & 1) << at for at, bit in enumerate(order))


def exchange(value, axis, bits):
    return lax.ppermute(value, axis, [(i, i ^ bits) for i in range(lax.axis_size(axis))])


def swap(value, axis, bit):
    return exchange(value, axis, 1 << bit)


def sum_over(value, axis):
    for bit in range(bits_of(lax.axis_size(axis))):
        value = value + swap(value, axis, bit)
    return value


def tile_lanes(column, width):
    return jnp.concatenate([column] * (width // LANES), axis=1)


def column_of(row, length):
    return jnp.transpose(jnp.broadcast_to(row, (LANES, length)))


class Order:
    def __init__(self):
        self.last = ()

    def wait(self, value):
        self.last += tuple(value) if isinstance(value, list) else (value,)

    def run(self, step, first, *others):
        if self.last:
            first = lax.optimization_barrier((first, *self.last))[0]
        results = step(first, *others)
        self.last = (results[-1],)
        return results


def column_stats(index, logits, sizes, tile):
    rows, spots = logits.shape

    def kernel(index_ref, logit_ref, size_ref, sums_ref, column_ref, acc):
        step = pl.program_id(0)
        expo = jnp.exp(logit_ref[...])
        part = size_ref[pl.ds(pl.multiple_of(step * tile, LANES), tile)]
        column = column_of(part.astype(F32).reshape(1, tile), tile)
        column_ref[...] = column
        mass = expo * tile_lanes(column, spots)
        total = expo.reshape(tile // 8, 8, spots).sum(0)
        mass = mass.reshape(tile // 8, 8, spots).sum(0)

        @pl.when(step == 0)
        def _():
            acc[0] = total
            acc[1] = mass

        @pl.when(step > 0)
        def _():
            acc[0] += total
            acc[1] += mass

        @pl.when(step == pl.num_programs(0) - 1)
        def _():
            sums_ref[0:1, :] = acc[0].sum(0, keepdims=True)
            sums_ref[1:2, :] = acc[1].sum(0, keepdims=True)

    return pl.pallas_call(
        kernel,
        grid_spec=pltpu.PrefetchScalarGridSpec(
            num_scalar_prefetch=1,
            grid=(rows // tile,),
            in_specs=[
                pl.BlockSpec((tile, spots), lambda i, s: (i, 0)),
                pl.BlockSpec((rows,), lambda i, s: (0,)),
            ],
            out_specs=[
                pl.BlockSpec((2, spots), lambda i, s: (0, 0)),
                pl.BlockSpec((tile, LANES), lambda i, s: (i, 0)),
            ],
            scratch_shapes=[pltpu.VMEM((2, 8, spots), F32)],
        ),
        out_shape=[shape((2, spots), F32), shape((rows, LANES), F32)],
        cost_estimate=COST,
        compiler_params=params(20),
        name="column_stats",
    )(index, in_hbm(logits), in_hbm(sizes))


def predict(index, chunk, parts, expr, weights, first=None, turned_before=None):
    rows = first[0].shape[0] if first is not None else weights.shape[0]
    spots = (weights if first is None else first[0]).shape[1]
    genes = expr.shape[1]
    per_device = genes // parts
    size = per_device // CHUNKS
    width = parts * size
    starts = [d * per_device + chunk * size for d in range(parts)]
    blocks = sorted({s // LANES for s in starts})
    shares = chunk + 1 < CHUNKS and sorted({(s + size) // LANES for s in starts}) == blocks
    shares = shares and turned_before is None
    tile = TILE_P
    order = bit_order(chunk, bits_of(parts))
    order_next = bit_order(chunk + 1, bits_of(parts))
    n_in = (1 if turned_before is not None else len(blocks)) + (1 if first is None else 3)

    def kernel(index_ref, *refs):
        inputs, rest = refs[:n_in], refs[n_in:]
        keep_ref, send_ref = rest[:2]
        turned = inputs[0] if turned_before is not None else rest[-1]
        turned_next = rest[2] if shares else None
        if first is None:
            weight_ref = inputs[-1]
        else:
            logit_ref, sums_ref, column_ref = inputs[-3:]
            weight_ref = rest[3 if shares else 2]

        if turned_before is None:

            @pl.when(pl.program_id(0) == 0)
            def _():
                for number, block in enumerate(blocks):
                    block_t = jnp.transpose(inputs[number][...])
                    for d, start in enumerate(starts):
                        if start // LANES == block:
                            at_row = start % LANES
                            at = place_among(d, order) * size
                            turned[at : at + size, :] = block_t[at_row : at_row + size]
                            if shares:
                                at = place_among(d, order_next) * size
                                turned_next[at : at + size, :] = block_t[at_row + size : at_row + 2 * size]

        if first is not None:
            scale = 1.0 / sums_ref[0:1, :]
            weight = jnp.exp(logit_ref[...]) * scale * tile_lanes(column_ref[...], tile)
            weight_ref[...] = weight.astype(BF16)
        out = jnp.dot(turned[...], weight_ref[...], preferred_element_type=F32)
        even = ((index_ref[0] >> order[0]) & 1) == 0
        for j in range(parts // 2):
            a = out[2 * j * size : (2 * j + 1) * size]
            b = out[(2 * j + 1) * size : (2 * j + 2) * size]
            keep_ref[j] = jnp.where(even, a, b)
            send_ref[j] = jnp.where(even, b, a).astype(BF16)

    half = pl.BlockSpec((parts // 2, size, tile), lambda i, s: (0, 0, i))
    columns = pl.BlockSpec((rows, tile), lambda i, s: (0, i))
    whole = pl.BlockSpec((width, rows), lambda i, s: (0, 0))
    if turned_before is None:
        in_specs = [
            pl.BlockSpec((rows, LANES), lambda i, s, b=b: (0, b), pipeline_mode=pl.Buffered(1)) for b in blocks
        ]
        operands = [in_hbm(expr)] * len(blocks)
    else:
        in_specs, operands = [whole], [turned_before]
    out_specs = [half, half]
    out_shapes = [shape((parts // 2, size, spots), F32), shape((parts // 2, size, spots), BF16)]
    if shares:
        out_specs.append(whole)
        out_shapes.append(shape((width, rows), BF16))
    if first is None:
        in_specs.append(columns)
        operands.append(weights)
    else:
        in_specs += [columns, pl.BlockSpec((2, tile), lambda i, s: (0, i)), pl.BlockSpec((rows, LANES), lambda i, s: (0, 0))]
        operands += [in_hbm(first[0]), *first[1:]]
        out_specs.append(columns)
        out_shapes.append(shape((rows, spots), BF16))
    return pl.pallas_call(
        kernel,
        grid_spec=pltpu.PrefetchScalarGridSpec(
            num_scalar_prefetch=1,
            grid=(spots // tile,),
            in_specs=in_specs,
            out_specs=out_specs,
            scratch_shapes=[pltpu.VMEM((width, rows), BF16)] if turned_before is None else [],
        ),
        out_shape=out_shapes,
        cost_estimate=COST,
        compiler_params=params(20 if first is None else 36),
        name="predict",
    )(index, *operands)


def add_and_halve(index, bit, keep, received):
    count, size, spots = keep.shape

    def kernel(index_ref, keep_ref, received_ref, keep_out, send_out):
        a = keep_ref[0] + received_ref[0].astype(F32)
        b = keep_ref[1] + received_ref[1].astype(F32)
        even = ((index_ref[0] >> bit) & 1) == 0
        keep_out[0] = jnp.where(even, a, b)
        send_out[0] = jnp.where(even, b, a).astype(BF16)

    pair = pl.BlockSpec((2, size, spots), lambda i, s: (i, 0, 0))
    one = pl.BlockSpec((1, size, spots), lambda i, s: (i, 0, 0))
    return pl.pallas_call(
        kernel,
        grid_spec=pltpu.PrefetchScalarGridSpec(
            num_scalar_prefetch=1, grid=(count // 2,), in_specs=[pair, pair], out_specs=[one, one]
        ),
        out_shape=[shape((count // 2, size, spots), F32), shape((count // 2, size, spots), BF16)],
        cost_estimate=COST,
        compiler_params=params(10),
        name="add_and_halve",
    )(index, keep, received)


def finish_rows(index, chunk, per_device, keep, received, target_rows, earlier):
    _, size, spots = keep.shape

    def kernel(index_ref, keep_ref, received_ref, target_ref, *refs):
        pred_ref, gene_ref, spot_ref, low_ref = refs[-4:]
        pred = keep_ref[0] + received_ref[0].astype(F32)
        target = target_ref[0].astype(F32)
        pred_ref[...] = pred
        low_ref[0] = pred.astype(BF16)
        for at, product in enumerate((pred * target, pred * pred, target * target)):
            by_gene = jnp.sum(product, axis=1, keepdims=True)
            by_gene = jnp.transpose(jnp.broadcast_to(by_gene, (size, LANES)))
            gene_ref[0, at : at + 1, :] = by_gene[0:1, :]
            by_spot = jnp.sum(product, axis=0, keepdims=True)
            if earlier is not None:
                by_spot = by_spot + refs[0][at : at + 1, :]
            spot_ref[at : at + 1, :] = by_spot

    one = pl.BlockSpec((1, size, spots), lambda i, s: (0, 0, 0))
    by_spot = pl.BlockSpec((3, spots), lambda i, s: (0, 0))
    whole = pl.BlockSpec(memory_space=pl.ANY)
    operands = [] if earlier is None else [earlier[2], in_hbm(earlier[0]), earlier[1]]
    return pl.pallas_call(
        kernel,
        grid_spec=pltpu.PrefetchScalarGridSpec(
            num_scalar_prefetch=1,
            grid=(1,),
            in_specs=[one, one, pl.BlockSpec((1, size, spots), lambda i, s: (s[0] * CHUNKS + chunk, 0, 0))]
            + [by_spot, whole, whole][: len(operands)],
            out_specs=[
                pl.BlockSpec((size, spots), lambda i, s: (chunk, 0)),
                pl.BlockSpec((1, 3, size), lambda i, s: (chunk, 0, 0)),
                by_spot,
                one,
            ],
        ),
        out_shape=[
            pltpu.HBM((per_device, spots), F32),
            shape((CHUNKS, 3, size), F32),
            shape((3, spots), F32),
            shape((1, size, spots), BF16),
        ],
        input_output_aliases={5: 0, 6: 1} if operands else {},
        cost_estimate=COST,
        compiler_params=params(10),
        name="finish_rows",
    )(index, keep, received, in_hbm(target_rows), *operands)


def row_of(*values):
    lane = lax.broadcasted_iota(jnp.int32, (1, LANES), 1)
    return sum(jnp.where(lane == at, value, 0.0) for at, value in enumerate(values))


def spot_totals(sums, counts):
    def kernel(sums_ref, counts_ref, out_ref):
        mass = sums_ref[1:2, :] / sums_ref[0:1, :]
        count = counts_ref[...]
        diverged = count * (jnp.log(count) - jnp.log(mass))
        out_ref[...] = row_of(jnp.sum(diverged), jnp.sum(mass), jnp.sum(count))

    return pl.pallas_call(
        kernel, out_shape=shape((1, LANES), F32), cost_estimate=COST, compiler_params=params(4), name="spot_totals"
    )(sums, counts)


def gene_slots(index, gene_sums, spot_sums, parts):
    chunks, _, size = gene_sums.shape
    spots = spot_sums.shape[1]
    genes = parts * chunks * size
    width = max(genes, spots)

    def kernel(index_ref, gene_ref, spot_ref, out_ref):
        out_ref[...] = jnp.zeros((8, width), F32)
        out_ref[3:6, 0:spots] = spot_ref[...]
        lane = lax.broadcasted_iota(jnp.int32, (1, parts * size), 1)
        mine = (lane >= index_ref[0] * size) & (lane < (index_ref[0] + 1) * size)
        for k in range(chunks):
            dot, pp, tt = (gene_ref[k, at : at + 1, :] for at in range(3))
            scale = lax.rsqrt(pp + EPS) * lax.rsqrt(tt + EPS)
            cosine = dot * scale
            for at, value in enumerate(((-1.0 / genes) * scale, (1.0 / genes) * cosine / (pp + EPS), cosine)):
                spread = jnp.concatenate([value] * parts, axis=1)
                out_ref[at : at + 1, k * parts * size : (k + 1) * parts * size] = jnp.where(mine, spread, 0.0)

    smem = pl.BlockSpec(memory_space=pltpu.SMEM)
    vmem = pl.BlockSpec(memory_space=pltpu.VMEM)
    return pl.pallas_call(
        kernel,
        in_specs=[smem, vmem, vmem],
        out_shape=shape((8, width), F32),
        cost_estimate=COST,
        compiler_params=params(4),
        name="gene_slots",
    )(index, gene_sums, spot_sums)


def gradient_terms(slots, totals, genes, spots, chunks, spots_all):
    def kernel(slots_ref, totals_ref, gene_ref, spot_ref, row_ref):
        for k in range(chunks):
            gene_ref[k] = slots_ref[0:2, k * (genes // chunks) : (k + 1) * (genes // chunks)]
        dot, pp, tt = (slots_ref[3 + at : 4 + at, 0:spots] for at in range(3))
        scale = lax.rsqrt(pp + EPS) * lax.rsqrt(tt + EPS)
        cosine = dot * scale
        spot_ref[0:1, :] = (-1.0 / spots_all) * scale
        spot_ref[1:2, :] = (1.0 / spots_all) * cosine / (pp + EPS)
        row_ref[...] = totals_ref[...] + row_of(0.0, 0.0, 0.0, jnp.sum(slots_ref[2:3, 0:genes]), jnp.sum(cosine))

    return pl.pallas_call(
        kernel,
        out_shape=[shape((chunks, 2, genes // chunks), F32), shape((2, spots), F32), shape((1, LANES), F32)],
        cost_estimate=COST,
        compiler_params=params(4),
        name="gradient_terms",
    )(slots, totals)


def loss_row(row, genes, spots_all, n_spot):
    def kernel(row_ref, out_ref):
        kl_sum, mass_total, count_total, gene_sum, spot_sum = (row_ref[0:1, at : at + 1] for at in range(5))
        gene_mean = gene_sum / (genes * n_spot)
        spot_mean = spot_sum / spots_all
        kl = kl_sum / count_total + jnp.log(mass_total) - jnp.log(count_total)
        out_ref[...] = row_of(kl - gene_mean - spot_mean, gene_mean, spot_mean, kl)

    return pl.pallas_call(
        kernel, out_shape=shape((1, LANES), F32), cost_estimate=COST, compiler_params=params(4), name="loss_row"
    )(row)


def join(*pieces):
    count, size, spots = pieces[0].shape

    def kernel(*refs):
        for at, ref in enumerate(refs[:-1]):
            refs[-1][at * count : (at + 1) * count] = ref[...]

    vmem = pl.BlockSpec(memory_space=pltpu.VMEM)
    return pl.pallas_call(
        kernel,
        in_specs=[vmem] * len(pieces),
        out_specs=vmem,
        out_shape=shape((len(pieces) * count, size, spots), BF16),
        cost_estimate=COST,
        compiler_params=params(4),
        name="join",
    )(*pieces)


def fetch(index, chunk, target):
    parts, _, size, spots = target.shape

    def kernel(index_ref, target_ref, out_ref):
        out_ref[...] = target_ref[:, 0]

    return pl.pallas_call(
        kernel,
        grid_spec=pltpu.PrefetchScalarGridSpec(
            num_scalar_prefetch=1,
            grid=(1,),
            in_specs=[pl.BlockSpec((parts, 1, size, spots), lambda i, s: (0, chunk, 0, 0))],
            out_specs=pl.BlockSpec((parts, size, spots), lambda i, s: (0, 0, 0)),
        ),
        out_shape=shape((parts, size, spots), BF16),
        cost_estimate=COST,
        compiler_params=params(8),
        name="fetch",
    )(index, in_hbm(target))


def gradients(index, chunk, n_spot, pred_near, pred_far, target, gene_rows, spot_rows, weights):
    parts, size, spots = target.shape
    rows = weights.shape[0]
    tile = TILE_G
    width = parts * size
    per_spot = parts // n_spot
    spot_bits = bits_of(n_spot)
    order = bit_order(chunk, bits_of(parts))

    def kernel(index_ref, near_ref, far_ref, target_ref, gene_ref, spot_ref, weight_ref, *refs):
        grad_ref, back_ref, keep_ref, *send_refs, turned, columns = refs

        @pl.when(pl.program_id(0) == 0)
        def _():
            columns[0] = column_of(gene_ref[0, 0:1, :], width)
            columns[1] = column_of(gene_ref[0, 1:2, :], width)
            back = jnp.zeros((1, spots), F32)
            for j in range(parts):
                d = index_ref[0] ^ j
                apart = reversed_bits((d // per_spot) ^ index_ref[1], spot_bits)
                place = apart * per_spot + d % per_spot
                at = pl.multiple_of(d * size, size)
                among = place_among(j, order[:0:-1])
                pred = (far_ref if (j >> order[0]) & 1 else near_ref)[0, among].astype(F32)
                by_target = tile_lanes(columns[0, pl.ds(at, size), :], spots) + spot_ref[0:1, :]
                by_pred = tile_lanes(columns[1, pl.ds(at, size), :], spots) + spot_ref[1:2, :]
                grad = (target_ref[d].astype(F32) * by_target + pred * by_pred).astype(BF16)
                grad_ref[d] = grad
                turned[pl.ds(pl.multiple_of(place * size, size), size), :] = grad
                back = back + jnp.sum(grad.astype(F32) * pred, axis=0, keepdims=True)
            back_ref[...] = back

        @pl.loop(0, tile, step=PART_G)
        def _(start):
            part = pl.ds(pl.multiple_of(start, PART_G), PART_G)
            out = lax.dot_general(weight_ref[part, :], turned[...], (((1,), (1,)), ((), ())), preferred_element_type=F32)
            keep_ref[part, :] = out[:, : width // 2]
            for column, send_ref in enumerate(send_refs):
                left = width // 2 + column * (width // 4)
                send_ref[part, :] = out[:, left : left + width // 4].astype(BF16)

    member = gathered_with(chunk).index(chunk)
    half = pl.BlockSpec((1, parts // 2, size, spots), lambda i, s: (member, 0, 0, 0))
    piece = pl.BlockSpec((tile, width // 2), lambda i, s: (i, 0))
    return pl.pallas_call(
        kernel,
        grid_spec=pltpu.PrefetchScalarGridSpec(
            num_scalar_prefetch=1,
            grid=(rows // tile,),
            in_specs=[
                half,
                half,
                pl.BlockSpec((parts, size, spots), lambda i, s: (0, 0, 0)),
                pl.BlockSpec((1, 2, width), lambda i, s: (chunk, 0, 0)),
                pl.BlockSpec((2, spots), lambda i, s: (0, 0)),
                pl.BlockSpec((tile, spots), lambda i, s: (i, 0)),
            ],
            out_specs=[
                pl.BlockSpec((parts, size, spots), lambda i, s: (0, 0, 0)),
                pl.BlockSpec((1, spots), lambda i, s: (0, 0)),
                piece,
            ]
            + [pl.BlockSpec((tile, width // 4), lambda i, s: (i, 0))] * 2,
            scratch_shapes=[pltpu.VMEM((width, spots), BF16), pltpu.VMEM((2, width, LANES), F32)],
        ),
        out_shape=[
            shape((parts, size, spots), BF16),
            shape((1, spots), F32),
            shape((rows, width // 2), F32),
        ]
        + [shape((rows, width // 4), BF16)] * 2,
        cost_estimate=COST,
        compiler_params=params(30),
        name="gradients",
    )(index, pred_near, pred_far, target, gene_rows, spot_rows, weights)


def add_columns(keep, *received):
    rows, width = keep.shape
    tile = rows // 2
    half = width // 2

    def kernel(keep_ref, *refs):
        received_refs, (keep_out, send_out) = refs[:-2], refs[-2:]
        if len(received) == 1:
            keep_out[...] = keep_ref[:, :half] + received_refs[0][:, :half].astype(F32)
            send_out[...] = (keep_ref[:, half:] + received_refs[0][:, half:].astype(F32)).astype(BF16)
        else:
            keep_out[...] = keep_ref[:, :half] + received_refs[0][...].astype(F32)
            send_out[...] = (keep_ref[:, half:] + received_refs[1][...].astype(F32)).astype(BF16)

    whole = pl.BlockSpec((tile, width), lambda i: (i, 0))
    out = pl.BlockSpec((tile, half), lambda i: (i, 0))
    return pl.pallas_call(
        kernel,
        grid=(rows // tile,),
        in_specs=[whole] + ([whole] if len(received) == 1 else [out] * 2),
        out_specs=[out, out],
        out_shape=[shape((rows, half), F32), shape((rows, half), BF16)],
        cost_estimate=COST,
        compiler_params=params(20),
        name="add_columns",
    )(keep, *received)


def assemble(kept, received, size):
    rows, width = kept[0].shape
    chunks = len(kept)
    tile = TILE_Y

    def kernel(*refs):
        out_ref = refs[-1]
        sums = [refs[k][...] + refs[chunks + k][...].astype(F32) for k in range(chunks)]
        pieces = [sums[k][:, d * size : (d + 1) * size] for d in range(width // size) for k in range(chunks)]
        out_ref[...] = jnp.concatenate(pieces, axis=1)

    spec = pl.BlockSpec((tile, width), lambda i: (i, 0))
    return pl.pallas_call(
        kernel,
        grid=(rows // tile,),
        in_specs=[spec] * (2 * chunks),
        out_specs=pl.BlockSpec((tile, width * chunks), lambda i: (i, 0)),
        out_shape=shape((rows, width * chunks), F32),
        cost_estimate=COST,
        compiler_params=params(24),
        name="assemble",
    )(*kept, *received)


def assemble_pair(pair, kept, received, size, before):
    rows, width = kept[0].shape
    tile = rows

    def kernel(*refs):
        out_ref = refs[-1]
        sums = [refs[k][...] + refs[2 + k][...].astype(F32) for k in range(2)]
        for d in range(width // size):

            @pl.when(pl.program_id(1) == d)
            def _():
                out_ref[...] = jnp.concatenate([v[:, d * size : (d + 1) * size] for v in sums], axis=1)

    spec = pl.BlockSpec((tile, width), lambda i, d: (i, 0))
    others = [] if before is None else [before]
    return pl.pallas_call(
        kernel,
        grid=(rows // tile, width // size),
        in_specs=[spec] * 4 + [pl.BlockSpec(memory_space=pl.ANY)] * len(others),
        out_specs=pl.BlockSpec((tile, 2 * size), lambda i, d: (i, d * (CHUNKS // 2) + pair)),
        out_shape=pltpu.HBM((rows, width * CHUNKS), F32),
        input_output_aliases={4: 0} if others else {},
        cost_estimate=COST,
        compiler_params=params(24),
        name="assemble_pair",
    )(*kept, *received, *[in_hbm(v) for v in others])


def logit_gradient(sums, expr, grads, logits, size_column, counts, totals, backs):
    rows, genes = expr.shape
    parts, size, spots = grads[0].shape
    chunks = len(grads)
    tile = TILE_X

    def kernel(sums_ref, expr_ref, logit_ref, column_ref, counts_ref, totals_ref, *refs):
        grad_refs, back_refs, (out_ref, grad) = refs[:chunks], refs[chunks : 2 * chunks], refs[2 * chunks :]

        @pl.when(pl.program_id(0) == 0)
        def _():
            for k, ref in enumerate(grad_refs):
                for d in range(parts):
                    at = (d * chunks + k) * size
                    grad[at : at + size, :] = ref[d]

        inverse = 1.0 / sums_ref[0:1, :]
        mass = sums_ref[1:2, :] / sums_ref[0:1, :]
        mass_grad = 1.0 / totals_ref[0:1, 1:2] - counts_ref[...] / (totals_ref[0:1, 2:3] * mass)
        back = sum(ref[...] for ref in back_refs) + mass * mass_grad
        acc = jnp.dot(expr_ref[...], grad[...], preferred_element_type=F32)
        probs = jnp.exp(logit_ref[...]) * inverse
        out_ref[...] = probs * ((acc + mass_grad) * tile_lanes(column_ref[...], spots) - back)

    across = pl.BlockSpec((tile, spots), lambda i: (i, 0))
    row = pl.BlockSpec((1, spots), lambda i: (0, 0))
    vmem = pl.BlockSpec(memory_space=pltpu.VMEM)
    return pl.pallas_call(
        kernel,
        grid=(rows // tile,),
        in_specs=[
            pl.BlockSpec((2, spots), lambda i: (0, 0)),
            pl.BlockSpec((tile, genes), lambda i: (i, 0)),
            across,
            pl.BlockSpec((tile, LANES), lambda i: (i, 0)),
            row,
            pl.BlockSpec((1, LANES), lambda i: (0, 0)),
        ]
        + [vmem] * chunks
        + [row] * chunks,
        out_specs=across,
        out_shape=pltpu.HBM((rows, spots), F32),
        scratch_shapes=[pltpu.VMEM((genes, spots), BF16)],
        cost_estimate=COST,
        compiler_params=params(34),
        name="logit_gradient",
    )(sums, in_hbm(expr), in_hbm(logits), size_column, counts, totals, *grads, *backs)


def on_device(logits, centroid_expr, target, sizes, counts):
    parts = lax.axis_size("cent")
    halves = bits_of(parts)
    n_spot = lax.axis_size("spot")
    spot_bits = bits_of(n_spot)
    rows, genes = centroid_expr.shape
    spots = logits.shape[1]
    spots_all = spots * n_spot
    per_device = genes // parts
    size = per_device // CHUNKS
    counts_f = counts.astype(F32).reshape(1, spots)
    target_rows = target.reshape(parts * CHUNKS, size, spots)
    target_chunks = target.reshape(parts, CHUNKS, size, spots)
    order = Order()
    index = jnp.stack([lax.axis_index("cent"), lax.axis_index("spot")])

    made = {}
    keeps, arrived, nears, fars, fetched, grads, backs, kept, landed = ([None] * CHUNKS for _ in range(9))

    def stats_step():
        sums, made["column"] = order.run(lambda i, *a: column_stats(i, *a, rows // 4), index, logits, sizes)
        made["total"] = sum_over(sums, "cent")

    def predict_step(k):
        if k == 0:
            out = order.run(
                lambda i, e, *a: predict(i, 0, parts, e, None, a), index, centroid_expr, logits, made["total"], made["column"]
            )
            made["weights"] = out[-1]
        else:
            before = made.pop("turned", None)
            out = order.run(lambda i, e, w: predict(i, k, parts, e, w, None, before), index, centroid_expr, made["weights"])
        if len(out) > (3 if k == 0 else 2):
            made["turned"] = out[2]
        keeps[k] = out[0]
        arrived[k] = swap(out[1], "cent", bit_order(k, halves)[0])

    def halve_step(at):
        def step(k):
            b = bit_order(k, halves)[at]
            keeps[k], send = order.run(lambda i, *a: add_and_halve(i, b, *a), index, keeps[k], arrived[k])
            arrived[k] = swap(send, "cent", b)

        return step

    def finish_step(k):
        *made["rows"], low = order.run(
            lambda i, *a: finish_rows(i, k, per_device, *a), index, keeps[k], arrived[k], target_rows, made.get("rows")
        )
        nears[k], fars[k] = low, swap(low, "cent", bit_order(k, halves)[-1])

    def pair_up_step(k):
        pieces = [v[c] for c in gathered_with(k) for v in (nears, fars)]
        (nears[k],) = order.run(lambda *a: (join(*a),), *pieces)
        fars[k] = swap(nears[k], "cent", bit_order(k, halves)[0])

    def join_step(at):
        def step(k):
            (nears[k],) = order.run(lambda *a: (join(*a),), nears[k], fars[k])
            fars[k] = swap(nears[k], "cent", bit_order(k, halves)[at])

        return step

    def totals_step():
        (made["totals"],) = order.run(lambda *a: (spot_totals(*a),), made["total"], counts_f)

    def genes_step():
        made["sums"] = made["rows"][1]
        made["hop"] = swap(made["sums"], "spot", 0)

    def genes_hop(b):
        def step():
            (made["sums"],) = order.run(lambda *a: (a[0] + a[1],), made["sums"], made["hop"])
            if b + 1 < spot_bits:
                made["hop"] = swap(made["sums"], "spot", b + 1)

        return step

    def slots_step():
        (made["slots"],) = order.run(lambda *a: (gene_slots(*a, parts),), index, made["sums"], made["rows"][2])
        made["hop"] = [swap(made["slots"], "cent", 0)]

    def slots_hop(last):
        def step():
            (made["slots"],) = order.run(lambda *a: (sum(a),), made["slots"], *made["hop"])
            if not last:
                made["hop"] = [exchange(made["slots"], "cent", 2 * j) for j in range(1, parts // 2)]

        return step

    def terms_step():
        made["genes"], made["terms"], made["row"] = order.run(
            lambda *a: gradient_terms(*a, genes, spots, CHUNKS, spots_all), made["slots"], made["totals"]
        )
        made["row_hop"] = swap(made["row"], "spot", 0)

    def row_hop(b):
        def step():
            (made["row"],) = order.run(lambda *a: (a[0] + a[1],), made["row"], made["row_hop"])
            if b + 1 < spot_bits:
                made["row_hop"] = swap(made["row"], "spot", b + 1)

        return step

    def losses_step():
        (made["losses"],) = order.run(lambda *a: (loss_row(*a, genes, spots_all, n_spot),), made["row"])

    def fetch_step(k):
        (fetched[k],) = order.run(lambda i, t: (fetch(i, k, t),), index, target_chunks)

    def gradients_step(k):
        first, *_ = group = gathered_with(k)
        near, far = (v[first].reshape(len(group), parts // 2, size, spots) for v in (nears, fars))
        operands = (near, far, fetched[k], made["genes"], made["terms"], made["weights"])
        grads[k], backs[k], kept[k], *sends = order.run(lambda i, *a: gradients(i, k, n_spot, *a), index, *operands)
        landed[k] = [swap(send, "spot", 0) for send in sends]

    def columns_step(b):
        def step(k):
            kept[k], send = order.run(add_columns, kept[k], *landed[k])
            landed[k] = [swap(send, "spot", b)]

        return step

    def logits_step():
        (made["logit_grad"],) = order.run(
            lambda t, e, *a: (logit_gradient(t, e, grads, *a, backs),),
            *(made["total"], centroid_expr, logits, made["column"], counts_f, made["row"])
        )

    def centroids_step():
        (made["centroid_grad"],) = order.run(lambda *a: (assemble(a[:CHUNKS], a[CHUNKS:], size),), *kept, *sum(landed, []))

    def pair_step(pair):
        chunks = slice(2 * pair, 2 * pair + 2)
        before = made.get("centroid_grad")
        (made["centroid_grad"],) = order.run(
            lambda *a: (assemble_pair(pair, a[:2], a[2:], size, before),), *kept[chunks], *sum(landed[chunks], [])
        )

    def wait_for(values):
        return lambda k: order.wait(values[k])

    steps = {"C": stats_step, "P": predict_step, "F": finish_step, "T": totals_step, "g": genes_step}
    steps |= {"S": slots_step, "s0": slots_hop(False), "s1": slots_hop(True), "R": terms_step, "L": losses_step}
    steps |= {"p": pair_up_step, "t": fetch_step, "G": gradients_step, "X": logits_step, "Y": centroids_step, "y": pair_step}
    steps |= {"wa": wait_for(arrived), "wf": wait_for(fars), "wl": wait_for(landed)}
    steps |= {f"a{b}": halve_step(b) for b in range(1, halves)}
    steps |= {f"j{b}": join_step(b) for b in range(halves - 1)}
    steps |= {f"e{b}": columns_step(b) for b in range(1, spot_bits)}
    steps |= {f"g{b}": genes_hop(b) for b in range(spot_bits)}
    steps |= {f"r{b}": row_hop(b) for b in range(spot_bits)}
    for name in schedule(halves, spot_bits).split():
        step, _, k = name.partition(".")
        steps[step](*([int(k)] if k else []))
    return made["losses"][0, :4], made["rows"][0], made["logit_grad"], made["centroid_grad"]


def schedule(halves, spot_bits):
    if (halves, spot_bits) == (3, 2):
        steps = (
            "C P.0 P.1 P.2", "a1.0 P.3 a1.1 a2.0", "a1.2 wa.0 F.0 a1.3", "a2.2 j1.0 a2.1 F.2",
            "a2.3 wf.0 F.1 F.3", "wf.2 g j0.0 g0", "j1.2 t.0 g1 T", "S t.1 s0 wf.2",
            "j1.1 t.2 j1.3 t.3", "s1 R r0 p.2", "j0.1 G.0 e1.0 G.1", "wl.0 e1.1 G.2 r1",
            "L G.3 e1.2 y.0", "e1.3 X y.1",
        )
        return " ".join(steps)
    forward = ["P", *(f"a{b}" for b in range(1, halves)), "F"]
    backward = ["G", *(f"e{b}" for b in range(1, spot_bits))]
    waves = [
        [f"{chain[wave - k]}.{k}" for wave in range(len(chain) + CHUNKS) for k in range(CHUNKS) if 0 <= wave - k < len(chain)]
        for chain in (forward, backward)
    ]
    gather = []
    for group in sorted({tuple(gathered_with(k)) for k in range(CHUNKS)}):
        gather += [f"j{b}.{k}" for k in group for b in range(halves - 2, 0, -1)]
        gather.append(f"j0.{group[0]}" if len(group) == 1 else f"p.{group[0]}")
    middle = gather + [f"t.{k}" for k in range(CHUNKS)] + ["T", "g", *(f"g{b}" for b in range(spot_bits)), "S", "s0", "s1", "R"]
    middle += [*(f"r{b}" for b in range(spot_bits)), "L"]
    return " ".join(["C"] + waves[0] + middle + waves[1] + ["X", "Y"])


def solution(mesh):
    in_specs = (P("cent", "spot"), P("cent", None), P(None, "spot"), P("cent"), P("spot"))
    out_specs = (P(), P("cent", "spot"), P("cent", "spot"), P("cent", "spot"))
    return jax.shard_map(
        on_device, mesh=mesh, in_specs=in_specs, out_specs=out_specs, check_vma=False
    )
```

```python
import functools

import jax
import jax.numpy as jnp
from jax import lax
from jax.experimental import pallas as pl
from jax.experimental.pallas import tpu as pltpu
from jax.sharding import PartitionSpec as P

EPS = 1e-06
F32 = jnp.float32
BF16 = jnp.bfloat16
LANES = 128
CHUNKS = 4
TILE_P = 512
TILE_G = 2560
PART_G = 640
TILE_X = 512
TILE_Y = 512
COST = pl.CostEstimate(flops=1, transcendentals=0, bytes_accessed=1)


def params(mebibytes):
    return pltpu.CompilerParams(vmem_limit_bytes=mebibytes << 20)


def shape(dims, dtype):
    return jax.ShapeDtypeStruct(dims, dtype)


def in_hbm(value):
    return pltpu.with_memory_space_constraint(value, pltpu.HBM)


def bits_of(count):
    return count.bit_length() - 1


def reversed_bits(value, bits):
    return sum(((value >> b) & 1) << (bits - 1 - b) for b in range(bits))


def bit_order(chunk, bits):
    return (1, 0, *range(2, bits)) if chunk == 1 and bits > 2 else tuple(range(bits))


def gathered_with(chunk):
    last = [CHUNKS - 2, CHUNKS - 1]
    return last if chunk in last else [chunk]


def place_among(device, order):
    return sum(((device >> bit) & 1) << at for at, bit in enumerate(order))


def exchange(value, axis, bits):
    return lax.ppermute(value, axis, [(i, i ^ bits) for i in range(lax.axis_size(axis))])


def swap(value, axis, bit):
    return exchange(value, axis, 1 << bit)


def sum_over(value, axis):
    for bit in range(bits_of(lax.axis_size(axis))):
        value = value + swap(value, axis, bit)
    return value


def tile_lanes(column, width):
    return jnp.concatenate([column] * (width // LANES), axis=1)


def column_of(row, length):
    return jnp.transpose(jnp.broadcast_to(row, (LANES, length)))


class Order:
    def __init__(self):
        self.last = ()

    def wait(self, value):
        self.last += tuple(value) if isinstance(value, list) else (value,)

    def run(self, step, first, *others):
        if self.last:
            first = lax.optimization_barrier((first, *self.last))[0]
        results = step(first, *others)
        self.last = (results[-1],)
        return results


def column_stats(index, logits, sizes, tile):
    rows, spots = logits.shape

    def kernel(index_ref, logit_ref, size_ref, sums_ref, column_ref, acc):
        step = pl.program_id(0)
        expo = jnp.exp(logit_ref[...])
        part = size_ref[pl.ds(pl.multiple_of(step * tile, LANES), tile)]
        column = column_of(part.astype(F32).reshape(1, tile), tile)
        column_ref[...] = column
        mass = expo * tile_lanes(column, spots)
        total = expo.reshape(tile // 8, 8, spots).sum(0)
        mass = mass.reshape(tile // 8, 8, spots).sum(0)

        @pl.when(step == 0)
        def _():
            acc[0] = total
            acc[1] = mass

        @pl.when(step > 0)
        def _():
            acc[0] += total
            acc[1] += mass

        @pl.when(step == pl.num_programs(0) - 1)
        def _():
            sums_ref[0:1, :] = acc[0].sum(0, keepdims=True)
            sums_ref[1:2, :] = acc[1].sum(0, keepdims=True)

    return pl.pallas_call(
        kernel,
        grid_spec=pltpu.PrefetchScalarGridSpec(
            num_scalar_prefetch=1,
            grid=(rows // tile,),
            in_specs=[
                pl.BlockSpec((tile, spots), lambda i, s: (i, 0)),
                pl.BlockSpec((rows,), lambda i, s: (0,)),
            ],
            out_specs=[
                pl.BlockSpec((2, spots), lambda i, s: (0, 0)),
                pl.BlockSpec((tile, LANES), lambda i, s: (i, 0)),
            ],
            scratch_shapes=[pltpu.VMEM((2, 8, spots), F32)],
        ),
        out_shape=[shape((2, spots), F32), shape((rows, LANES), F32)],
        cost_estimate=COST,
        compiler_params=params(20),
        name="column_stats",
    )(index, in_hbm(logits), in_hbm(sizes))


def predict(index, chunk, parts, expr, weights, first=None, turned_before=None):
    rows = first[0].shape[0] if first is not None else weights.shape[0]
    spots = (weights if first is None else first[0]).shape[1]
    genes = expr.shape[1]
    per_device = genes // parts
    size = per_device // CHUNKS
    width = parts * size
    starts = [d * per_device + chunk * size for d in range(parts)]
    blocks = sorted({s // LANES for s in starts})
    shares = chunk + 1 < CHUNKS and sorted({(s + size) // LANES for s in starts}) == blocks
    shares = shares and turned_before is None
    tile = TILE_P
    order = bit_order(chunk, bits_of(parts))
    order_next = bit_order(chunk + 1, bits_of(parts))
    n_in = (1 if turned_before is not None else len(blocks)) + (1 if first is None else 3)

    def kernel(index_ref, *refs):
        inputs, rest = refs[:n_in], refs[n_in:]
        keep_ref, send_ref = rest[:2]
        turned = inputs[0] if turned_before is not None else rest[-1]
        turned_next = rest[2] if shares else None
        if first is None:
            weight_ref = inputs[-1]
        else:
            logit_ref, sums_ref, column_ref = inputs[-3:]
            weight_ref = rest[3 if shares else 2]

        if turned_before is None:

            @pl.when(pl.program_id(0) == 0)
            def _():
                for number, block in enumerate(blocks):
                    block_t = jnp.transpose(inputs[number][...])
                    for d, start in enumerate(starts):
                        if start // LANES == block:
                            at_row = start % LANES
                            at = place_among(d, order) * size
                            turned[at : at + size, :] = block_t[at_row : at_row + size]
                            if shares:
                                at = place_among(d, order_next) * size
                                turned_next[at : at + size, :] = block_t[at_row + size : at_row + 2 * size]

        if first is not None:
            scale = 1.0 / sums_ref[0:1, :]
            weight = jnp.exp(logit_ref[...]) * scale * tile_lanes(column_ref[...], tile)
            weight_ref[...] = weight.astype(BF16)
        out = jnp.dot(turned[...], weight_ref[...], preferred_element_type=F32)
        even = ((index_ref[0] >> order[0]) & 1) == 0
        for j in range(parts // 2):
            a = out[2 * j * size : (2 * j + 1) * size]
            b = out[(2 * j + 1) * size : (2 * j + 2) * size]
            keep_ref[j] = jnp.where(even, a, b)
            send_ref[j] = jnp.where(even, b, a).astype(BF16)

    half = pl.BlockSpec((parts // 2, size, tile), lambda i, s: (0, 0, i))
    columns = pl.BlockSpec((rows, tile), lambda i, s: (0, i))
    whole = pl.BlockSpec((width, rows), lambda i, s: (0, 0))
    if turned_before is None:
        in_specs = [
            pl.BlockSpec((rows, LANES), lambda i, s, b=b: (0, b), pipeline_mode=pl.Buffered(1)) for b in blocks
        ]
        operands = [in_hbm(expr)] * len(blocks)
    else:
        in_specs, operands = [whole], [turned_before]
    out_specs = [half, half]
    out_shapes = [shape((parts // 2, size, spots), F32), shape((parts // 2, size, spots), BF16)]
    if shares:
        out_specs.append(whole)
        out_shapes.append(shape((width, rows), BF16))
    if first is None:
        in_specs.append(columns)
        operands.append(weights)
    else:
        in_specs += [columns, pl.BlockSpec((2, tile), lambda i, s: (0, i)), pl.BlockSpec((rows, LANES), lambda i, s: (0, 0))]
        operands += [in_hbm(first[0]), *first[1:]]
        out_specs.append(columns)
        out_shapes.append(shape((rows, spots), BF16))
    return pl.pallas_call(
        kernel,
        grid_spec=pltpu.PrefetchScalarGridSpec(
            num_scalar_prefetch=1,
            grid=(spots // tile,),
            in_specs=in_specs,
            out_specs=out_specs,
            scratch_shapes=[pltpu.VMEM((width, rows), BF16)] if turned_before is None else [],
        ),
        out_shape=out_shapes,
        cost_estimate=COST,
        compiler_params=params(20 if first is None else 36),
        name="predict",
    )(index, *operands)


def add_and_halve(index, bit, keep, received):
    count, size, spots = keep.shape

    def kernel(index_ref, keep_ref, received_ref, keep_out, send_out):
        a = keep_ref[0] + received_ref[0].astype(F32)
        b = keep_ref[1] + received_ref[1].astype(F32)
        even = ((index_ref[0] >> bit) & 1) == 0
        keep_out[0] = jnp.where(even, a, b)
        send_out[0] = jnp.where(even, b, a).astype(BF16)

    pair = pl.BlockSpec((2, size, spots), lambda i, s: (i, 0, 0))
    one = pl.BlockSpec((1, size, spots), lambda i, s: (i, 0, 0))
    return pl.pallas_call(
        kernel,
        grid_spec=pltpu.PrefetchScalarGridSpec(
            num_scalar_prefetch=1, grid=(count // 2,), in_specs=[pair, pair], out_specs=[one, one]
        ),
        out_shape=[shape((count // 2, size, spots), F32), shape((count // 2, size, spots), BF16)],
        cost_estimate=COST,
        compiler_params=params(10),
        name="add_and_halve",
    )(index, keep, received)


def finish_rows(index, chunk, per_device, keep, received, target_rows, earlier):
    _, size, spots = keep.shape

    def kernel(index_ref, keep_ref, received_ref, target_ref, *refs):
        pred_ref, gene_ref, spot_ref, low_ref = refs[-4:]
        pred = keep_ref[0] + received_ref[0].astype(F32)
        target = target_ref[0].astype(F32)
        pred_ref[...] = pred
        low_ref[0] = pred.astype(BF16)
        for at, product in enumerate((pred * target, pred * pred, target * target)):
            by_gene = jnp.sum(product, axis=1, keepdims=True)
            by_gene = jnp.transpose(jnp.broadcast_to(by_gene, (size, LANES)))
            gene_ref[0, at : at + 1, :] = by_gene[0:1, :]
            by_spot = jnp.sum(product, axis=0, keepdims=True)
            if earlier is not None:
                by_spot = by_spot + refs[0][at : at + 1, :]
            spot_ref[at : at + 1, :] = by_spot

    one = pl.BlockSpec((1, size, spots), lambda i, s: (0, 0, 0))
    by_spot = pl.BlockSpec((3, spots), lambda i, s: (0, 0))
    whole = pl.BlockSpec(memory_space=pl.ANY)
    operands = [] if earlier is None else [earlier[2], in_hbm(earlier[0]), earlier[1]]
    return pl.pallas_call(
        kernel,
        grid_spec=pltpu.PrefetchScalarGridSpec(
            num_scalar_prefetch=1,
            grid=(1,),
            in_specs=[one, one, pl.BlockSpec((1, size, spots), lambda i, s: (s[0] * CHUNKS + chunk, 0, 0))]
            + [by_spot, whole, whole][: len(operands)],
            out_specs=[
                pl.BlockSpec((size, spots), lambda i, s: (chunk, 0)),
                pl.BlockSpec((1, 3, size), lambda i, s: (chunk, 0, 0)),
                by_spot,
                one,
            ],
        ),
        out_shape=[
            pltpu.HBM((per_device, spots), F32),
            shape((CHUNKS, 3, size), F32),
            shape((3, spots), F32),
            shape((1, size, spots), BF16),
        ],
        input_output_aliases={5: 0, 6: 1} if operands else {},
        cost_estimate=COST,
        compiler_params=params(10),
        name="finish_rows",
    )(index, keep, received, in_hbm(target_rows), *operands)


def row_of(*values):
    lane = lax.broadcasted_iota(jnp.int32, (1, LANES), 1)
    return sum(jnp.where(lane == at, value, 0.0) for at, value in enumerate(values))


def spot_totals(sums, counts):
    def kernel(sums_ref, counts_ref, out_ref):
        mass = sums_ref[1:2, :] / sums_ref[0:1, :]
        count = counts_ref[...]
        diverged = count * (jnp.log(count) - jnp.log(mass))
        out_ref[...] = row_of(jnp.sum(diverged), jnp.sum(mass), jnp.sum(count))

    return pl.pallas_call(
        kernel, out_shape=shape((1, LANES), F32), cost_estimate=COST, compiler_params=params(4), name="spot_totals"
    )(sums, counts)


def gene_slots(index, gene_sums, spot_sums, parts):
    chunks, _, size = gene_sums.shape
    spots = spot_sums.shape[1]
    genes = parts * chunks * size
    width = max(genes, spots)

    def kernel(index_ref, gene_ref, spot_ref, out_ref):
        out_ref[...] = jnp.zeros((8, width), F32)
        out_ref[3:6, 0:spots] = spot_ref[...]
        lane = lax.broadcasted_iota(jnp.int32, (1, parts * size), 1)
        mine = (lane >= index_ref[0] * size) & (lane < (index_ref[0] + 1) * size)
        for k in range(chunks):
            dot, pp, tt = (gene_ref[k, at : at + 1, :] for at in range(3))
            scale = lax.rsqrt(pp + EPS) * lax.rsqrt(tt + EPS)
            cosine = dot * scale
            for at, value in enumerate(((-1.0 / genes) * scale, (1.0 / genes) * cosine / (pp + EPS), cosine)):
                spread = jnp.concatenate([value] * parts, axis=1)
                out_ref[at : at + 1, k * parts * size : (k + 1) * parts * size] = jnp.where(mine, spread, 0.0)

    smem = pl.BlockSpec(memory_space=pltpu.SMEM)
    vmem = pl.BlockSpec(memory_space=pltpu.VMEM)
    return pl.pallas_call(
        kernel,
        in_specs=[smem, vmem, vmem],
        out_shape=shape((8, width), F32),
        cost_estimate=COST,
        compiler_params=params(4),
        name="gene_slots",
    )(index, gene_sums, spot_sums)


def gradient_terms(slots, totals, genes, spots, chunks, spots_all):
    def kernel(slots_ref, totals_ref, gene_ref, spot_ref, row_ref):
        for k in range(chunks):
            gene_ref[k] = slots_ref[0:2, k * (genes // chunks) : (k + 1) * (genes // chunks)]
        dot, pp, tt = (slots_ref[3 + at : 4 + at, 0:spots] for at in range(3))
        scale = lax.rsqrt(pp + EPS) * lax.rsqrt(tt + EPS)
        cosine = dot * scale
        spot_ref[0:1, :] = (-1.0 / spots_all) * scale
        spot_ref[1:2, :] = (1.0 / spots_all) * cosine / (pp + EPS)
        row_ref[...] = totals_ref[...] + row_of(0.0, 0.0, 0.0, jnp.sum(slots_ref[2:3, 0:genes]), jnp.sum(cosine))

    return pl.pallas_call(
        kernel,
        out_shape=[shape((chunks, 2, genes // chunks), F32), shape((2, spots), F32), shape((1, LANES), F32)],
        cost_estimate=COST,
        compiler_params=params(4),
        name="gradient_terms",
    )(slots, totals)


def loss_row(row, genes, spots_all, n_spot):
    def kernel(row_ref, out_ref):
        kl_sum, mass_total, count_total, gene_sum, spot_sum = (row_ref[0:1, at : at + 1] for at in range(5))
        gene_mean = gene_sum / (genes * n_spot)
        spot_mean = spot_sum / spots_all
        kl = kl_sum / count_total + jnp.log(mass_total) - jnp.log(count_total)
        out_ref[...] = row_of(kl - gene_mean - spot_mean, gene_mean, spot_mean, kl)

    return pl.pallas_call(
        kernel, out_shape=shape((1, LANES), F32), cost_estimate=COST, compiler_params=params(4), name="loss_row"
    )(row)


def join(*pieces):
    count, size, spots = pieces[0].shape

    def kernel(*refs):
        for at, ref in enumerate(refs[:-1]):
            refs[-1][at * count : (at + 1) * count] = ref[...]

    vmem = pl.BlockSpec(memory_space=pltpu.VMEM)
    return pl.pallas_call(
        kernel,
        in_specs=[vmem] * len(pieces),
        out_specs=vmem,
        out_shape=shape((len(pieces) * count, size, spots), BF16),
        cost_estimate=COST,
        compiler_params=params(4),
        name="join",
    )(*pieces)


def fetch(index, chunk, target):
    parts, _, size, spots = target.shape

    def kernel(index_ref, target_ref, out_ref):
        out_ref[...] = target_ref[:, 0]

    return pl.pallas_call(
        kernel,
        grid_spec=pltpu.PrefetchScalarGridSpec(
            num_scalar_prefetch=1,
            grid=(1,),
            in_specs=[pl.BlockSpec((parts, 1, size, spots), lambda i, s: (0, chunk, 0, 0))],
            out_specs=pl.BlockSpec((parts, size, spots), lambda i, s: (0, 0, 0)),
        ),
        out_shape=shape((parts, size, spots), BF16),
        cost_estimate=COST,
        compiler_params=params(8),
        name="fetch",
    )(index, in_hbm(target))


def gradients(index, chunk, n_spot, pred_near, pred_far, target, gene_rows, spot_rows, weights):
    parts, size, spots = target.shape
    rows = weights.shape[0]
    tile = TILE_G
    width = parts * size
    per_spot = parts // n_spot
    spot_bits = bits_of(n_spot)
    order = bit_order(chunk, bits_of(parts))

    def kernel(index_ref, near_ref, far_ref, target_ref, gene_ref, spot_ref, weight_ref, *refs):
        grad_ref, back_ref, keep_ref, *send_refs, turned, columns = refs

        @pl.when(pl.program_id(0) == 0)
        def _():
            columns[0] = column_of(gene_ref[0, 0:1, :], width)
            columns[1] = column_of(gene_ref[0, 1:2, :], width)
            back = jnp.zeros((1, spots), F32)
            for j in range(parts):
                d = index_ref[0] ^ j
                apart = reversed_bits((d // per_spot) ^ index_ref[1], spot_bits)
                place = apart * per_spot + d % per_spot
                at = pl.multiple_of(d * size, size)
                among = place_among(j, order[:0:-1])
                pred = (far_ref if (j >> order[0]) & 1 else near_ref)[0, among].astype(F32)
                by_target = tile_lanes(columns[0, pl.ds(at, size), :], spots) + spot_ref[0:1, :]
                by_pred = tile_lanes(columns[1, pl.ds(at, size), :], spots) + spot_ref[1:2, :]
                grad = (target_ref[d].astype(F32) * by_target + pred * by_pred).astype(BF16)
                grad_ref[d] = grad
                turned[pl.ds(pl.multiple_of(place * size, size), size), :] = grad
                back = back + jnp.sum(grad.astype(F32) * pred, axis=0, keepdims=True)
            back_ref[...] = back

        @pl.loop(0, tile, step=PART_G)
        def _(start):
            part = pl.ds(pl.multiple_of(start, PART_G), PART_G)
            out = lax.dot_general(weight_ref[part, :], turned[...], (((1,), (1,)), ((), ())), preferred_element_type=F32)
            keep_ref[part, :] = out[:, : width // 2]
            for column, send_ref in enumerate(send_refs):
                left = width // 2 + column * (width // 4)
                send_ref[part, :] = out[:, left : left + width // 4].astype(BF16)

    member = gathered_with(chunk).index(chunk)
    half = pl.BlockSpec((1, parts // 2, size, spots), lambda i, s: (member, 0, 0, 0))
    piece = pl.BlockSpec((tile, width // 2), lambda i, s: (i, 0))
    return pl.pallas_call(
        kernel,
        grid_spec=pltpu.PrefetchScalarGridSpec(
            num_scalar_prefetch=1,
            grid=(rows // tile,),
            in_specs=[
                half,
                half,
                pl.BlockSpec((parts, size, spots), lambda i, s: (0, 0, 0)),
                pl.BlockSpec((1, 2, width), lambda i, s: (chunk, 0, 0)),
                pl.BlockSpec((2, spots), lambda i, s: (0, 0)),
                pl.BlockSpec((tile, spots), lambda i, s: (i, 0)),
            ],
            out_specs=[
                pl.BlockSpec((parts, size, spots), lambda i, s: (0, 0, 0)),
                pl.BlockSpec((1, spots), lambda i, s: (0, 0)),
                piece,
            ]
            + [pl.BlockSpec((tile, width // 4), lambda i, s: (i, 0))] * 2,
            scratch_shapes=[pltpu.VMEM((width, spots), BF16), pltpu.VMEM((2, width, LANES), F32)],
        ),
        out_shape=[
            shape((parts, size, spots), BF16),
            shape((1, spots), F32),
            shape((rows, width // 2), F32),
        ]
        + [shape((rows, width // 4), BF16)] * 2,
        cost_estimate=COST,
        compiler_params=params(30),
        name="gradients",
    )(index, pred_near, pred_far, target, gene_rows, spot_rows, weights)


def add_columns(keep, *received):
    rows, width = keep.shape
    tile = rows // 2
    half = width // 2

    def kernel(keep_ref, *refs):
        received_refs, (keep_out, send_out) = refs[:-2], refs[-2:]
        if len(received) == 1:
            keep_out[...] = keep_ref[:, :half] + received_refs[0][:, :half].astype(F32)
            send_out[...] = (keep_ref[:, half:] + received_refs[0][:, half:].astype(F32)).astype(BF16)
        else:
            keep_out[...] = keep_ref[:, :half] + received_refs[0][...].astype(F32)
            send_out[...] = (keep_ref[:, half:] + received_refs[1][...].astype(F32)).astype(BF16)

    whole = pl.BlockSpec((tile, width), lambda i: (i, 0))
    out = pl.BlockSpec((tile, half), lambda i: (i, 0))
    return pl.pallas_call(
        kernel,
        grid=(rows // tile,),
        in_specs=[whole] + ([whole] if len(received) == 1 else [out] * 2),
        out_specs=[out, out],
        out_shape=[shape((rows, half), F32), shape((rows, half), BF16)],
        cost_estimate=COST,
        compiler_params=params(20),
        name="add_columns",
    )(keep, *received)


def assemble(kept, received, size):
    rows, width = kept[0].shape
    chunks = len(kept)
    tile = TILE_Y

    def kernel(*refs):
        out_ref = refs[-1]
        sums = [refs[k][...] + refs[chunks + k][...].astype(F32) for k in range(chunks)]
        pieces = [sums[k][:, d * size : (d + 1) * size] for d in range(width // size) for k in range(chunks)]
        out_ref[...] = jnp.concatenate(pieces, axis=1)

    spec = pl.BlockSpec((tile, width), lambda i: (i, 0))
    return pl.pallas_call(
        kernel,
        grid=(rows // tile,),
        in_specs=[spec] * (2 * chunks),
        out_specs=pl.BlockSpec((tile, width * chunks), lambda i: (i, 0)),
        out_shape=shape((rows, width * chunks), F32),
        cost_estimate=COST,
        compiler_params=params(24),
        name="assemble",
    )(*kept, *received)


def assemble_pair(pair, kept, received, size, before):
    rows, width = kept[0].shape
    tile = rows

    def kernel(*refs):
        out_ref = refs[-1]
        for d in range(width // size):

            @pl.when(pl.program_id(1) == d)
            def _():
                sums = [refs[k][...] + refs[2 + k][...].astype(F32) for k in range(2)]
                if width == LANES == 2 * size:
                    left, right = (sums[k] if d == k else pltpu.roll(sums[k], size, 1) for k in range(2))
                    lane = lax.broadcasted_iota(jnp.int32, (1, LANES), 1)
                    out_ref[...] = jnp.where(lane < size, left, right)
                else:
                    out_ref[...] = jnp.concatenate([v[:, d * size : (d + 1) * size] for v in sums], axis=1)

    spec = pl.BlockSpec(memory_space=pltpu.VMEM)
    others = [] if before is None else [before]
    return pl.pallas_call(
        kernel,
        grid=(rows // tile, width // size),
        in_specs=[spec] * 4 + [pl.BlockSpec(memory_space=pl.ANY)] * len(others),
        out_specs=pl.BlockSpec((tile, 2 * size), lambda i, d: (i, d * (CHUNKS // 2) + pair)),
        out_shape=pltpu.HBM((rows, width * CHUNKS), F32),
        input_output_aliases={4: 0} if others else {},
        cost_estimate=COST,
        compiler_params=params(24),
        name="assemble_pair",
    )(*kept, *received, *[in_hbm(v) for v in others])


def logit_gradient(sums, expr, grads, logits, size_column, counts, totals, backs):
    rows, genes = expr.shape
    parts, size, spots = grads[0].shape
    chunks = len(grads)
    tile = TILE_X

    def kernel(sums_ref, expr_ref, logit_ref, column_ref, counts_ref, totals_ref, *refs):
        grad_refs, back_refs, (out_ref, grad) = refs[:chunks], refs[chunks : 2 * chunks], refs[2 * chunks :]

        @pl.when(pl.program_id(0) == 0)
        def _():
            for k, ref in enumerate(grad_refs):
                for d in range(parts):
                    at = (d * chunks + k) * size
                    grad[at : at + size, :] = ref[d]

        inverse = 1.0 / sums_ref[0:1, :]
        mass = sums_ref[1:2, :] / sums_ref[0:1, :]
        mass_grad = 1.0 / totals_ref[0:1, 1:2] - counts_ref[...] / (totals_ref[0:1, 2:3] * mass)
        back = sum(ref[...] for ref in back_refs) + mass * mass_grad
        acc = jnp.dot(expr_ref[...], grad[...], preferred_element_type=F32)
        probs = jnp.exp(logit_ref[...]) * inverse
        out_ref[...] = probs * ((acc + mass_grad) * tile_lanes(column_ref[...], spots) - back)

    across = pl.BlockSpec((tile, spots), lambda i: (i, 0))
    row = pl.BlockSpec((1, spots), lambda i: (0, 0))
    vmem = pl.BlockSpec(memory_space=pltpu.VMEM)
    return pl.pallas_call(
        kernel,
        grid=(rows // tile,),
        in_specs=[
            pl.BlockSpec((2, spots), lambda i: (0, 0)),
            pl.BlockSpec((tile, genes), lambda i: (i, 0)),
            across,
            pl.BlockSpec((tile, LANES), lambda i: (i, 0)),
            row,
            pl.BlockSpec((1, LANES), lambda i: (0, 0)),
        ]
        + [vmem] * chunks
        + [row] * chunks,
        out_specs=across,
        out_shape=pltpu.HBM((rows, spots), F32),
        scratch_shapes=[pltpu.VMEM((genes, spots), BF16)],
        cost_estimate=COST,
        compiler_params=params(34),
        name="logit_gradient",
    )(sums, in_hbm(expr), in_hbm(logits), size_column, counts, totals, *grads, *backs)


def on_device(logits, centroid_expr, target, sizes, counts):
    parts = lax.axis_size("cent")
    halves = bits_of(parts)
    n_spot = lax.axis_size("spot")
    spot_bits = bits_of(n_spot)
    rows, genes = centroid_expr.shape
    spots = logits.shape[1]
    spots_all = spots * n_spot
    per_device = genes // parts
    size = per_device // CHUNKS
    counts_f = counts.astype(F32).reshape(1, spots)
    target_rows = target.reshape(parts * CHUNKS, size, spots)
    target_chunks = target.reshape(parts, CHUNKS, size, spots)
    order = Order()
    index = jnp.stack([lax.axis_index("cent"), lax.axis_index("spot")])

    made = {}
    keeps, arrived, nears, fars, fetched, grads, backs, kept, landed = ([None] * CHUNKS for _ in range(9))

    def stats_step():
        sums, made["column"] = order.run(lambda i, *a: column_stats(i, *a, rows // 4), index, logits, sizes)
        made["total"] = sum_over(sums, "cent")

    def predict_step(k):
        if k == 0:
            out = order.run(
                lambda i, e, *a: predict(i, 0, parts, e, None, a), index, centroid_expr, logits, made["total"], made["column"]
            )
            made["weights"] = out[-1]
        else:
            before = made.pop("turned", None)
            out = order.run(lambda i, e, w: predict(i, k, parts, e, w, None, before), index, centroid_expr, made["weights"])
        if len(out) > (3 if k == 0 else 2):
            made["turned"] = out[2]
        keeps[k] = out[0]
        arrived[k] = swap(out[1], "cent", bit_order(k, halves)[0])

    def halve_step(at):
        def step(k):
            b = bit_order(k, halves)[at]
            keeps[k], send = order.run(lambda i, *a: add_and_halve(i, b, *a), index, keeps[k], arrived[k])
            arrived[k] = swap(send, "cent", b)

        return step

    def finish_step(k):
        *made["rows"], low = order.run(
            lambda i, *a: finish_rows(i, k, per_device, *a), index, keeps[k], arrived[k], target_rows, made.get("rows")
        )
        nears[k], fars[k] = low, swap(low, "cent", bit_order(k, halves)[-1])

    def pair_up_step(k):
        pieces = [v[c] for c in gathered_with(k) for v in (nears, fars)]
        (nears[k],) = order.run(lambda *a: (join(*a),), *pieces)
        fars[k] = swap(nears[k], "cent", bit_order(k, halves)[0])

    def join_step(at):
        def step(k):
            (nears[k],) = order.run(lambda *a: (join(*a),), nears[k], fars[k])
            fars[k] = swap(nears[k], "cent", bit_order(k, halves)[at])

        return step

    def totals_step():
        (made["totals"],) = order.run(lambda *a: (spot_totals(*a),), made["total"], counts_f)

    def genes_step():
        made["sums"] = made["rows"][1]
        made["hop"] = swap(made["sums"], "spot", 0)

    def genes_hop(b):
        def step():
            (made["sums"],) = order.run(lambda *a: (a[0] + a[1],), made["sums"], made["hop"])
            if b + 1 < spot_bits:
                made["hop"] = swap(made["sums"], "spot", b + 1)

        return step

    def slots_step():
        (made["slots"],) = order.run(lambda *a: (gene_slots(*a, parts),), index, made["sums"], made["rows"][2])
        made["hop"] = [swap(made["slots"], "cent", 0)]

    def slots_hop(last):
        def step():
            (made["slots"],) = order.run(lambda *a: (sum(a),), made["slots"], *made["hop"])
            if not last:
                made["hop"] = [exchange(made["slots"], "cent", 2 * j) for j in range(1, parts // 2)]

        return step

    def terms_step():
        made["genes"], made["terms"], made["row"] = order.run(
            lambda *a: gradient_terms(*a, genes, spots, CHUNKS, spots_all), made["slots"], made["totals"]
        )
        made["row_hop"] = swap(made["row"], "spot", 0)

    def row_hop(b):
        def step():
            (made["row"],) = order.run(lambda *a: (a[0] + a[1],), made["row"], made["row_hop"])
            if b + 1 < spot_bits:
                made["row_hop"] = swap(made["row"], "spot", b + 1)

        return step

    def losses_step():
        (row,) = order.run(lambda *a: (loss_row(*a, genes, spots_all, n_spot),), made["row"])
        (made["losses"],) = order.run(lambda a: (a[0, :4],), row)

    def fetch_step(k):
        (fetched[k],) = order.run(lambda i, t: (fetch(i, k, t),), index, target_chunks)

    def gradients_step(k):
        first, *_ = group = gathered_with(k)
        near, far = (v[first].reshape(len(group), parts // 2, size, spots) for v in (nears, fars))
        operands = (near, far, fetched[k], made["genes"], made["terms"], made["weights"])
        grads[k], backs[k], kept[k], *sends = order.run(lambda i, *a: gradients(i, k, n_spot, *a), index, *operands)
        landed[k] = [swap(send, "spot", 0) for send in sends]

    def columns_step(b):
        def step(k):
            kept[k], send = order.run(add_columns, kept[k], *landed[k])
            landed[k] = [swap(send, "spot", b)]

        return step

    def logits_step():
        (made["logit_grad"],) = order.run(
            lambda t, e, *a: (logit_gradient(t, e, grads, *a, backs),),
            *(made["total"], centroid_expr, logits, made["column"], counts_f, made["row"])
        )

    def centroids_step():
        (made["centroid_grad"],) = order.run(lambda *a: (assemble(a[:CHUNKS], a[CHUNKS:], size),), *kept, *sum(landed, []))

    def pair_step(pair):
        chunks = slice(2 * pair, 2 * pair + 2)
        before = made.get("centroid_grad")
        (made["centroid_grad"],) = order.run(
            lambda *a: (assemble_pair(pair, a[:2], a[2:], size, before),), *kept[chunks], *sum(landed[chunks], [])
        )

    def wait_for(values):
        return lambda k: order.wait(values[k])

    steps = {"C": stats_step, "P": predict_step, "F": finish_step, "T": totals_step, "g": genes_step}
    steps |= {"S": slots_step, "s0": slots_hop(False), "s1": slots_hop(True), "R": terms_step, "L": losses_step}
    steps |= {"p": pair_up_step, "t": fetch_step, "G": gradients_step, "X": logits_step, "Y": centroids_step, "y": pair_step}
    steps |= {"wa": wait_for(arrived), "wf": wait_for(fars), "wl": wait_for(landed)}
    steps |= {f"a{b}": halve_step(b) for b in range(1, halves)}
    steps |= {f"j{b}": join_step(b) for b in range(halves - 1)}
    steps |= {f"e{b}": columns_step(b) for b in range(1, spot_bits)}
    steps |= {f"g{b}": genes_hop(b) for b in range(spot_bits)}
    steps |= {f"r{b}": row_hop(b) for b in range(spot_bits)}
    for name in schedule(halves, spot_bits).split():
        step, _, k = name.partition(".")
        steps[step](*([int(k)] if k else []))
    return made["losses"], made["rows"][0], made["logit_grad"], made["centroid_grad"]


def schedule(halves, spot_bits):
    if (halves, spot_bits) == (3, 2):
        steps = (
            "C P.0 P.1 P.2", "a1.0 P.3 a1.1 t.0", "t.1 t.2 a2.0 a1.2", "t.3 wa.0 F.0 a1.3",
            "a2.2 j1.0 a2.1 F.2", "a2.3 wf.0 F.1 F.3", "wf.2 g j0.0 g0", "j1.2 g1 T S",
            "s0 wf.2 j1.1 j1.3", "s1 R r0 p.2", "j0.1 G.0 e1.0 G.1", "wl.0 e1.1 G.2 r1",
            "L G.3 e1.2 y.0", "e1.3 X y.1",
        )
        return " ".join(steps)
    forward = ["P", *(f"a{b}" for b in range(1, halves)), "F"]
    backward = ["G", *(f"e{b}" for b in range(1, spot_bits))]
    waves = [
        [f"{chain[wave - k]}.{k}" for wave in range(len(chain) + CHUNKS) for k in range(CHUNKS) if 0 <= wave - k < len(chain)]
        for chain in (forward, backward)
    ]
    gather = []
    for group in sorted({tuple(gathered_with(k)) for k in range(CHUNKS)}):
        gather += [f"j{b}.{k}" for k in group for b in range(halves - 2, 0, -1)]
        gather.append(f"j0.{group[0]}" if len(group) == 1 else f"p.{group[0]}")
    middle = gather + [f"t.{k}" for k in range(CHUNKS)] + ["T", "g", *(f"g{b}" for b in range(spot_bits)), "S", "s0", "s1", "R"]
    middle += [*(f"r{b}" for b in range(spot_bits)), "L"]
    return " ".join(["C"] + waves[0] + middle + waves[1] + ["X", "Y"])


def solution(mesh):
    in_specs = (P("cent", "spot"), P("cent", None), P(None, "spot"), P("cent"), P("spot"))
    out_specs = (P(), P("cent", "spot"), P("cent", "spot"), P("cent", "spot"))
    return jax.shard_map(
        on_device, mesh=mesh, in_specs=in_specs, out_specs=out_specs, check_vma=False
    )
```

```python
import functools

import jax
import jax.numpy as jnp
from jax import lax
from jax.experimental import pallas as pl
from jax.experimental.pallas import tpu as pltpu
from jax.sharding import PartitionSpec as P

EPS = 1e-06
F32 = jnp.float32
BF16 = jnp.bfloat16
LANES = 128
CHUNKS = 4
TILE_P = 512
TILE_G = 2560
PART_G = 640
TILE_X = 512
TILE_Y = 512
COST = pl.CostEstimate(flops=1, transcendentals=0, bytes_accessed=1)


def params(mebibytes):
    return pltpu.CompilerParams(vmem_limit_bytes=mebibytes << 20)


def shape(dims, dtype):
    return jax.ShapeDtypeStruct(dims, dtype)


def in_hbm(value):
    return pltpu.with_memory_space_constraint(value, pltpu.HBM)


def bits_of(count):
    return count.bit_length() - 1


def reversed_bits(value, bits):
    return sum(((value >> b) & 1) << (bits - 1 - b) for b in range(bits))


def bit_order(chunk, bits):
    return (1, 0, *range(2, bits)) if chunk == 1 and bits > 2 else tuple(range(bits))


def gathered_with(chunk):
    last = [CHUNKS - 2, CHUNKS - 1]
    return last if chunk in last else [chunk]


def place_among(device, order):
    return sum(((device >> bit) & 1) << at for at, bit in enumerate(order))


def exchange(value, axis, bits):
    return lax.ppermute(value, axis, [(i, i ^ bits) for i in range(lax.axis_size(axis))])


def swap(value, axis, bit):
    return exchange(value, axis, 1 << bit)


def sum_over(value, axis):
    for bit in range(bits_of(lax.axis_size(axis))):
        value = value + swap(value, axis, bit)
    return value


def tile_lanes(column, width):
    return jnp.concatenate([column] * (width // LANES), axis=1)


def column_of(row, length):
    return jnp.transpose(jnp.broadcast_to(row, (LANES, length)))


class Order:
    def __init__(self):
        self.last = ()

    def wait(self, value):
        self.last += tuple(value) if isinstance(value, list) else (value,)

    def run(self, step, first, *others):
        if self.last:
            first = lax.optimization_barrier((first, *self.last))[0]
        results = step(first, *others)
        self.last = (results[-1],)
        return results


def column_stats(index, logits, sizes, tile):
    rows, spots = logits.shape

    def kernel(index_ref, logit_ref, size_ref, sums_ref, column_ref, acc):
        step = pl.program_id(0)
        expo = jnp.exp(logit_ref[...])
        part = size_ref[pl.ds(pl.multiple_of(step * tile, LANES), tile)]
        column = column_of(part.astype(F32).reshape(1, tile), tile)
        column_ref[...] = column
        mass = expo * tile_lanes(column, spots)
        total = expo.reshape(tile // 8, 8, spots).sum(0)
        mass = mass.reshape(tile // 8, 8, spots).sum(0)

        @pl.when(step == 0)
        def _():
            acc[0] = total
            acc[1] = mass

        @pl.when(step > 0)
        def _():
            acc[0] += total
            acc[1] += mass

        @pl.when(step == pl.num_programs(0) - 1)
        def _():
            sums_ref[0:1, :] = acc[0].sum(0, keepdims=True)
            sums_ref[1:2, :] = acc[1].sum(0, keepdims=True)

    return pl.pallas_call(
        kernel,
        grid_spec=pltpu.PrefetchScalarGridSpec(
            num_scalar_prefetch=1,
            grid=(rows // tile,),
            in_specs=[
                pl.BlockSpec((tile, spots), lambda i, s: (i, 0)),
                pl.BlockSpec((rows,), lambda i, s: (0,)),
            ],
            out_specs=[
                pl.BlockSpec((2, spots), lambda i, s: (0, 0)),
                pl.BlockSpec((tile, LANES), lambda i, s: (i, 0)),
            ],
            scratch_shapes=[pltpu.VMEM((2, 8, spots), F32)],
        ),
        out_shape=[shape((2, spots), F32), shape((rows, LANES), F32)],
        cost_estimate=COST,
        compiler_params=params(20),
        name="column_stats",
    )(index, in_hbm(logits), in_hbm(sizes))


def predict(index, chunk, parts, expr, weights, first=None, turned_before=None):
    rows = first[0].shape[0] if first is not None else weights.shape[0]
    spots = (weights if first is None else first[0]).shape[1]
    genes = expr.shape[1]
    per_device = genes // parts
    size = per_device // CHUNKS
    width = parts * size
    starts = [d * per_device + chunk * size for d in range(parts)]
    blocks = sorted({s // LANES for s in starts})
    shares = chunk + 1 < CHUNKS and sorted({(s + size) // LANES for s in starts}) == blocks
    shares = shares and turned_before is None
    tile = TILE_P if first is not None else 768
    order = bit_order(chunk, bits_of(parts))
    order_next = bit_order(chunk + 1, bits_of(parts))
    n_in = (1 if turned_before is not None else len(blocks)) + (1 if first is None else 3)

    def kernel(index_ref, *refs):
        inputs, rest = refs[:n_in], refs[n_in:]
        keep_ref, send_ref = rest[:2]
        turned = inputs[0] if turned_before is not None else rest[-1]
        turned_next = rest[2] if shares else None
        if first is None:
            weight_ref = inputs[-1]
        else:
            logit_ref, sums_ref, column_ref = inputs[-3:]
            weight_ref = rest[3 if shares else 2]

        if turned_before is None:

            @pl.when(pl.program_id(0) == 0)
            def _():
                for number, block in enumerate(blocks):
                    block_t = jnp.transpose(inputs[number][...])
                    for d, start in enumerate(starts):
                        if start // LANES == block:
                            at_row = start % LANES
                            at = place_among(d, order) * size
                            turned[at : at + size, :] = block_t[at_row : at_row + size]
                            if shares:
                                at = place_among(d, order_next) * size
                                turned_next[at : at + size, :] = block_t[at_row + size : at_row + 2 * size]

        if first is not None:
            scale = 1.0 / sums_ref[0:1, :]
            weight = jnp.exp(logit_ref[...]) * scale * tile_lanes(column_ref[...], tile)
            weight_ref[...] = weight.astype(BF16)
        out = jnp.dot(turned[...], weight_ref[...], preferred_element_type=F32)
        even = ((index_ref[0] >> order[0]) & 1) == 0
        for j in range(parts // 2):
            a = out[2 * j * size : (2 * j + 1) * size]
            b = out[(2 * j + 1) * size : (2 * j + 2) * size]
            keep_ref[j] = jnp.where(even, a, b)
            send_ref[j] = jnp.where(even, b, a).astype(BF16)

    half = pl.BlockSpec((parts // 2, size, tile), lambda i, s: (0, 0, i))
    columns = pl.BlockSpec((rows, tile), lambda i, s: (0, i))
    whole = pl.BlockSpec((width, rows), lambda i, s: (0, 0))
    if turned_before is None:
        in_specs = [
            pl.BlockSpec((rows, LANES), lambda i, s, b=b: (0, b), pipeline_mode=pl.Buffered(1)) for b in blocks
        ]
        operands = [in_hbm(expr)] * len(blocks)
    else:
        in_specs, operands = [whole], [turned_before]
    out_specs = [half, half]
    out_shapes = [shape((parts // 2, size, spots), F32), shape((parts // 2, size, spots), BF16)]
    if shares:
        out_specs.append(whole)
        out_shapes.append(shape((width, rows), BF16))
    if first is None:
        in_specs.append(columns)
        operands.append(weights)
    else:
        in_specs += [columns, pl.BlockSpec((2, tile), lambda i, s: (0, i)), pl.BlockSpec((rows, LANES), lambda i, s: (0, 0))]
        operands += [in_hbm(first[0]), *first[1:]]
        out_specs.append(columns)
        out_shapes.append(shape((rows, spots), BF16))
    return pl.pallas_call(
        kernel,
        grid_spec=pltpu.PrefetchScalarGridSpec(
            num_scalar_prefetch=1,
            grid=(spots // tile,),
            in_specs=in_specs,
            out_specs=out_specs,
            scratch_shapes=[pltpu.VMEM((width, rows), BF16)] if turned_before is None else [],
        ),
        out_shape=out_shapes,
        cost_estimate=COST,
        compiler_params=params(28 if first is None else 36),
        name="predict",
    )(index, *operands)


def add_and_halve(index, bit, keep, received):
    count, size, spots = keep.shape

    def kernel(index_ref, keep_ref, received_ref, keep_out, send_out):
        a = keep_ref[0] + received_ref[0].astype(F32)
        b = keep_ref[1] + received_ref[1].astype(F32)
        even = ((index_ref[0] >> bit) & 1) == 0
        keep_out[0] = jnp.where(even, a, b)
        send_out[0] = jnp.where(even, b, a).astype(BF16)

    pair = pl.BlockSpec((2, size, spots), lambda i, s: (i, 0, 0))
    one = pl.BlockSpec((1, size, spots), lambda i, s: (i, 0, 0))
    return pl.pallas_call(
        kernel,
        grid_spec=pltpu.PrefetchScalarGridSpec(
            num_scalar_prefetch=1, grid=(count // 2,), in_specs=[pair, pair], out_specs=[one, one]
        ),
        out_shape=[shape((count // 2, size, spots), F32), shape((count // 2, size, spots), BF16)],
        cost_estimate=COST,
        compiler_params=params(10),
        name="add_and_halve",
    )(index, keep, received)


def finish_rows(index, chunk, per_device, keep, received, target_rows, earlier):
    _, size, spots = keep.shape

    def kernel(index_ref, keep_ref, received_ref, target_ref, *refs):
        pred_ref, gene_ref, spot_ref, low_ref = refs[-4:]
        pred = keep_ref[0] + received_ref[0].astype(F32)
        target = target_ref[0].astype(F32)
        pred_ref[...] = pred
        low_ref[0] = pred.astype(BF16)
        for at, product in enumerate((pred * target, pred * pred, target * target)):
            by_gene = jnp.sum(product, axis=1, keepdims=True)
            by_gene = jnp.transpose(jnp.broadcast_to(by_gene, (size, LANES)))
            gene_ref[0, at : at + 1, :] = by_gene[0:1, :]
            by_spot = jnp.sum(product, axis=0, keepdims=True)
            if earlier is not None:
                by_spot = by_spot + refs[0][at : at + 1, :]
            spot_ref[at : at + 1, :] = by_spot

    one = pl.BlockSpec((1, size, spots), lambda i, s: (0, 0, 0))
    by_spot = pl.BlockSpec((3, spots), lambda i, s: (0, 0))
    whole = pl.BlockSpec(memory_space=pl.ANY)
    operands = [] if earlier is None else [earlier[2], in_hbm(earlier[0]), earlier[1]]
    return pl.pallas_call(
        kernel,
        grid_spec=pltpu.PrefetchScalarGridSpec(
            num_scalar_prefetch=1,
            grid=(1,),
            in_specs=[one, one, pl.BlockSpec((1, size, spots), lambda i, s: (s[0] * CHUNKS + chunk, 0, 0))]
            + [by_spot, whole, whole][: len(operands)],
            out_specs=[
                pl.BlockSpec((size, spots), lambda i, s: (chunk, 0)),
                pl.BlockSpec((1, 3, size), lambda i, s: (chunk, 0, 0)),
                by_spot,
                one,
            ],
        ),
        out_shape=[
            pltpu.HBM((per_device, spots), F32),
            shape((CHUNKS, 3, size), F32),
            shape((3, spots), F32),
            shape((1, size, spots), BF16),
        ],
        input_output_aliases={5: 0, 6: 1} if operands else {},
        cost_estimate=COST,
        compiler_params=params(10),
        name="finish_rows",
    )(index, keep, received, in_hbm(target_rows), *operands)


def row_of(*values):
    lane = lax.broadcasted_iota(jnp.int32, (1, LANES), 1)
    return sum(jnp.where(lane == at, value, 0.0) for at, value in enumerate(values))


def spot_totals(sums, counts):
    def kernel(sums_ref, counts_ref, out_ref):
        mass = sums_ref[1:2, :] / sums_ref[0:1, :]
        count = counts_ref[...]
        diverged = count * (jnp.log(count) - jnp.log(mass))
        out_ref[...] = row_of(jnp.sum(diverged), jnp.sum(mass), jnp.sum(count))

    return pl.pallas_call(
        kernel, out_shape=shape((1, LANES), F32), cost_estimate=COST, compiler_params=params(4), name="spot_totals"
    )(sums, counts)


def gene_slots(index, gene_sums, spot_sums, parts):
    chunks, _, size = gene_sums.shape
    spots = spot_sums.shape[1]
    genes = parts * chunks * size
    width = max(genes, spots)

    def kernel(index_ref, gene_ref, spot_ref, out_ref):
        out_ref[...] = jnp.zeros((8, width), F32)
        out_ref[3:6, 0:spots] = spot_ref[...]
        lane = lax.broadcasted_iota(jnp.int32, (1, parts * size), 1)
        mine = (lane >= index_ref[0] * size) & (lane < (index_ref[0] + 1) * size)
        for k in range(chunks):
            dot, pp, tt = (gene_ref[k, at : at + 1, :] for at in range(3))
            scale = lax.rsqrt(pp + EPS) * lax.rsqrt(tt + EPS)
            cosine = dot * scale
            for at, value in enumerate(((-1.0 / genes) * scale, (1.0 / genes) * cosine / (pp + EPS), cosine)):
                spread = jnp.concatenate([value] * parts, axis=1)
                out_ref[at : at + 1, k * parts * size : (k + 1) * parts * size] = jnp.where(mine, spread, 0.0)

    smem = pl.BlockSpec(memory_space=pltpu.SMEM)
    vmem = pl.BlockSpec(memory_space=pltpu.VMEM)
    return pl.pallas_call(
        kernel,
        in_specs=[smem, vmem, vmem],
        out_shape=shape((8, width), F32),
        cost_estimate=COST,
        compiler_params=params(4),
        name="gene_slots",
    )(index, gene_sums, spot_sums)


def gradient_terms(slots, totals, genes, spots, chunks, spots_all):
    def kernel(slots_ref, totals_ref, gene_ref, spot_ref, row_ref):
        for k in range(chunks):
            gene_ref[k] = slots_ref[0:2, k * (genes // chunks) : (k + 1) * (genes // chunks)]
        dot, pp, tt = (slots_ref[3 + at : 4 + at, 0:spots] for at in range(3))
        scale = lax.rsqrt(pp + EPS) * lax.rsqrt(tt + EPS)
        cosine = dot * scale
        spot_ref[0:1, :] = (-1.0 / spots_all) * scale
        spot_ref[1:2, :] = (1.0 / spots_all) * cosine / (pp + EPS)
        row_ref[...] = totals_ref[...] + row_of(0.0, 0.0, 0.0, jnp.sum(slots_ref[2:3, 0:genes]), jnp.sum(cosine))

    return pl.pallas_call(
        kernel,
        out_shape=[shape((chunks, 2, genes // chunks), F32), shape((2, spots), F32), shape((1, LANES), F32)],
        cost_estimate=COST,
        compiler_params=params(4),
        name="gradient_terms",
    )(slots, totals)


def loss_row(row, genes, spots_all, n_spot):
    def kernel(row_ref, out_ref):
        kl_sum, mass_total, count_total, gene_sum, spot_sum = (row_ref[0:1, at : at + 1] for at in range(5))
        gene_mean = gene_sum / (genes * n_spot)
        spot_mean = spot_sum / spots_all
        kl = kl_sum / count_total + jnp.log(mass_total) - jnp.log(count_total)
        out_ref[...] = row_of(kl - gene_mean - spot_mean, gene_mean, spot_mean, kl)

    return pl.pallas_call(
        kernel, out_shape=shape((1, LANES), F32), cost_estimate=COST, compiler_params=params(4), name="loss_row"
    )(row)


def join(*pieces):
    count, size, spots = pieces[0].shape

    def kernel(*refs):
        for at, ref in enumerate(refs[:-1]):
            refs[-1][at * count : (at + 1) * count] = ref[...]

    vmem = pl.BlockSpec(memory_space=pltpu.VMEM)
    return pl.pallas_call(
        kernel,
        in_specs=[vmem] * len(pieces),
        out_specs=vmem,
        out_shape=shape((len(pieces) * count, size, spots), BF16),
        cost_estimate=COST,
        compiler_params=params(4),
        name="join",
    )(*pieces)


def fetch(index, chunk, target):
    parts, _, size, spots = target.shape

    def kernel(index_ref, target_ref, out_ref):
        out_ref[...] = target_ref[:, 0]

    return pl.pallas_call(
        kernel,
        grid_spec=pltpu.PrefetchScalarGridSpec(
            num_scalar_prefetch=1,
            grid=(1,),
            in_specs=[pl.BlockSpec((parts, 1, size, spots), lambda i, s: (0, chunk, 0, 0))],
            out_specs=pl.BlockSpec((parts, size, spots), lambda i, s: (0, 0, 0)),
        ),
        out_shape=shape((parts, size, spots), BF16),
        cost_estimate=COST,
        compiler_params=params(8),
        name="fetch",
    )(index, in_hbm(target))


def gradients(index, chunk, n_spot, pred_near, pred_far, target, gene_rows, spot_rows, weights):
    parts, size, spots = target.shape
    rows = weights.shape[0]
    tile = TILE_G
    width = parts * size
    per_spot = parts // n_spot
    spot_bits = bits_of(n_spot)
    order = bit_order(chunk, bits_of(parts))

    def kernel(index_ref, near_ref, far_ref, target_ref, gene_ref, spot_ref, weight_ref, *refs):
        grad_ref, back_ref, keep_ref, *send_refs, turned, columns = refs

        @pl.when(pl.program_id(0) == 0)
        def _():
            columns[0] = column_of(gene_ref[0, 0:1, :], width)
            columns[1] = column_of(gene_ref[0, 1:2, :], width)
            back = jnp.zeros((1, spots), F32)
            for j in range(parts):
                d = index_ref[0] ^ j
                apart = reversed_bits((d // per_spot) ^ index_ref[1], spot_bits)
                place = apart * per_spot + d % per_spot
                at = pl.multiple_of(d * size, size)
                among = place_among(j, order[:0:-1])
                pred = (far_ref if (j >> order[0]) & 1 else near_ref)[0, among].astype(F32)
                by_target = tile_lanes(columns[0, pl.ds(at, size), :], spots) + spot_ref[0:1, :]
                by_pred = tile_lanes(columns[1, pl.ds(at, size), :], spots) + spot_ref[1:2, :]
                grad = (target_ref[d].astype(F32) * by_target + pred * by_pred).astype(BF16)
                grad_ref[d] = grad
                turned[pl.ds(pl.multiple_of(place * size, size), size), :] = grad
                back = back + jnp.sum(grad.astype(F32) * pred, axis=0, keepdims=True)
            back_ref[...] = back

        @pl.loop(0, tile, step=PART_G)
        def _(start):
            part = pl.ds(pl.multiple_of(start, PART_G), PART_G)
            out = lax.dot_general(weight_ref[part, :], turned[...], (((1,), (1,)), ((), ())), preferred_element_type=F32)
            keep_ref[part, :] = out[:, : width // 2]
            for column, send_ref in enumerate(send_refs):
                left = width // 2 + column * (width // 4)
                send_ref[part, :] = out[:, left : left + width // 4].astype(BF16)

    member = gathered_with(chunk).index(chunk)
    half = pl.BlockSpec((1, parts // 2, size, spots), lambda i, s: (member, 0, 0, 0))
    piece = pl.BlockSpec((tile, width // 2), lambda i, s: (i, 0))
    return pl.pallas_call(
        kernel,
        grid_spec=pltpu.PrefetchScalarGridSpec(
            num_scalar_prefetch=1,
            grid=(rows // tile,),
            in_specs=[
                half,
                half,
                pl.BlockSpec((parts, size, spots), lambda i, s: (0, 0, 0)),
                pl.BlockSpec((1, 2, width), lambda i, s: (chunk, 0, 0)),
                pl.BlockSpec((2, spots), lambda i, s: (0, 0)),
                pl.BlockSpec((tile, spots), lambda i, s: (i, 0)),
            ],
            out_specs=[
                pl.BlockSpec((parts, size, spots), lambda i, s: (0, 0, 0)),
                pl.BlockSpec((1, spots), lambda i, s: (0, 0)),
                piece,
            ]
            + [pl.BlockSpec((tile, width // 4), lambda i, s: (i, 0))] * 2,
            scratch_shapes=[pltpu.VMEM((width, spots), BF16), pltpu.VMEM((2, width, LANES), F32)],
        ),
        out_shape=[
            shape((parts, size, spots), BF16),
            shape((1, spots), F32),
            shape((rows, width // 2), F32),
        ]
        + [shape((rows, width // 4), BF16)] * 2,
        cost_estimate=COST,
        compiler_params=params(30),
        name="gradients",
    )(index, pred_near, pred_far, target, gene_rows, spot_rows, weights)


def add_columns(keep, *received):
    rows, width = keep.shape
    tile = rows // 2
    half = width // 2

    def kernel(keep_ref, *refs):
        received_refs, (keep_out, send_out) = refs[:-2], refs[-2:]
        if len(received) == 1:
            keep_out[...] = keep_ref[:, :half] + received_refs[0][:, :half].astype(F32)
            send_out[...] = (keep_ref[:, half:] + received_refs[0][:, half:].astype(F32)).astype(BF16)
        else:
            keep_out[...] = keep_ref[:, :half] + received_refs[0][...].astype(F32)
            send_out[...] = (keep_ref[:, half:] + received_refs[1][...].astype(F32)).astype(BF16)

    whole = pl.BlockSpec((tile, width), lambda i: (i, 0))
    out = pl.BlockSpec((tile, half), lambda i: (i, 0))
    return pl.pallas_call(
        kernel,
        grid=(rows // tile,),
        in_specs=[whole] + ([whole] if len(received) == 1 else [out] * 2),
        out_specs=[out, out],
        out_shape=[shape((rows, half), F32), shape((rows, half), BF16)],
        cost_estimate=COST,
        compiler_params=params(20),
        name="add_columns",
    )(keep, *received)


def assemble(kept, received, size):
    rows, width = kept[0].shape
    chunks = len(kept)
    tile = TILE_Y

    def kernel(*refs):
        out_ref = refs[-1]
        sums = [refs[k][...] + refs[chunks + k][...].astype(F32) for k in range(chunks)]
        pieces = [sums[k][:, d * size : (d + 1) * size] for d in range(width // size) for k in range(chunks)]
        out_ref[...] = jnp.concatenate(pieces, axis=1)

    spec = pl.BlockSpec((tile, width), lambda i: (i, 0))
    return pl.pallas_call(
        kernel,
        grid=(rows // tile,),
        in_specs=[spec] * (2 * chunks),
        out_specs=pl.BlockSpec((tile, width * chunks), lambda i: (i, 0)),
        out_shape=shape((rows, width * chunks), F32),
        cost_estimate=COST,
        compiler_params=params(24),
        name="assemble",
    )(*kept, *received)


def assemble_pair(pair, kept, received, size, before):
    rows, width = kept[0].shape
    tile = rows

    def kernel(*refs):
        out_ref = refs[-1]
        for d in range(width // size):

            @pl.when(pl.program_id(1) == d)
            def _():
                sums = [refs[k][...] + refs[2 + k][...].astype(F32) for k in range(2)]
                if width == LANES == 2 * size:
                    left, right = (sums[k] if d == k else pltpu.roll(sums[k], size, 1) for k in range(2))
                    lane = lax.broadcasted_iota(jnp.int32, (1, LANES), 1)
                    out_ref[...] = jnp.where(lane < size, left, right)
                else:
                    out_ref[...] = jnp.concatenate([v[:, d * size : (d + 1) * size] for v in sums], axis=1)

    spec = pl.BlockSpec(memory_space=pltpu.VMEM)
    others = [] if before is None else [before]
    return pl.pallas_call(
        kernel,
        grid=(rows // tile, width // size),
        in_specs=[spec] * 4 + [pl.BlockSpec(memory_space=pl.ANY)] * len(others),
        out_specs=pl.BlockSpec((tile, 2 * size), lambda i, d: (i, d * (CHUNKS // 2) + pair)),
        out_shape=pltpu.HBM((rows, width * CHUNKS), F32),
        input_output_aliases={4: 0} if others else {},
        cost_estimate=COST,
        compiler_params=params(24),
        name="assemble_pair",
    )(*kept, *received, *[in_hbm(v) for v in others])


def logit_gradient(sums, expr, grads, logits, size_column, counts, totals, backs):
    rows, genes = expr.shape
    parts, size, spots = grads[0].shape
    chunks = len(grads)
    tile = TILE_X

    def kernel(sums_ref, expr_ref, logit_ref, column_ref, counts_ref, totals_ref, *refs):
        grad_refs, back_refs, (out_ref, grad) = refs[:chunks], refs[chunks : 2 * chunks], refs[2 * chunks :]

        @pl.when(pl.program_id(0) == 0)
        def _():
            for k, ref in enumerate(grad_refs):
                for d in range(parts):
                    at = (d * chunks + k) * size
                    grad[at : at + size, :] = ref[d]

        inverse = 1.0 / sums_ref[0:1, :]
        mass = sums_ref[1:2, :] / sums_ref[0:1, :]
        mass_grad = 1.0 / totals_ref[0:1, 1:2] - counts_ref[...] / (totals_ref[0:1, 2:3] * mass)
        back = sum(ref[...] for ref in back_refs) + mass * mass_grad
        acc = jnp.dot(expr_ref[...], grad[...], preferred_element_type=F32)
        probs = jnp.exp(logit_ref[...]) * inverse
        out_ref[...] = probs * ((acc + mass_grad) * tile_lanes(column_ref[...], spots) - back)

    across = pl.BlockSpec((tile, spots), lambda i: (i, 0))
    row = pl.BlockSpec((1, spots), lambda i: (0, 0))
    vmem = pl.BlockSpec(memory_space=pltpu.VMEM)
    return pl.pallas_call(
        kernel,
        grid=(rows // tile,),
        in_specs=[
            pl.BlockSpec((2, spots), lambda i: (0, 0)),
            pl.BlockSpec((tile, genes), lambda i: (i, 0)),
            across,
            pl.BlockSpec((tile, LANES), lambda i: (i, 0)),
            row,
            pl.BlockSpec((1, LANES), lambda i: (0, 0)),
        ]
        + [vmem] * chunks
        + [row] * chunks,
        out_specs=across,
        out_shape=pltpu.HBM((rows, spots), F32),
        scratch_shapes=[pltpu.VMEM((genes, spots), BF16)],
        cost_estimate=COST,
        compiler_params=params(34),
        name="logit_gradient",
    )(sums, in_hbm(expr), in_hbm(logits), size_column, counts, totals, *grads, *backs)


def on_device(logits, centroid_expr, target, sizes, counts):
    parts = lax.axis_size("cent")
    halves = bits_of(parts)
    n_spot = lax.axis_size("spot")
    spot_bits = bits_of(n_spot)
    rows, genes = centroid_expr.shape
    spots = logits.shape[1]
    spots_all = spots * n_spot
    per_device = genes // parts
    size = per_device // CHUNKS
    counts_f = counts.astype(F32).reshape(1, spots)
    target_rows = target.reshape(parts * CHUNKS, size, spots)
    target_chunks = target.reshape(parts, CHUNKS, size, spots)
    order = Order()
    index = jnp.stack([lax.axis_index("cent"), lax.axis_index("spot")])

    made = {}
    keeps, arrived, nears, fars, fetched, grads, backs, kept, landed = ([None] * CHUNKS for _ in range(9))

    def stats_step():
        sums, made["column"] = order.run(lambda i, *a: column_stats(i, *a, rows // 4), index, logits, sizes)
        made["total"] = sum_over(sums, "cent")

    def predict_step(k):
        if k == 0:
            out = order.run(
                lambda i, e, *a: predict(i, 0, parts, e, None, a), index, centroid_expr, logits, made["total"], made["column"]
            )
            made["weights"] = out[-1]
        else:
            before = made.pop("turned", None)
            out = order.run(lambda i, e, w: predict(i, k, parts, e, w, None, before), index, centroid_expr, made["weights"])
        if len(out) > (3 if k == 0 else 2):
            made["turned"] = out[2]
        keeps[k] = out[0]
        arrived[k] = swap(out[1], "cent", bit_order(k, halves)[0])

    def halve_step(at):
        def step(k):
            b = bit_order(k, halves)[at]
            keeps[k], send = order.run(lambda i, *a: add_and_halve(i, b, *a), index, keeps[k], arrived[k])
            arrived[k] = swap(send, "cent", b)

        return step

    def finish_step(k):
        *made["rows"], low = order.run(
            lambda i, *a: finish_rows(i, k, per_device, *a), index, keeps[k], arrived[k], target_rows, made.get("rows")
        )
        nears[k], fars[k] = low, swap(low, "cent", bit_order(k, halves)[-1])

    def pair_up_step(k):
        pieces = [v[c] for c in gathered_with(k) for v in (nears, fars)]
        (nears[k],) = order.run(lambda *a: (join(*a),), *pieces)
        fars[k] = swap(nears[k], "cent", bit_order(k, halves)[0])

    def join_step(at):
        def step(k):
            (nears[k],) = order.run(lambda *a: (join(*a),), nears[k], fars[k])
            fars[k] = swap(nears[k], "cent", bit_order(k, halves)[at])

        return step

    def totals_step():
        (made["totals"],) = order.run(lambda *a: (spot_totals(*a),), made["total"], counts_f)

    def genes_step():
        made["sums"] = made["rows"][1]
        made["hop"] = swap(made["sums"], "spot", 0)

    def genes_hop(b):
        def step():
            (made["sums"],) = order.run(lambda *a: (a[0] + a[1],), made["sums"], made["hop"])
            if b + 1 < spot_bits:
                made["hop"] = swap(made["sums"], "spot", b + 1)

        return step

    def slots_step():
        (made["slots"],) = order.run(lambda *a: (gene_slots(*a, parts),), index, made["sums"], made["rows"][2])
        made["hop"] = [swap(made["slots"], "cent", 0)]

    def slots_hop(last):
        def step():
            (made["slots"],) = order.run(lambda *a: (sum(a),), made["slots"], *made["hop"])
            if not last:
                made["hop"] = [exchange(made["slots"], "cent", 2 * j) for j in range(1, parts // 2)]

        return step

    def terms_step():
        made["genes"], made["terms"], made["row"] = order.run(
            lambda *a: gradient_terms(*a, genes, spots, CHUNKS, spots_all), made["slots"], made["totals"]
        )
        made["row_hop"] = swap(made["row"], "spot", 0)

    def row_hop(b):
        def step():
            (made["row"],) = order.run(lambda *a: (a[0] + a[1],), made["row"], made["row_hop"])
            if b + 1 < spot_bits:
                made["row_hop"] = swap(made["row"], "spot", b + 1)

        return step

    def losses_step():
        (row,) = order.run(lambda *a: (loss_row(*a, genes, spots_all, n_spot),), made["row"])
        (made["losses"],) = order.run(lambda a: (a[0, :4],), row)

    def fetch_step(k):
        (fetched[k],) = order.run(lambda i, t: (fetch(i, k, t),), index, target_chunks)

    def gradients_step(k):
        first, *_ = group = gathered_with(k)
        near, far = (v[first].reshape(len(group), parts // 2, size, spots) for v in (nears, fars))
        operands = (near, far, fetched[k], made["genes"], made["terms"], made["weights"])
        grads[k], backs[k], kept[k], *sends = order.run(lambda i, *a: gradients(i, k, n_spot, *a), index, *operands)
        landed[k] = [swap(send, "spot", 0) for send in sends]

    def columns_step(b):
        def step(k):
            kept[k], send = order.run(add_columns, kept[k], *landed[k])
            landed[k] = [swap(send, "spot", b)]

        return step

    def logits_step():
        (made["logit_grad"],) = order.run(
            lambda t, e, *a: (logit_gradient(t, e, grads, *a, backs),),
            *(made["total"], centroid_expr, logits, made["column"], counts_f, made["row"])
        )

    def centroids_step():
        (made["centroid_grad"],) = order.run(lambda *a: (assemble(a[:CHUNKS], a[CHUNKS:], size),), *kept, *sum(landed, []))

    def pair_step(pair):
        chunks = slice(2 * pair, 2 * pair + 2)
        before = made.get("centroid_grad")
        (made["centroid_grad"],) = order.run(
            lambda *a: (assemble_pair(pair, a[:2], a[2:], size, before),), *kept[chunks], *sum(landed[chunks], [])
        )

    def wait_for(values):
        return lambda k: order.wait(values[k])

    steps = {"C": stats_step, "P": predict_step, "F": finish_step, "T": totals_step, "g": genes_step}
    steps |= {"S": slots_step, "s0": slots_hop(False), "s1": slots_hop(True), "R": terms_step, "L": losses_step}
    steps |= {"p": pair_up_step, "t": fetch_step, "G": gradients_step, "X": logits_step, "Y": centroids_step, "y": pair_step}
    steps |= {"wa": wait_for(arrived), "wf": wait_for(fars), "wl": wait_for(landed)}
    steps |= {f"a{b}": halve_step(b) for b in range(1, halves)}
    steps |= {f"j{b}": join_step(b) for b in range(halves - 1)}
    steps |= {f"e{b}": columns_step(b) for b in range(1, spot_bits)}
    steps |= {f"g{b}": genes_hop(b) for b in range(spot_bits)}
    steps |= {f"r{b}": row_hop(b) for b in range(spot_bits)}
    for name in schedule(halves, spot_bits).split():
        step, _, k = name.partition(".")
        steps[step](*([int(k)] if k else []))
    return made["losses"], made["rows"][0], made["logit_grad"], made["centroid_grad"]


def schedule(halves, spot_bits):
    if (halves, spot_bits) == (3, 2):
        steps = (
            "C P.0 P.1 P.2", "a1.0 P.3 a1.1 t.0", "t.1 t.2 a2.0 a1.2", "t.3 wa.0 F.0 a1.3",
            "a2.2 j1.0 a2.1 F.2", "a2.3 wf.0 F.1 F.3", "wf.2 g j0.0 g0", "j1.2 g1 S T",
            "s0 wf.2 j1.1 j1.3", "s1 R r0 p.2", "j0.1 G.0 e1.0 G.1", "wl.0 e1.1 G.2 r1",
            "L G.3 e1.2 y.0", "e1.3 X y.1",
        )
        return " ".join(steps)
    forward = ["P", *(f"a{b}" for b in range(1, halves)), "F"]
    backward = ["G", *(f"e{b}" for b in range(1, spot_bits))]
    waves = [
        [f"{chain[wave - k]}.{k}" for wave in range(len(chain) + CHUNKS) for k in range(CHUNKS) if 0 <= wave - k < len(chain)]
        for chain in (forward, backward)
    ]
    gather = []
    for group in sorted({tuple(gathered_with(k)) for k in range(CHUNKS)}):
        gather += [f"j{b}.{k}" for k in group for b in range(halves - 2, 0, -1)]
        gather.append(f"j0.{group[0]}" if len(group) == 1 else f"p.{group[0]}")
    middle = gather + [f"t.{k}" for k in range(CHUNKS)] + ["T", "g", *(f"g{b}" for b in range(spot_bits)), "S", "s0", "s1", "R"]
    middle += [*(f"r{b}" for b in range(spot_bits)), "L"]
    return " ".join(["C"] + waves[0] + middle + waves[1] + ["X", "Y"])


def solution(mesh):
    in_specs = (P("cent", "spot"), P("cent", None), P(None, "spot"), P("cent"), P("spot"))
    out_specs = (P(), P("cent", "spot"), P("cent", "spot"), P("cent", "spot"))
    return jax.shard_map(
        on_device, mesh=mesh, in_specs=in_specs, out_specs=out_specs, check_vma=False
    )
```

```python
import functools

import jax
import jax.numpy as jnp
from jax import lax
from jax.experimental import pallas as pl
from jax.experimental.pallas import tpu as pltpu
from jax.sharding import PartitionSpec as P

EPS = 1e-06
F32 = jnp.float32
BF16 = jnp.bfloat16
LANES = 128
CHUNKS = 4
TILE_P = 512
TILE_G = 2560
PART_G = 640
TILE_X = 512
TILE_Y = 512
COST = pl.CostEstimate(flops=1, transcendentals=0, bytes_accessed=1)


def params(mebibytes):
    return pltpu.CompilerParams(vmem_limit_bytes=mebibytes << 20)


def shape(dims, dtype):
    return jax.ShapeDtypeStruct(dims, dtype)


def in_hbm(value):
    return pltpu.with_memory_space_constraint(value, pltpu.HBM)


def bits_of(count):
    return count.bit_length() - 1


def reversed_bits(value, bits):
    return sum(((value >> b) & 1) << (bits - 1 - b) for b in range(bits))


def bit_order(chunk, bits):
    return (1, 0, *range(2, bits)) if chunk == 1 and bits > 2 else tuple(range(bits))


def gathered_with(chunk):
    last = [CHUNKS - 2, CHUNKS - 1]
    return last if chunk in last else [chunk]


def place_among(device, order):
    return sum(((device >> bit) & 1) << at for at, bit in enumerate(order))


def exchange(value, axis, bits):
    return lax.ppermute(value, axis, [(i, i ^ bits) for i in range(lax.axis_size(axis))])


def swap(value, axis, bit):
    return exchange(value, axis, 1 << bit)


def sum_over(value, axis):
    for bit in range(bits_of(lax.axis_size(axis))):
        value = value + swap(value, axis, bit)
    return value


def tile_lanes(column, width):
    return jnp.concatenate([column] * (width // LANES), axis=1)


def column_of(row, length):
    return jnp.transpose(jnp.broadcast_to(row, (LANES, length)))


class Order:
    def __init__(self):
        self.last = ()

    def wait(self, value):
        self.last += tuple(value) if isinstance(value, list) else (value,)

    def run(self, step, first, *others):
        if self.last:
            first = lax.optimization_barrier((first, *self.last))[0]
        results = step(first, *others)
        self.last = (results[-1],)
        return results


def column_stats(index, logits, sizes, tile):
    rows, spots = logits.shape

    def kernel(index_ref, logit_ref, size_ref, sums_ref, column_ref, acc):
        step = pl.program_id(0)
        expo = jnp.exp(logit_ref[...])
        part = size_ref[pl.ds(pl.multiple_of(step * tile, LANES), tile)]
        column = column_of(part.astype(F32).reshape(1, tile), tile)
        column_ref[...] = column
        mass = expo * tile_lanes(column, spots)
        total = expo.reshape(tile // 8, 8, spots).sum(0)
        mass = mass.reshape(tile // 8, 8, spots).sum(0)

        @pl.when(step == 0)
        def _():
            acc[0] = total
            acc[1] = mass

        @pl.when(step > 0)
        def _():
            acc[0] += total
            acc[1] += mass

        @pl.when(step == pl.num_programs(0) - 1)
        def _():
            sums_ref[0:1, :] = acc[0].sum(0, keepdims=True)
            sums_ref[1:2, :] = acc[1].sum(0, keepdims=True)

    return pl.pallas_call(
        kernel,
        grid_spec=pltpu.PrefetchScalarGridSpec(
            num_scalar_prefetch=1,
            grid=(rows // tile,),
            in_specs=[
                pl.BlockSpec((tile, spots), lambda i, s: (i, 0)),
                pl.BlockSpec((rows,), lambda i, s: (0,)),
            ],
            out_specs=[
                pl.BlockSpec((2, spots), lambda i, s: (0, 0)),
                pl.BlockSpec((tile, LANES), lambda i, s: (i, 0)),
            ],
            scratch_shapes=[pltpu.VMEM((2, 8, spots), F32)],
        ),
        out_shape=[shape((2, spots), F32), shape((rows, LANES), F32)],
        cost_estimate=COST,
        compiler_params=params(20),
        name="column_stats",
    )(index, in_hbm(logits), in_hbm(sizes))


def predict(index, chunk, parts, expr, weights, first=None, turned_before=None):
    rows = first[0].shape[0] if first is not None else weights.shape[0]
    spots = (weights if first is None else first[0]).shape[1]
    genes = expr.shape[1]
    per_device = genes // parts
    size = per_device // CHUNKS
    width = parts * size
    starts = [d * per_device + chunk * size for d in range(parts)]
    blocks = sorted({s // LANES for s in starts})
    shares = chunk + 1 < CHUNKS and sorted({(s + size) // LANES for s in starts}) == blocks
    shares = shares and turned_before is None
    tile = TILE_P if first is not None else 768
    order = bit_order(chunk, bits_of(parts))
    order_next = bit_order(chunk + 1, bits_of(parts))
    n_in = (1 if turned_before is not None else len(blocks)) + (1 if first is None else 3)

    def kernel(index_ref, *refs):
        inputs, rest = refs[:n_in], refs[n_in:]
        keep_ref, send_ref = rest[:2]
        turned = inputs[0] if turned_before is not None else rest[-1]
        turned_next = rest[2] if shares else None
        if first is None:
            weight_ref = inputs[-1]
        else:
            logit_ref, sums_ref, column_ref = inputs[-3:]
            weight_ref = rest[3 if shares else 2]

        if turned_before is None:

            @pl.when(pl.program_id(0) == 0)
            def _():
                for number, block in enumerate(blocks):
                    block_t = jnp.transpose(inputs[number][...])
                    for d, start in enumerate(starts):
                        if start // LANES == block:
                            at_row = start % LANES
                            at = place_among(d, order) * size
                            turned[at : at + size, :] = block_t[at_row : at_row + size]
                            if shares:
                                at = place_among(d, order_next) * size
                                turned_next[at : at + size, :] = block_t[at_row + size : at_row + 2 * size]

        if first is not None:
            scale = 1.0 / sums_ref[0:1, :]
            weight = jnp.exp(logit_ref[...]) * scale * tile_lanes(column_ref[...], tile)
            weight_ref[...] = weight.astype(BF16)
        out = jnp.dot(turned[...], weight_ref[...], preferred_element_type=F32)
        even = ((index_ref[0] >> order[0]) & 1) == 0
        for j in range(parts // 2):
            a = out[2 * j * size : (2 * j + 1) * size]
            b = out[(2 * j + 1) * size : (2 * j + 2) * size]
            keep_ref[j] = jnp.where(even, a, b)
            send_ref[j] = jnp.where(even, b, a).astype(BF16)

    half = pl.BlockSpec((parts // 2, size, tile), lambda i, s: (0, 0, i))
    columns = pl.BlockSpec((rows, tile), lambda i, s: (0, i))
    whole = pl.BlockSpec((width, rows), lambda i, s: (0, 0))
    if turned_before is None:
        in_specs = [
            pl.BlockSpec((rows, LANES), lambda i, s, b=b: (0, b), pipeline_mode=pl.Buffered(1)) for b in blocks
        ]
        operands = [in_hbm(expr)] * len(blocks)
    else:
        in_specs, operands = [whole], [turned_before]
    out_specs = [half, half]
    out_shapes = [shape((parts // 2, size, spots), F32), shape((parts // 2, size, spots), BF16)]
    if shares:
        out_specs.append(whole)
        out_shapes.append(shape((width, rows), BF16))
    if first is None:
        in_specs.append(columns)
        operands.append(weights)
    else:
        in_specs += [columns, pl.BlockSpec((2, tile), lambda i, s: (0, i)), pl.BlockSpec((rows, LANES), lambda i, s: (0, 0))]
        operands += [in_hbm(first[0]), *first[1:]]
        out_specs.append(columns)
        out_shapes.append(shape((rows, spots), BF16))
    return pl.pallas_call(
        kernel,
        grid_spec=pltpu.PrefetchScalarGridSpec(
            num_scalar_prefetch=1,
            grid=(spots // tile,),
            in_specs=in_specs,
            out_specs=out_specs,
            scratch_shapes=[pltpu.VMEM((width, rows), BF16)] if turned_before is None else [],
        ),
        out_shape=out_shapes,
        cost_estimate=COST,
        compiler_params=params(28 if first is None else 36),
        name="predict",
    )(index, *operands)


def add_and_halve(index, bit, keep, received):
    count, size, spots = keep.shape

    def kernel(index_ref, keep_ref, received_ref, keep_out, send_out):
        a = keep_ref[0] + received_ref[0].astype(F32)
        b = keep_ref[1] + received_ref[1].astype(F32)
        even = ((index_ref[0] >> bit) & 1) == 0
        keep_out[0] = jnp.where(even, a, b)
        send_out[0] = jnp.where(even, b, a).astype(BF16)

    pair = pl.BlockSpec((2, size, spots), lambda i, s: (i, 0, 0))
    one = pl.BlockSpec((1, size, spots), lambda i, s: (i, 0, 0))
    return pl.pallas_call(
        kernel,
        grid_spec=pltpu.PrefetchScalarGridSpec(
            num_scalar_prefetch=1, grid=(count // 2,), in_specs=[pair, pair], out_specs=[one, one]
        ),
        out_shape=[shape((count // 2, size, spots), F32), shape((count // 2, size, spots), BF16)],
        cost_estimate=COST,
        compiler_params=params(10),
        name="add_and_halve",
    )(index, keep, received)


def finish_rows(index, chunk, per_device, keep, received, target_rows, earlier):
    _, size, spots = keep.shape

    def kernel(index_ref, keep_ref, received_ref, target_ref, *refs):
        pred_ref, gene_ref, spot_ref, low_ref = refs[-4:]
        pred = keep_ref[0] + received_ref[0].astype(F32)
        target = target_ref[0].astype(F32)
        pred_ref[...] = pred
        low_ref[0] = pred.astype(BF16)
        for at, product in enumerate((pred * target, pred * pred, target * target)):
            by_gene = jnp.sum(product, axis=1, keepdims=True)
            by_gene = jnp.transpose(jnp.broadcast_to(by_gene, (size, LANES)))
            gene_ref[0, at : at + 1, :] = by_gene[0:1, :]
            by_spot = jnp.sum(product, axis=0, keepdims=True)
            if earlier is not None:
                by_spot = by_spot + refs[0][at : at + 1, :]
            spot_ref[at : at + 1, :] = by_spot

    one = pl.BlockSpec((1, size, spots), lambda i, s: (0, 0, 0))
    by_spot = pl.BlockSpec((3, spots), lambda i, s: (0, 0))
    whole = pl.BlockSpec(memory_space=pl.ANY)
    operands = [] if earlier is None else [earlier[2], in_hbm(earlier[0]), earlier[1]]
    return pl.pallas_call(
        kernel,
        grid_spec=pltpu.PrefetchScalarGridSpec(
            num_scalar_prefetch=1,
            grid=(1,),
            in_specs=[one, one, pl.BlockSpec((1, size, spots), lambda i, s: (s[0] * CHUNKS + chunk, 0, 0))]
            + [by_spot, whole, whole][: len(operands)],
            out_specs=[
                pl.BlockSpec((size, spots), lambda i, s: (chunk, 0)),
                pl.BlockSpec((1, 3, size), lambda i, s: (chunk, 0, 0)),
                by_spot,
                one,
            ],
        ),
        out_shape=[
            pltpu.HBM((per_device, spots), F32),
            shape((CHUNKS, 3, size), F32),
            shape((3, spots), F32),
            shape((1, size, spots), BF16),
        ],
        input_output_aliases={5: 0, 6: 1} if operands else {},
        cost_estimate=COST,
        compiler_params=params(10),
        name="finish_rows",
    )(index, keep, received, in_hbm(target_rows), *operands)


def row_of(*values):
    lane = lax.broadcasted_iota(jnp.int32, (1, LANES), 1)
    return sum(jnp.where(lane == at, value, 0.0) for at, value in enumerate(values))


def spot_totals(sums, counts):
    def kernel(sums_ref, counts_ref, out_ref):
        mass = sums_ref[1:2, :] / sums_ref[0:1, :]
        count = counts_ref[...]
        diverged = count * (jnp.log(count) - jnp.log(mass))
        out_ref[...] = row_of(jnp.sum(diverged), jnp.sum(mass), jnp.sum(count))

    return pl.pallas_call(
        kernel, out_shape=shape((1, LANES), F32), cost_estimate=COST, compiler_params=params(4), name="spot_totals"
    )(sums, counts)


def gene_slots(index, gene_sums, spot_sums, parts):
    chunks, _, size = gene_sums.shape
    spots = spot_sums.shape[1]
    genes = parts * chunks * size
    width = max(genes, spots)

    def kernel(index_ref, gene_ref, spot_ref, out_ref):
        out_ref[...] = jnp.zeros((8, width), F32)
        out_ref[3:6, 0:spots] = spot_ref[...]
        lane = lax.broadcasted_iota(jnp.int32, (1, parts * size), 1)
        mine = (lane >= index_ref[0] * size) & (lane < (index_ref[0] + 1) * size)
        for k in range(chunks):
            dot, pp, tt = (gene_ref[k, at : at + 1, :] for at in range(3))
            scale = lax.rsqrt(pp + EPS) * lax.rsqrt(tt + EPS)
            cosine = dot * scale
            for at, value in enumerate(((-1.0 / genes) * scale, (1.0 / genes) * cosine / (pp + EPS), cosine)):
                spread = jnp.concatenate([value] * parts, axis=1)
                out_ref[at : at + 1, k * parts * size : (k + 1) * parts * size] = jnp.where(mine, spread, 0.0)

    smem = pl.BlockSpec(memory_space=pltpu.SMEM)
    vmem = pl.BlockSpec(memory_space=pltpu.VMEM)
    return pl.pallas_call(
        kernel,
        in_specs=[smem, vmem, vmem],
        out_shape=shape((8, width), F32),
        cost_estimate=COST,
        compiler_params=params(4),
        name="gene_slots",
    )(index, gene_sums, spot_sums)


def gradient_terms(slots, totals, genes, spots, chunks, spots_all):
    def kernel(slots_ref, totals_ref, gene_ref, spot_ref, row_ref):
        for k in range(chunks):
            gene_ref[k] = slots_ref[0:2, k * (genes // chunks) : (k + 1) * (genes // chunks)]
        dot, pp, tt = (slots_ref[3 + at : 4 + at, 0:spots] for at in range(3))
        scale = lax.rsqrt(pp + EPS) * lax.rsqrt(tt + EPS)
        cosine = dot * scale
        spot_ref[0:1, :] = (-1.0 / spots_all) * scale
        spot_ref[1:2, :] = (1.0 / spots_all) * cosine / (pp + EPS)
        row_ref[...] = totals_ref[...] + row_of(0.0, 0.0, 0.0, jnp.sum(slots_ref[2:3, 0:genes]), jnp.sum(cosine))

    return pl.pallas_call(
        kernel,
        out_shape=[shape((chunks, 2, genes // chunks), F32), shape((2, spots), F32), shape((1, LANES), F32)],
        cost_estimate=COST,
        compiler_params=params(4),
        name="gradient_terms",
    )(slots, totals)


def loss_row(row, genes, spots_all, n_spot):
    def kernel(row_ref, out_ref):
        kl_sum, mass_total, count_total, gene_sum, spot_sum = (row_ref[0:1, at : at + 1] for at in range(5))
        gene_mean = gene_sum / (genes * n_spot)
        spot_mean = spot_sum / spots_all
        kl = kl_sum / count_total + jnp.log(mass_total) - jnp.log(count_total)
        out_ref[...] = row_of(kl - gene_mean - spot_mean, gene_mean, spot_mean, kl)

    return pl.pallas_call(
        kernel, out_shape=shape((1, LANES), F32), cost_estimate=COST, compiler_params=params(4), name="loss_row"
    )(row)


def join(*pieces):
    count, size, spots = pieces[0].shape

    def kernel(*refs):
        for at, ref in enumerate(refs[:-1]):
            refs[-1][at * count : (at + 1) * count] = ref[...]

    vmem = pl.BlockSpec(memory_space=pltpu.VMEM)
    return pl.pallas_call(
        kernel,
        in_specs=[vmem] * len(pieces),
        out_specs=vmem,
        out_shape=shape((len(pieces) * count, size, spots), BF16),
        cost_estimate=COST,
        compiler_params=params(4),
        name="join",
    )(*pieces)


def fetch(index, chunk, target):
    parts, _, size, spots = target.shape

    def kernel(index_ref, target_ref, out_ref):
        out_ref[...] = target_ref[:, 0]

    return pl.pallas_call(
        kernel,
        grid_spec=pltpu.PrefetchScalarGridSpec(
            num_scalar_prefetch=1,
            grid=(1,),
            in_specs=[pl.BlockSpec((parts, 1, size, spots), lambda i, s: (0, chunk, 0, 0))],
            out_specs=pl.BlockSpec((parts, size, spots), lambda i, s: (0, 0, 0)),
        ),
        out_shape=shape((parts, size, spots), BF16),
        cost_estimate=COST,
        compiler_params=params(8),
        name="fetch",
    )(index, in_hbm(target))


def gradients(index, chunk, n_spot, pred_near, pred_far, target, gene_rows, spot_rows, weights):
    parts, size, spots = target.shape
    rows = weights.shape[0]
    tile = TILE_G
    width = parts * size
    per_spot = parts // n_spot
    spot_bits = bits_of(n_spot)
    order = bit_order(chunk, bits_of(parts))

    def kernel(index_ref, near_ref, far_ref, target_ref, gene_ref, spot_ref, weight_ref, *refs):
        grad_ref, back_ref, keep_ref, *send_refs, turned, columns = refs

        @pl.when(pl.program_id(0) == 0)
        def _():
            columns[0] = column_of(gene_ref[0, 0:1, :], width)
            columns[1] = column_of(gene_ref[0, 1:2, :], width)
            back = jnp.zeros((1, spots), F32)
            for j in range(parts):
                d = index_ref[0] ^ j
                apart = reversed_bits((d // per_spot) ^ index_ref[1], spot_bits)
                place = apart * per_spot + d % per_spot
                at = pl.multiple_of(d * size, size)
                among = place_among(j, order[:0:-1])
                pred = (far_ref if (j >> order[0]) & 1 else near_ref)[0, among].astype(F32)
                by_target = tile_lanes(columns[0, pl.ds(at, size), :], spots) + spot_ref[0:1, :]
                by_pred = tile_lanes(columns[1, pl.ds(at, size), :], spots) + spot_ref[1:2, :]
                grad = (target_ref[d].astype(F32) * by_target + pred * by_pred).astype(BF16)
                grad_ref[d] = grad
                turned[pl.ds(pl.multiple_of(place * size, size), size), :] = grad
                back = back + jnp.sum(grad.astype(F32) * pred, axis=0, keepdims=True)
            back_ref[...] = back

        @pl.loop(0, tile, step=PART_G)
        def _(start):
            part = pl.ds(pl.multiple_of(start, PART_G), PART_G)
            out = lax.dot_general(weight_ref[part, :], turned[...], (((1,), (1,)), ((), ())), preferred_element_type=F32)
            keep_ref[part, :] = out[:, : width // 2]
            for column, send_ref in enumerate(send_refs):
                left = width // 2 + column * (width // 4)
                send_ref[part, :] = out[:, left : left + width // 4].astype(BF16)

    member = gathered_with(chunk).index(chunk)
    half = pl.BlockSpec((1, parts // 2, size, spots), lambda i, s: (member, 0, 0, 0))
    piece = pl.BlockSpec((tile, width // 2), lambda i, s: (i, 0))
    return pl.pallas_call(
        kernel,
        grid_spec=pltpu.PrefetchScalarGridSpec(
            num_scalar_prefetch=1,
            grid=(rows // tile,),
            in_specs=[
                half,
                half,
                pl.BlockSpec((parts, size, spots), lambda i, s: (0, 0, 0)),
                pl.BlockSpec((1, 2, width), lambda i, s: (chunk, 0, 0)),
                pl.BlockSpec((2, spots), lambda i, s: (0, 0)),
                pl.BlockSpec((tile, spots), lambda i, s: (i, 0)),
            ],
            out_specs=[
                pl.BlockSpec((parts, size, spots), lambda i, s: (0, 0, 0)),
                pl.BlockSpec((1, spots), lambda i, s: (0, 0)),
                piece,
            ]
            + [pl.BlockSpec((tile, width // 4), lambda i, s: (i, 0))] * 2,
            scratch_shapes=[pltpu.VMEM((width, spots), BF16), pltpu.VMEM((2, width, LANES), F32)],
        ),
        out_shape=[
            shape((parts, size, spots), BF16),
            shape((1, spots), F32),
            shape((rows, width // 2), F32),
        ]
        + [shape((rows, width // 4), BF16)] * 2,
        cost_estimate=COST,
        compiler_params=params(30),
        name="gradients",
    )(index, pred_near, pred_far, target, gene_rows, spot_rows, weights)


def add_columns(keep, *received):
    rows, width = keep.shape
    tile = rows // 2
    half = width // 2

    def kernel(keep_ref, *refs):
        received_refs, (keep_out, send_out) = refs[:-2], refs[-2:]
        if len(received) == 1:
            keep_out[...] = keep_ref[:, :half] + received_refs[0][:, :half].astype(F32)
            send_out[...] = (keep_ref[:, half:] + received_refs[0][:, half:].astype(F32)).astype(BF16)
        else:
            keep_out[...] = keep_ref[:, :half] + received_refs[0][...].astype(F32)
            send_out[...] = (keep_ref[:, half:] + received_refs[1][...].astype(F32)).astype(BF16)

    whole = pl.BlockSpec((tile, width), lambda i: (i, 0))
    out = pl.BlockSpec((tile, half), lambda i: (i, 0))
    return pl.pallas_call(
        kernel,
        grid=(rows // tile,),
        in_specs=[whole] + ([whole] if len(received) == 1 else [out] * 2),
        out_specs=[out, out],
        out_shape=[shape((rows, half), F32), shape((rows, half), BF16)],
        cost_estimate=COST,
        compiler_params=params(20),
        name="add_columns",
    )(keep, *received)


def assemble(kept, received, size):
    rows, width = kept[0].shape
    chunks = len(kept)
    tile = TILE_Y

    def kernel(*refs):
        out_ref = refs[-1]
        sums = [refs[k][...] + refs[chunks + k][...].astype(F32) for k in range(chunks)]
        pieces = [sums[k][:, d * size : (d + 1) * size] for d in range(width // size) for k in range(chunks)]
        out_ref[...] = jnp.concatenate(pieces, axis=1)

    spec = pl.BlockSpec((tile, width), lambda i: (i, 0))
    return pl.pallas_call(
        kernel,
        grid=(rows // tile,),
        in_specs=[spec] * (2 * chunks),
        out_specs=pl.BlockSpec((tile, width * chunks), lambda i: (i, 0)),
        out_shape=shape((rows, width * chunks), F32),
        cost_estimate=COST,
        compiler_params=params(24),
        name="assemble",
    )(*kept, *received)


def assemble_pair(pair, kept, received, size, before):
    rows, width = kept[0].shape
    tile = rows

    def kernel(*refs):
        out_ref = refs[-1]
        for d in range(width // size):

            @pl.when(pl.program_id(1) == d)
            def _():
                sums = [refs[k][...] + refs[2 + k][...].astype(F32) for k in range(2)]
                if width == LANES == 2 * size:
                    left, right = (sums[k] if d == k else pltpu.roll(sums[k], size, 1) for k in range(2))
                    lane = lax.broadcasted_iota(jnp.int32, (1, LANES), 1)
                    out_ref[...] = jnp.where(lane < size, left, right)
                else:
                    out_ref[...] = jnp.concatenate([v[:, d * size : (d + 1) * size] for v in sums], axis=1)

    spec = pl.BlockSpec(memory_space=pltpu.VMEM)
    others = [] if before is None else [before]
    return pl.pallas_call(
        kernel,
        grid=(rows // tile, width // size),
        in_specs=[spec] * 4 + [pl.BlockSpec(memory_space=pl.ANY)] * len(others),
        out_specs=pl.BlockSpec((tile, 2 * size), lambda i, d: (i, d * (CHUNKS // 2) + pair)),
        out_shape=pltpu.HBM((rows, width * CHUNKS), F32),
        input_output_aliases={4: 0} if others else {},
        cost_estimate=COST,
        compiler_params=params(24),
        name="assemble_pair",
    )(*kept, *received, *[in_hbm(v) for v in others])


def logit_gradient(sums, expr, grads, logits, size_column, counts, totals, backs):
    rows, genes = expr.shape
    parts, size, spots = grads[0].shape
    chunks = len(grads)
    tile = TILE_X

    def kernel(sums_ref, expr_ref, logit_ref, column_ref, counts_ref, totals_ref, *refs):
        grad_refs, back_refs, (out_ref, grad) = refs[:chunks], refs[chunks : 2 * chunks], refs[2 * chunks :]

        @pl.when(pl.program_id(0) == 0)
        def _():
            for k, ref in enumerate(grad_refs):
                for d in range(parts):
                    at = (d * chunks + k) * size
                    grad[at : at + size, :] = ref[d]

        inverse = 1.0 / sums_ref[0:1, :]
        mass = sums_ref[1:2, :] / sums_ref[0:1, :]
        mass_grad = 1.0 / totals_ref[0:1, 1:2] - counts_ref[...] / (totals_ref[0:1, 2:3] * mass)
        back = sum(ref[...] for ref in back_refs) + mass * mass_grad
        acc = jnp.dot(expr_ref[...], grad[...], preferred_element_type=F32)
        probs = jnp.exp(logit_ref[...]) * inverse
        out_ref[...] = probs * ((acc + mass_grad) * tile_lanes(column_ref[...], spots) - back)

    across = pl.BlockSpec((tile, spots), lambda i: (i, 0))
    row = pl.BlockSpec((1, spots), lambda i: (0, 0))
    vmem = pl.BlockSpec(memory_space=pltpu.VMEM)
    return pl.pallas_call(
        kernel,
        grid=(rows // tile,),
        in_specs=[
            pl.BlockSpec((2, spots), lambda i: (0, 0)),
            pl.BlockSpec((tile, genes), lambda i: (i, 0)),
            across,
            pl.BlockSpec((tile, LANES), lambda i: (i, 0)),
            row,
            pl.BlockSpec((1, LANES), lambda i: (0, 0)),
        ]
        + [vmem] * chunks
        + [row] * chunks,
        out_specs=across,
        out_shape=pltpu.HBM((rows, spots), F32),
        scratch_shapes=[pltpu.VMEM((genes, spots), BF16)],
        cost_estimate=COST,
        compiler_params=params(34),
        name="logit_gradient",
    )(sums, in_hbm(expr), in_hbm(logits), size_column, counts, totals, *grads, *backs)


def on_device(logits, centroid_expr, target, sizes, counts):
    parts = lax.axis_size("cent")
    halves = bits_of(parts)
    n_spot = lax.axis_size("spot")
    spot_bits = bits_of(n_spot)
    rows, genes = centroid_expr.shape
    spots = logits.shape[1]
    spots_all = spots * n_spot
    per_device = genes // parts
    size = per_device // CHUNKS
    counts_f = counts.astype(F32).reshape(1, spots)
    target_rows = target.reshape(parts * CHUNKS, size, spots)
    target_chunks = target.reshape(parts, CHUNKS, size, spots)
    order = Order()
    index = jnp.stack([lax.axis_index("cent"), lax.axis_index("spot")])

    made = {}
    keeps, arrived, nears, fars, fetched, grads, backs, kept, landed = ([None] * CHUNKS for _ in range(9))

    def stats_step():
        sums, made["column"] = order.run(lambda i, *a: column_stats(i, *a, rows // 4), index, logits, sizes)
        made["total"] = sum_over(sums, "cent")

    def predict_step(k):
        if k == 0:
            out = order.run(
                lambda i, e, *a: predict(i, 0, parts, e, None, a), index, centroid_expr, logits, made["total"], made["column"]
            )
            made["weights"] = out[-1]
        else:
            before = made.pop("turned", None)
            out = order.run(lambda i, e, w: predict(i, k, parts, e, w, None, before), index, centroid_expr, made["weights"])
        if len(out) > (3 if k == 0 else 2):
            made["turned"] = out[2]
        keeps[k] = out[0]
        arrived[k] = swap(out[1], "cent", bit_order(k, halves)[0])

    def halve_step(at):
        def step(k):
            b = bit_order(k, halves)[at]
            keeps[k], send = order.run(lambda i, *a: add_and_halve(i, b, *a), index, keeps[k], arrived[k])
            arrived[k] = swap(send, "cent", b)

        return step

    def finish_step(k):
        *made["rows"], low = order.run(
            lambda i, *a: finish_rows(i, k, per_device, *a), index, keeps[k], arrived[k], target_rows, made.get("rows")
        )
        nears[k], fars[k] = low, swap(low, "cent", bit_order(k, halves)[-1])

    def pair_up_step(k):
        pieces = [v[c] for c in gathered_with(k) for v in (nears, fars)]
        (nears[k],) = order.run(lambda *a: (join(*a),), *pieces)
        fars[k] = swap(nears[k], "cent", bit_order(k, halves)[0])

    def join_step(at):
        def step(k):
            (nears[k],) = order.run(lambda *a: (join(*a),), nears[k], fars[k])
            fars[k] = swap(nears[k], "cent", bit_order(k, halves)[at])

        return step

    def totals_step():
        (made["totals"],) = order.run(lambda *a: (spot_totals(*a),), made["total"], counts_f)

    def genes_step():
        made["sums"] = made["rows"][1]
        made["hop"] = swap(made["sums"], "spot", 0)

    def genes_hop(b):
        def step():
            (made["sums"],) = order.run(lambda *a: (a[0] + a[1],), made["sums"], made["hop"])
            if b + 1 < spot_bits:
                made["hop"] = swap(made["sums"], "spot", b + 1)

        return step

    def slots_step():
        (made["slots"],) = order.run(lambda *a: (gene_slots(*a, parts),), index, made["sums"], made["rows"][2])
        made["hop"] = [swap(made["slots"], "cent", 0)]

    def slots_hop(last):
        def step():
            (made["slots"],) = order.run(lambda *a: (sum(a),), made["slots"], *made["hop"])
            if not last:
                made["hop"] = [exchange(made["slots"], "cent", 2 * j) for j in range(1, parts // 2)]

        return step

    def terms_step():
        made["genes"], made["terms"], made["row"] = order.run(
            lambda *a: gradient_terms(*a, genes, spots, CHUNKS, spots_all), made["slots"], made["totals"]
        )
        made["row_hop"] = swap(made["row"], "spot", 0)

    def row_hop(b):
        def step():
            (made["row"],) = order.run(lambda *a: (a[0] + a[1],), made["row"], made["row_hop"])
            if b + 1 < spot_bits:
                made["row_hop"] = swap(made["row"], "spot", b + 1)

        return step

    def losses_step():
        (row,) = order.run(lambda *a: (loss_row(*a, genes, spots_all, n_spot),), made["row"])
        (made["losses"],) = order.run(lambda a: (a[0, :4],), row)

    def fetch_step(k):
        (fetched[k],) = order.run(lambda i, t: (fetch(i, k, t),), index, target_chunks)

    def gradients_step(k):
        first, *_ = group = gathered_with(k)
        near, far = (v[first].reshape(len(group), parts // 2, size, spots) for v in (nears, fars))
        operands = (near, far, fetched[k], made["genes"], made["terms"], made["weights"])
        grads[k], backs[k], kept[k], *sends = order.run(lambda i, *a: gradients(i, k, n_spot, *a), index, *operands)
        landed[k] = [swap(send, "spot", 0) for send in sends]

    def columns_step(b):
        def step(k):
            kept[k], send = order.run(add_columns, kept[k], *landed[k])
            landed[k] = [swap(send, "spot", b)]

        return step

    def logits_step():
        (made["logit_grad"],) = order.run(
            lambda t, e, *a: (logit_gradient(t, e, grads, *a, backs),),
            *(made["total"], centroid_expr, logits, made["column"], counts_f, made["row"])
        )

    def centroids_step():
        (made["centroid_grad"],) = order.run(lambda *a: (assemble(a[:CHUNKS], a[CHUNKS:], size),), *kept, *sum(landed, []))

    def pair_step(pair):
        chunks = slice(2 * pair, 2 * pair + 2)
        before = made.get("centroid_grad")
        (made["centroid_grad"],) = order.run(
            lambda *a: (assemble_pair(pair, a[:2], a[2:], size, before),), *kept[chunks], *sum(landed[chunks], [])
        )

    def wait_for(values):
        return lambda k: order.wait(values[k])

    steps = {"C": stats_step, "P": predict_step, "F": finish_step, "T": totals_step, "g": genes_step}
    steps |= {"S": slots_step, "s0": slots_hop(False), "s1": slots_hop(True), "R": terms_step, "L": losses_step}
    steps |= {"p": pair_up_step, "t": fetch_step, "G": gradients_step, "X": logits_step, "Y": centroids_step, "y": pair_step}
    steps |= {"wa": wait_for(arrived), "wf": wait_for(fars), "wl": wait_for(landed)}
    steps |= {f"a{b}": halve_step(b) for b in range(1, halves)}
    steps |= {f"j{b}": join_step(b) for b in range(halves - 1)}
    steps |= {f"e{b}": columns_step(b) for b in range(1, spot_bits)}
    steps |= {f"g{b}": genes_hop(b) for b in range(spot_bits)}
    steps |= {f"r{b}": row_hop(b) for b in range(spot_bits)}
    for name in schedule(halves, spot_bits).split():
        step, _, k = name.partition(".")
        steps[step](*([int(k)] if k else []))
    return made["losses"], made["rows"][0], made["logit_grad"], made["centroid_grad"]


def schedule(halves, spot_bits):
    if (halves, spot_bits) == (3, 2):
        steps = (
            "C P.0 P.1 P.2", "a1.0 P.3 a1.1 t.0", "t.1 t.2 a2.0 a1.2", "t.3 wa.0 F.0 a1.3",
            "a2.2 j1.0 a2.1 F.2", "a2.3 wf.0 F.1 F.3", "g j0.0 g0 j1.2", "g1 T S s0",
            "wf.2 j1.1 j1.3 s1", "R r0 p.2 j0.1", "G.0 e1.0 G.1 wl.0", "e1.1 G.2 r1 L",
            "G.3 e1.2 y.0 e1.3", "X y.1",
        )
        return " ".join(steps)
    forward = ["P", *(f"a{b}" for b in range(1, halves)), "F"]
    backward = ["G", *(f"e{b}" for b in range(1, spot_bits))]
    waves = [
        [f"{chain[wave - k]}.{k}" for wave in range(len(chain) + CHUNKS) for k in range(CHUNKS) if 0 <= wave - k < len(chain)]
        for chain in (forward, backward)
    ]
    gather = []
    for group in sorted({tuple(gathered_with(k)) for k in range(CHUNKS)}):
        gather += [f"j{b}.{k}" for k in group for b in range(halves - 2, 0, -1)]
        gather.append(f"j0.{group[0]}" if len(group) == 1 else f"p.{group[0]}")
    middle = gather + [f"t.{k}" for k in range(CHUNKS)] + ["T", "g", *(f"g{b}" for b in range(spot_bits)), "S", "s0", "s1", "R"]
    middle += [*(f"r{b}" for b in range(spot_bits)), "L"]
    return " ".join(["C"] + waves[0] + middle + waves[1] + ["X", "Y"])


def solution(mesh):
    in_specs = (P("cent", "spot"), P("cent", None), P(None, "spot"), P("cent"), P("spot"))
    out_specs = (P(), P("cent", "spot"), P("cent", "spot"), P("cent", "spot"))
    return jax.shard_map(
        on_device, mesh=mesh, in_specs=in_specs, out_specs=out_specs, check_vma=False
    )
```
